32 devices in a mesh: seq: 16 (over z, x, core), mlp: 2 (over y).
Axes of the slice: x: 2, y: 2, z: 4, core: 2. Of those that a mesh axis runs over, the one named last changes fastest.
Arguments:
- patches: bfloat16 [16384, 768], P(('seq', 'mlp')), may hold values from -6 to 6
- segments: int32 [16384], P(('seq', 'mlp')), may hold values from 0 to 5, as said below
- prompt_slots: int32 [16384], P(('seq', 'mlp')), may hold values from 0 to 50, as said below
- norm_gains: float32 [2, 2, 768], replicated, may hold values from 0.25 to 1.75
- qkv_weight: bfloat16 [2, 768, 2304], P(None, 'seq'), may hold values from -0.21875 to 0.21875
- out_weight: bfloat16 [2, 768, 768], P(None, 'seq'), may hold values from -0.875 to 0.875
- up_weight: bfloat16 [2, 768, 3072], P(None, 'seq', 'mlp'), may hold values from -0.21875 to 0.21875
- down_weight: bfloat16 [2, 3072, 768], P(None, 'mlp', 'seq'), may hold values from -0.15625 to 0.15625
- cotangent: bfloat16 [16384, 768], P(('seq', 'mlp')), may hold values from -6 to 6
- prompts: float32 [76800], P(('seq', 'mlp')), may hold values from -5 to 5
- first_moment: float32 [76800], P(('seq', 'mlp')), may hold values from -0.24 to 0.24
- second_moment: float32 [76800], P(('seq', 'mlp')), may hold values from 1e-05 to 0.015
- adam_betas: float32 [2], replicated, may hold values from 0.4 to 0.6
- learn_rate: float32 [1], replicated, may hold values from 0.2 to 0.6
Outputs:
- block_output: bfloat16 [16384, 768], P(('seq', 'mlp'))
- input_grad: float32 [16384, 768], P(('seq', 'mlp'))
- new_prompts: float32 [76800], P(('seq', 'mlp'))
- new_first: float32 [76800], P(('seq', 'mlp'))
- new_second: float32 [76800], P(('seq', 'mlp'))
- grad_norm: float32 [1], replicated
The draws below stay inside these ranges and needn't reach their ends.
Inputs may be any that keep to these rules, and one draw needn't show every extreme that they name: `segments`: the 512 tokens of one device form aligned blocks in which whole images lie one after another, numbered 0, 1, 2 and so on; each image has 51 to 247 tokens, and every block holds an image of exactly 247 tokens. `prompt_slots`: the first 50 tokens of each image hold slots 0 to 49 in order; all other tokens hold 50.
All inputs are finite; a program needn't handle non-finite values.
Results may differ from the reference program's by a relative error of at most 0.02.
Values may be sent and summed in bfloat16 or wider, within the bound.
No kernel may reach another device: no remote copies, remote signals or barrier semaphores. Data moves between devices by JAX's collectives and lax.ppermute only.
A program may use at most 192 MiB of HBM per device.

```python
import math
import jax
import jax.numpy as jnp
from jax import lax

D = 768
HEADS = 12
HEAD_DIM = 64
FF = 3072
PROMPTS = 50
IMG_TOK = 197
LAYERS = 2
ADAM_STEP = 2
TOK_DEV = 512
TOKENS = 16384


def packing(key):
    row_count = TOKENS // TOK_DEV
    candidates = TOK_DEV // (PROMPTS + 1) + 2
    draw_key, pick_key = jax.random.split(jax.random.fold_in(key, 17))
    image_lens = PROMPTS + jax.random.randint(draw_key, (row_count, candidates), 1, IMG_TOK - PROMPTS + 1)
    row_number = jnp.arange(row_count)[:, None]
    image_lens = jnp.where(row_number == 0, PROMPTS + 1, image_lens)
    forced_pick = jax.random.randint(pick_key, (row_count, 1), 0, 2)
    image_index = jnp.arange(candidates)[None, :]
    image_lens = jnp.where(image_index == forced_pick, PROMPTS + IMG_TOK, image_lens)
    image_ends = jnp.cumsum(image_lens, axis=1)
    image_starts = image_ends - image_lens
    position = jnp.arange(TOK_DEV)[None, :, None]
    segment = jnp.sum((image_ends[:, None, :] <= position).astype(jnp.int32), axis=2)
    complete = jnp.sum((image_ends <= TOK_DEV).astype(jnp.int32), axis=1, keepdims=True)
    last_end = jnp.sum(jnp.where(image_index == complete - 1, image_ends, 0), axis=1, keepdims=True)
    too_short = TOK_DEV - last_end < PROMPTS + 1
    segment = jnp.where(too_short & (segment == complete), complete - 1, segment)
    image_begin = jnp.sum(jnp.where(segment[:, :, None] == image_index[:, None, :], image_starts[:, None, :], 0), axis=2)
    slot_index = jnp.arange(TOK_DEV)[None, :] - image_begin
    slot_index = jnp.where(slot_index < PROMPTS, slot_index, PROMPTS)
    return (segment.reshape(-1).astype(jnp.int32), slot_index.reshape(-1).astype(jnp.int32))


def draw_segments(key, part):
    return packing(key)[0]


def draw_prompt_slots(key, part):
    return packing(key)[1]


def layer_scale(total):
    layer_at = jnp.arange(total) // (PROMPTS * D)
    return jnp.where(layer_at == LAYERS - 1, 0.06, 0.01).astype(jnp.float32)


def draw_first_moment(key, part):
    total = LAYERS * PROMPTS * D
    base = jnp.clip(jax.random.normal(key, (total,), jnp.float32), -4.0, 4.0)
    return base * layer_scale(total)


def draw_second_moment(key, part):
    total = LAYERS * PROMPTS * D
    factor = jnp.exp(jax.random.uniform(key, (total,), jnp.float32, -1.2, 1.0986))
    scale_row = layer_scale(total)
    return factor * scale_row * scale_row


def shard_levels(rng, extent, cuts, least, high):
    loudness, own = 1.0, jax.random.fold_in(rng, 6)
    for axis_at, parts in cuts:
        draws = jnp.exp(jax.random.uniform(jax.random.fold_in(own, axis_at), (parts,), jnp.float32, least / len(cuts), high / len(cuts)))
        loudness = loudness * jnp.repeat(draws, extent[axis_at] // parts).reshape([-1 if axis == axis_at else 1 for axis in range(len(extent))])
    return loudness


def bell_draw(stream_key, shape, scale, bound, shards=(), dtype=jnp.bfloat16):
    entries = jax.random.normal(stream_key, shape, jnp.float32) * scale
    if len(shards) > 0:
        entries = shard_levels(stream_key, shape, shards, -0.22, 0.18) * entries
    return jnp.clip(entries, min=-bound, max=bound).astype(dtype)


def setup_inputs(seed: int = 0) -> dict:
    keys = jax.random.split(jax.random.key(seed), 15)
    return {
        "patches": bell_draw(keys[0], (TOKENS, D), 1.0, 6.0, ((0, 32),)),
        "segments": draw_segments(jax.random.fold_in(keys[14], 71), 0),
        "prompt_slots": draw_prompt_slots(jax.random.fold_in(keys[14], 71), 0),
        "norm_gains": jnp.clip(1.0 + 0.15 * jax.random.normal(keys[3], (LAYERS, 2, D), jnp.float32), 0.25, 1.75),
        "qkv_weight": bell_draw(keys[4], (LAYERS, D, 3 * D), D ** -0.5, 0.21875, ((1, 16),)),
        "out_weight": bell_draw(keys[5], (LAYERS, D, D), (D // 16) ** -0.5, 0.875, ((1, 16),)),
        "up_weight": bell_draw(keys[6], (LAYERS, D, FF), D ** -0.5, 0.21875, ((1, 16), (2, 2))),
        "down_weight": bell_draw(keys[7], (LAYERS, FF, D), (FF // 2) ** -0.5, 0.15625, ((1, 2), (2, 16))),
        "cotangent": bell_draw(keys[8], (TOKENS, D), 1.0, 6.0, ((0, 32),)),
        "prompts": bell_draw(keys[9], (LAYERS * PROMPTS * D,), 1.0, 5.0, ((0, 32),), jnp.float32),
        "first_moment": draw_first_moment(jax.random.fold_in(keys[14], 71), 0),
        "second_moment": draw_second_moment(jax.random.fold_in(keys[14], 71), 0),
        "adam_betas": jnp.clip(jax.random.uniform(keys[12], (2,), jnp.float32, 0.4, 0.6), 0.4, 0.6),
        "learn_rate": jnp.clip(jax.random.uniform(keys[13], (1,), jnp.float32, 0.2, 0.6), 0.2, 0.6),
    }


@jax.custom_vjp
def low(v):
    return lax.optimization_barrier(v.astype(jnp.bfloat16)).astype(jnp.float32)

@jax.custom_vjp
def low_back(v):
    return v

def low_keep(v):
    return (low(v), None)

def low_pass(kept, grad):
    return (grad,)

def back_keep(v):
    return (v, None)

def back_low(kept, grad):
    return (low(grad),)
low.defvjp(low_keep, low_pass)
low_back.defvjp(back_keep, back_low)
ln_eps = 1e-06
masked_score = -1e+30
clip_ratio = 0.05
adam_eps = 1e-08
decay_rate = 0.1
highest = lax.Precision.HIGHEST

def layer_norm(values, gain_row):
    center = values - lax.optimization_barrier(jnp.mean(values, axis=-1, keepdims=True))
    spread = lax.optimization_barrier(jnp.mean(center * center, axis=-1, keepdims=True))
    return center * lax.rsqrt(spread + ln_eps) * gain_row

def attend_row(row_parts):
    query_heads, key_heads, value_heads, segment = row_parts
    scores = jnp.einsum('qhd,khd->hqk', query_heads, key_heads, precision=highest) * HEAD_DIM ** (-0.5)
    scores = low_back(scores)
    allowed = (segment[:, None] == segment[None, :])[None]
    scores = jnp.where(allowed, scores, masked_score)
    row_max = lax.optimization_barrier(jnp.max(scores, axis=2, keepdims=True))
    exponent = jnp.exp(scores - row_max)
    attn_probs = low(exponent / lax.optimization_barrier(jnp.sum(exponent, axis=2, keepdims=True)))
    mixed_heads = jnp.einsum('hqk,khd->qhd', attn_probs, value_heads, precision=highest)
    return mixed_heads.reshape(mixed_heads.shape[0], -1)

def make_forward(segments, prompt_slots, norm_gains, w_qkv, w_out, w_up, w_down):
    row_count = segments.shape[0] // TOK_DEV
    onehot = (prompt_slots[:, None] == jnp.arange(PROMPTS)[None, :]).astype(jnp.float32)
    is_prompt = (prompt_slots < PROMPTS)[:, None]
    seg_rows = segments.reshape(row_count, TOK_DEV)

    def forward(patch_rows, prompt_flat):
        prompt_table = prompt_flat.reshape(LAYERS, PROMPTS, D)
        hidden = patch_rows
        for layer_at in range(LAYERS):
            inject = jnp.dot(onehot, prompt_table[layer_at], precision=highest)
            entry_rows = jnp.where(is_prompt, inject, hidden)
            normed = low(layer_norm(entry_rows, norm_gains[layer_at, 0]))
            qkv_proj = low(low_back(jnp.dot(normed, w_qkv[layer_at], precision=highest)))
            split_heads = qkv_proj.reshape(row_count, TOK_DEV, 3, HEADS, HEAD_DIM)
            mixed_rows = lax.map(jax.checkpoint(attend_row), (split_heads[:, :, 0], split_heads[:, :, 1], split_heads[:, :, 2], seg_rows))
            mixed_rows = low(low_back(mixed_rows.reshape(-1, D)))
            middle = entry_rows + low_back(jnp.dot(mixed_rows, w_out[layer_at], precision=highest))
            normed_two = low(layer_norm(middle, norm_gains[layer_at, 1]))
            before = low_back(jnp.dot(normed_two, w_up[layer_at], precision=highest))
            active = low(jax.nn.gelu(before, approximate=False))
            hidden = middle + low_back(jnp.dot(active, w_down[layer_at], precision=highest))
        return hidden
    return forward

def reference(patches, segments, prompt_slots, norm_gains, qkv_weight, out_weight, up_weight, down_weight, cotangent, prompts, first_moment, second_moment, adam_betas, learn_rate):
    forward = make_forward(segments, prompt_slots, norm_gains, qkv_weight.astype(jnp.float32), out_weight.astype(jnp.float32), up_weight.astype(jnp.float32), down_weight.astype(jnp.float32))
    output, pullback = jax.vjp(forward, patches.astype(jnp.float32), prompts)
    input_grad, prompt_grad = pullback(cotangent.astype(jnp.float32))
    grad_norm = jnp.sqrt(jnp.sum(prompt_grad * prompt_grad))
    clip_limit = clip_ratio * math.sqrt(prompts.shape[0])
    clipped = prompt_grad * jnp.minimum(1.0, clip_limit / (grad_norm + 1e-06))
    beta_one = adam_betas[0]
    beta_two = adam_betas[1]
    step_value = float(ADAM_STEP)
    new_first = beta_one * first_moment + (1.0 - beta_one) * clipped
    new_second = beta_two * second_moment + (1.0 - beta_two) * clipped * clipped
    first_hat = new_first / (1.0 - beta_one ** step_value)
    second_hat = new_second / (1.0 - beta_two ** step_value)
    new_prompts = prompts - learn_rate[0] * (first_hat / (jnp.sqrt(second_hat) + adam_eps) + decay_rate * prompts)
    return (output.astype(jnp.bfloat16), input_grad, new_prompts, new_first, new_second, grad_norm.reshape(1))
```

```python
import math
from functools import partial

import jax
import jax.numpy as jnp
from jax import lax
from jax.sharding import Mesh
from jax.sharding import PartitionSpec as P

HEADS = 12
HEAD_DIM = 64
ADAM_STEP = 2

ln_eps = 1e-06
masked_score = -1e30
clip_ratio = 0.05
adam_eps = 1e-08
decay_rate = 0.1
highest = lax.Precision.HIGHEST
ALL = ("z", "x", "core", "y")
f32 = jnp.float32
bf16 = jnp.bfloat16


def layer_norm(values, gain_row):
    center = values - jnp.mean(values, axis=-1, keepdims=True)
    spread = jnp.mean(center * center, axis=-1, keepdims=True)
    return center * lax.rsqrt(spread + ln_eps) * gain_row


def exact_gelu(values):
    return jax.nn.gelu(values, approximate=False)


def flip(value, axis):
    return lax.ppermute(value, axis, [(0, 1), (1, 0)])


def spread_over(value, axis):
    if lax.axis_size(axis) != 2:
        return lax.all_gather(value, axis)
    other = flip(value, axis)
    first = lax.axis_index(axis) == 0
    return jnp.stack([jnp.where(first, value, other), jnp.where(first, other, value)])


def ring_z(value):
    size = lax.axis_size("z")
    if size != 4:
        return lax.all_gather(value, "z")
    parts = [value]
    for step in range(1, size):
        parts.append(lax.ppermute(value, "z", [(i, (i + step) % size) for i in range(size)]))
    at = lax.axis_index("z")
    return jnp.stack(
        [lax.select_n((at - i) % size, *parts) for i in range(size)]
    )


def gather_group(part_a, part_b, first):
    width = part_a.shape[1]
    both = jnp.concatenate([part_a, part_b], axis=1)
    along = ring_z(both) if first else lax.all_gather(both, "z")
    a, b = along[:, :, :width], along[:, :, width:]
    a = spread_over(a, "x")
    b = spread_over(b, "y")
    a = spread_over(a, "y")
    b = spread_over(b, "x")
    a = spread_over(a, "core")
    b = spread_over(b, "core")
    return a.transpose(3, 2, 0, 4, 1, 5), b.transpose(3, 1, 0, 4, 2, 5)


def rows_of(gathered):
    z, x, core, rows, y, width = gathered.shape
    return gathered.reshape(z * x * core * rows, y, width)


def masked_scores(query_heads, key_heads, segments):
    raw_scores = jnp.einsum(
        "qhd,khd->hqk", query_heads, key_heads, preferred_element_type=f32
    ) * HEAD_DIM ** (-0.5)
    allowed = (segments[:, None] == segments[None, :])[None]
    return jnp.where(allowed, raw_scores, masked_score)


def attend_forward(query_heads, key_heads, value_heads, segments):
    scores = masked_scores(query_heads, key_heads, segments)
    row_max = jnp.max(scores, axis=2, keepdims=True)
    exponent = jnp.exp(scores - row_max)
    row_total = jnp.sum(exponent, axis=2, keepdims=True)
    attn_probs = (exponent / row_total).astype(bf16)
    mixed = jnp.einsum("hqk,khd->qhd", attn_probs, value_heads, preferred_element_type=f32)
    return mixed.astype(bf16).reshape(mixed.shape[0], -1), row_max + jnp.log(row_total)


def attend_backward(query_heads, key_heads, value_heads, segments, lse, grad_rows):
    scale = HEAD_DIM ** (-0.5)
    scores = masked_scores(query_heads, key_heads, segments)
    attn_probs = jnp.exp(scores - lse)
    grad_probs = jnp.einsum("qhd,khd->hqk", grad_rows, value_heads, preferred_element_type=f32)
    inner_sum = jnp.sum(attn_probs * grad_probs, axis=2, keepdims=True)
    grad_scores = (attn_probs * (grad_probs - inner_sum)).astype(bf16)
    grad_query = (
        jnp.einsum("hqk,khd->qhd", grad_scores, key_heads, preferred_element_type=f32) * scale
    )
    grad_keys = (
        jnp.einsum("hqk,qhd->khd", grad_scores, query_heads, preferred_element_type=f32) * scale
    )
    grad_values = jnp.einsum(
        "hqk,qhd->khd", attn_probs.astype(bf16), grad_rows, preferred_element_type=f32
    )
    tokens = grad_query.shape[0]
    return jnp.concatenate(
        [v.astype(bf16).reshape(tokens, -1) for v in (grad_query, grad_keys, grad_values)], axis=1
    )


def total_over(value):
    if lax.axis_size("z") != 4 or lax.axis_size("y") != 2:
        return lax.psum(value, ALL)
    core = lax.axis_index("core")
    low = value.astype(bf16)
    mine = jnp.where(core == 0, value[0], value[1])
    theirs = jnp.where(core == 0, low[1], low[0])
    total = mine + flip(theirs, "core").astype(f32)
    for axis in ("x", "y"):
        total = total + flip(total.astype(bf16), axis).astype(f32)
    for pairs in ([(0, 1), (1, 0), (2, 3), (3, 2)], [(0, 2), (2, 0), (1, 3), (3, 1)]):
        total = total + lax.ppermute(total.astype(bf16), "z", pairs).astype(f32)
    other = flip(total.astype(bf16), "core").astype(f32)
    return jnp.stack([jnp.where(core == 0, total, other), jnp.where(core == 0, other, total)])


def per_device(
    patches,
    segments,
    prompt_slots,
    norm_gains,
    qkv_weight,
    out_weight,
    up_weight,
    down_weight,
    cotangent,
    prompts,
    first_moment,
    second_moment,
    adam_betas,
    learn_rate,
):
    layers, _, width = norm_gains.shape
    tokens = patches.shape[0]
    y_size, y_at = lax.axis_size("y"), lax.axis_index("y")
    devices = y_size * lax.axis_size("z") * lax.axis_size("x") * lax.axis_size("core")
    rows = qkv_weight.shape[1]
    total_prompts = prompts.shape[0] * devices

    across = prompts.shape[0] // rows
    rides = across * rows == prompts.shape[0]
    if rides:
        shaped = prompts.reshape(rows, across)
        high_half = shaped.astype(bf16)
        low_half = (shaped - high_half.astype(f32)).astype(bf16)
        rider = jnp.concatenate([high_half, low_half], axis=1)
        rider = jnp.pad(rider, ((0, 0), (0, -rider.shape[1] % 128)))

    weights = []
    prompt_table = None
    if not rides:
        prompt_table = lax.all_gather(prompts, ALL).reshape(layers, -1, width)
    for layer_at in range(layers):
        cut = qkv_weight.shape[2] // y_size
        out_cut = width // y_size
        qkv_part = lax.dynamic_slice(qkv_weight[layer_at], (0, y_at * cut), (rows, cut))
        out_part = lax.dynamic_slice(out_weight[layer_at], (0, y_at * out_cut), (rows, out_cut))
        half = (cut + out_cut) // 2
        part_a = qkv_part[:, :half]
        part_b = jnp.concatenate([qkv_part[:, half:], out_part], axis=1)
        if layer_at == 0 and rides:
            part_a = jnp.concatenate([part_a, rider], axis=1)
        attn_a, attn_b = gather_group(part_a, part_b, layer_at == 0)
        if layer_at == 0 and rides:
            riders = attn_a[..., half:]
            riders = riders.transpose(0, 1, 2, 4, 3, 5)
            table = riders[..., :across].astype(f32) + riders[..., across : 2 * across].astype(f32)
            prompt_table = table.reshape(layers, -1, width)
        attn_a, attn_b = rows_of(attn_a[..., :half]), rows_of(attn_b)
        w_qkv = jnp.concatenate([attn_a, attn_b[..., : cut - half]], axis=2).reshape(width, -1)
        w_out = attn_b[..., cut - half :].reshape(width, -1)
        w_up, w_down = gather_group(up_weight[layer_at], down_weight[layer_at].T, False)
        w_up = rows_of(w_up).reshape(width, -1)
        w_down = rows_of(w_down).reshape(width, -1)
        weights.append((w_qkv, w_out, w_up, w_down))

    slot_total = prompt_table.shape[1]
    onehot = (prompt_slots[:, None] == jnp.arange(slot_total)[None, :]).astype(f32)
    is_prompt = (prompt_slots < slot_total)[:, None]
    hidden = patches.astype(f32)
    kept_state = []
    for layer_at in range(layers):
        w_qkv, w_out, w_up, w_down = weights[layer_at]
        inject = jnp.dot(onehot, prompt_table[layer_at], precision=highest)
        entry_rows = jnp.where(is_prompt, inject, hidden)
        normed_one, norm_one_back = jax.vjp(
            partial(layer_norm, gain_row=norm_gains[layer_at, 0]), entry_rows
        )
        qkv = jnp.dot(normed_one.astype(bf16), w_qkv, preferred_element_type=f32).astype(bf16)
        heads = [
            qkv[:, i * width : (i + 1) * width].reshape(tokens, HEADS, HEAD_DIM) for i in range(3)
        ]
        mixed_rows, lse = attend_forward(*heads, segments)
        middle = entry_rows + jnp.dot(mixed_rows, w_out, preferred_element_type=f32)
        normed_two, norm_two_back = jax.vjp(
            partial(layer_norm, gain_row=norm_gains[layer_at, 1]), middle
        )
        before = jnp.dot(normed_two.astype(bf16), w_up, preferred_element_type=f32)
        active = exact_gelu(before).astype(bf16)
        hidden = middle + jnp.einsum("tf,df->td", active, w_down, preferred_element_type=f32)
        kept_state.append((heads, lse, norm_one_back, norm_two_back, before))
    block_output = hidden.astype(bf16)
    gradient = cotangent.astype(f32)
    layer_grads = []
    for layer_at in reversed(range(layers)):
        w_qkv, w_out, w_up, w_down = weights[layer_at]
        heads, lse, norm_one_back, norm_two_back, before = kept_state[layer_at]
        grad_active = jnp.dot(gradient.astype(bf16), w_down, preferred_element_type=f32)
        grad_before = jax.vjp(exact_gelu, before)[1](grad_active)[0].astype(bf16)
        grad_normtwo = jnp.einsum("tf,df->td", grad_before, w_up, preferred_element_type=f32)
        grad_middle = gradient + norm_two_back(grad_normtwo)[0]
        grad_mixed = jnp.einsum(
            "te,de->td", grad_middle.astype(bf16), w_out, preferred_element_type=f32
        ).astype(bf16)
        grad_qkv = attend_backward(
            *heads, segments, lse, grad_mixed.reshape(tokens, HEADS, HEAD_DIM)
        )
        grad_normone = jnp.einsum("tc,dc->td", grad_qkv, w_qkv, preferred_element_type=f32)
        grad_entry = grad_middle + norm_one_back(grad_normone)[0]
        layer_grads.append(jnp.einsum("tp,td->pd", onehot, grad_entry, precision=highest))
        gradient = jnp.where(is_prompt, 0.0, grad_entry)

    prompt_grad = total_over(jnp.stack(layer_grads[::-1]))
    grad_norm = jnp.sqrt(jnp.sum(prompt_grad * prompt_grad))
    clip_limit = clip_ratio * math.sqrt(total_prompts)
    own_grads = lax.dynamic_slice(
        prompt_grad.reshape(-1), (lax.axis_index(ALL) * prompts.shape[0],), prompts.shape
    )
    clipped = own_grads * jnp.minimum(1.0, clip_limit / (grad_norm + 1e-06))
    beta_one = adam_betas[0]
    beta_two = adam_betas[1]
    step_value = float(ADAM_STEP)
    new_first = beta_one * first_moment + (1.0 - beta_one) * clipped
    new_second = beta_two * second_moment + (1.0 - beta_two) * clipped * clipped
    first_hat = new_first / (1.0 - beta_one**step_value)
    second_hat = new_second / (1.0 - beta_two**step_value)
    new_prompts = prompts - learn_rate[0] * (
        first_hat / (jnp.sqrt(second_hat) + adam_eps) + decay_rate * prompts
    )
    return (block_output, gradient, new_prompts, new_first, new_second, grad_norm.reshape(1))


def solution(mesh):
    seq_size, mlp_size = mesh.shape["seq"], mesh.shape["mlp"]
    grid = Mesh(mesh.devices.reshape(seq_size // 4, 2, 2, mlp_size), ALL)
    seq, mlp = ("z", "x", "core"), "y"
    in_specs = (
        P(ALL, None),
        P(ALL),
        P(ALL),
        P(),
        P(None, seq, None),
        P(None, seq, None),
        P(None, seq, mlp),
        P(None, mlp, seq),
        P(ALL, None),
        P(ALL),
        P(ALL),
        P(ALL),
        P(),
        P(),
    )
    out_specs = (P(ALL, None), P(ALL, None), P(ALL), P(ALL), P(ALL), P())
    return jax.shard_map(
        per_device, mesh=grid, in_specs=in_specs, out_specs=out_specs, check_vma=False
    )
```

```python
import math
from functools import partial

import jax
import jax.numpy as jnp
from jax import lax
from jax.experimental import pallas as pl
from jax.experimental.pallas import tpu as pltpu
from jax.sharding import Mesh
from jax.sharding import PartitionSpec as P

HEADS = 12
HEAD_DIM = 64
ADAM_STEP = 2

ln_eps = 1e-06
masked_score = -1e30
clip_ratio = 0.05
adam_eps = 1e-08
decay_rate = 0.1
ALL = ("z", "x", "core", "y")
f32 = jnp.float32
bf16 = jnp.bfloat16
LANES = 128
TILE = 256
VMEM_BYTES = 56 * 2**20

TAIL_SLOPE = 0.275
TAIL_POLY = (
    0.10971068582446765,
    0.1096543595961662,
    0.10219045697718625,
    0.07893593678575173,
    0.08800740710695068,
    -0.03516190352887128,
    0.13017028940734943,
    -0.11067510560848658,
    0.027167870070925505,
)


def mm(a, b):
    return jnp.dot(a, b, preferred_element_type=f32)


def mm_t(a, b):
    return lax.dot_general(a, b, (((1,), (1,)), ((), ())), preferred_element_type=f32)


def gelu_parts(v):
    a = jnp.abs(v)
    bell = jnp.exp(v * v * -0.5)
    t = 1.0 / (1.0 + TAIL_SLOPE * a)
    poly = jnp.full_like(v, TAIL_POLY[-1])
    for factor in TAIL_POLY[-2::-1]:
        poly = poly * t + factor
    tail = poly * t * bell
    return jnp.where(v >= 0.0, 1.0 - tail, tail), bell * (1.0 / math.sqrt(2.0 * math.pi))


def norm_stats(values):
    center = values - jnp.mean(values, axis=-1, keepdims=True)
    rstd = lax.rsqrt(jnp.mean(center * center, axis=-1, keepdims=True) + ln_eps)
    return center * rstd, rstd


def norm_back(grad, values, gain_row):
    unit, rstd = norm_stats(values)
    grad = grad * gain_row
    mean_grad = jnp.mean(grad, axis=-1, keepdims=True)
    mean_dot = jnp.mean(grad * unit, axis=-1, keepdims=True)
    return rstd * (grad - mean_grad - unit * mean_dot)


def places():
    _, x, core, y = (lax.axis_index(axis) for axis in ALL)
    found = []
    for other in range(2):
        c = lax.rem(core + other, 2)
        for dx, dy in ((0, 0), (1 - c, c), (c, 1 - c), (1, 1)):
            found.append((lax.rem(x + dx, 2), c, lax.rem(y + dy, 2)))
    return found


def ring_place(back, size):
    return lax.rem(lax.axis_index("z") + size - back, size)


class Copies:
    def __init__(self, pairs, sems):
        self.copies = [
            pltpu.make_async_copy(source, target, sems.at[i])
            for i, (source, target) in enumerate(pairs)
        ]

    def start(self):
        for copy in self.copies:
            copy.start()
        return self

    def wait(self):
        for copy in self.copies:
            copy.wait()


def weight_copies(refs, column, width, dest, sems, ringed):
    if len(refs) == 1:
        return Copies([(refs[0].at[:, pl.ds(column, dest.shape[-1])], dest)], sems)
    z_size, rows, _ = refs[0].shape
    columns = pl.ds(column, width)
    pairs = []
    for ref, (x, core, y) in zip(refs, places()):
        to_rows = pl.ds(pl.multiple_of((x * 2 + core) * rows, 16), rows)
        to_columns = pl.ds(pl.multiple_of(y * width, LANES), width)
        if ringed:
            for back in range(z_size):
                at = ring_place(back, z_size)
                pairs.append((ref.at[back, :, columns], dest.at[at, to_rows, to_columns]))
        else:
            pairs.append((ref.at[:, :, columns], dest.at[:, to_rows, to_columns]))
    return Copies(pairs, sems)


def rider_copies(refs, column, dest, sems):
    z_size = refs[0].shape[0]
    pairs = []
    for ref, (x, core, y) in zip(refs, places()):
        for back in range(z_size):
            at = ((ring_place(back, z_size) * 2 + x) * 2 + core) * 2 + y
            pairs.append((ref.at[back, :, pl.ds(column, LANES)], dest.at[at]))
    return Copies(pairs, sems)


def rows_view(ref, columns=None):
    value = ref[...] if columns is None else ref[..., columns]
    return value.reshape(-1, value.shape[-1])


def weight_scratch(refs, width, columns):
    if len(refs) == 1:
        return pltpu.VMEM((width, columns), bf16)
    z_size, rows, _ = refs[0].shape
    return pltpu.VMEM((z_size, width // z_size, columns), bf16)


def column_tile(at):
    return pl.ds(pl.multiple_of(at * TILE, TILE), TILE)


def pair_lanes(at):
    return pl.ds(pl.multiple_of(at * LANES, LANES), LANES)


def head_of(pair, head):
    lane = lax.broadcasted_iota(jnp.int32, pair.shape, 1)
    keep = (lane < HEAD_DIM) if head == 0 else (lane >= HEAD_DIM)
    return jnp.where(keep, pair, jnp.zeros_like(pair))


def fill_bias(bias_ref, seg_col_ref, seg_row_ref):
    bias_ref[...] = jnp.where(seg_col_ref[...] == seg_row_ref[...], 0.0, masked_score)


def attn_forward_body(static, *refs):
    count, ringed, layer_at, slot_total, takes_riders = static
    pieces, refs = refs[:count], refs[count:]
    x_ref, slot_ref, base_ref, seg_col_ref, seg_row_ref, gain_ref = refs[:6]
    refs = refs[6:]
    rider_ref = refs[4] if takes_riders else refs[0]
    entry_ref, qkv_ref, lse_ref, middle_ref = refs[:4] if takes_riders else refs[1:5]
    w_qkv, w_out, norm_ref, mixed_ref, bias_ref, sem_a, sem_b, sem_c = refs[5:]
    tokens, width = entry_ref.shape
    y_size = 1 if count == 1 else 2
    cut = 3 * width // y_size
    if takes_riders:
        load_riders = rider_copies(pieces, cut + width // y_size, rider_ref, sem_c).start()
    load_qkv = weight_copies(pieces, 0, cut, w_qkv, sem_a, ringed).start()
    load_out = weight_copies(pieces, cut, width // y_size, w_out, sem_b, ringed).start()
    fill_bias(bias_ref, seg_col_ref, seg_row_ref)
    slots = slot_ref[...]
    onehot = (slots == base_ref[...]).astype(bf16)
    is_prompt = slots < slot_total
    if takes_riders:
        load_riders.wait()
    holders = base_ref.shape[1] // 8
    windows = rider_ref[layer_at * holders : (layer_at + 1) * holders].astype(f32)
    for at in range(width // LANES):
        lanes = slice(at * LANES, (at + 1) * LANES)
        part = windows[:, at * 8 : (at + 1) * 8, :].reshape(-1, LANES)
        inject = mm(onehot, part.astype(bf16))
        entry_ref[:, lanes] = jnp.where(is_prompt, inject, x_ref[:, lanes].astype(f32))
    norm_ref[...] = (norm_stats(entry_ref[...])[0] * gain_ref[...]).astype(bf16)
    load_qkv.wait()

    @pl.loop(0, 3 * width // TILE)
    def _(at):
        columns = column_tile(at)
        scale = jnp.where(at < width // TILE, HEAD_DIM**-0.5, 1.0)
        out = mm(norm_ref[...], rows_view(w_qkv, columns)).astype(bf16)
        qkv_ref[:, columns] = (out.astype(f32) * scale).astype(bf16)

    pairs = width // LANES

    @pl.loop(0, pairs)
    def _(at):
        query, key = qkv_ref[:, pair_lanes(at)], qkv_ref[:, pair_lanes(at + pairs)]
        value_t = qkv_ref[:, pair_lanes(at + 2 * pairs)].T
        mixed = []
        for head in range(2):
            query_head = head_of(query, head)
            tiles, lses = [], []
            for t in range(tokens // TILE):
                q_rows = slice(t * TILE, (t + 1) * TILE)
                scores = mm_t(key, query_head[q_rows]) + bias_ref[:, q_rows]
                top = jnp.max(scores, axis=0, keepdims=True)
                exponent = jnp.exp(scores - top)
                total = jnp.sum(exponent, axis=0, keepdims=True)
                part = mm(value_t[head * HEAD_DIM : (head + 1) * HEAD_DIM], exponent.astype(bf16))
                tiles.append((part * (1.0 / total)).astype(bf16))
                lses.append(top + jnp.log(total))
            mixed.append(jnp.concatenate(tiles, axis=1))
            lse_ref[pl.ds(2 * at + head, 1), :] = jnp.concatenate(lses, axis=1)
        mixed_ref[:, pair_lanes(at)] = jnp.concatenate(mixed, axis=0).T

    load_out.wait()

    @pl.loop(0, width // TILE)
    def _(at):
        columns = column_tile(at)
        middle_ref[:, columns] = entry_ref[:, columns] + mm(
            mixed_ref[...], rows_view(w_out, columns)
        )


def attn_backward_body(static, *refs):
    count, ringed = static
    pieces, refs = refs[:count], refs[count:]
    grad_ref, entry_ref, qkv_ref, lse_ref = refs[:4]
    slot_col_ref, slot_row_ref, seg_col_ref, seg_row_ref, gain_ref = refs[4:9]
    out_ref, prompt_ref = refs[9:11]
    w_qkv, w_out, low_ref, mixed_ref, dqkv_ref, bias_ref, sem_a, sem_b = refs[11:]
    tokens, width = entry_ref.shape
    y_size = 1 if count == 1 else 2
    cut = 3 * width // y_size
    load_out = weight_copies(pieces, cut, width // y_size, w_out, sem_b, ringed).start()
    load_qkv = weight_copies(pieces, 0, cut, w_qkv, sem_a, ringed).start()
    low_ref[...] = grad_ref[...].astype(bf16)
    fill_bias(bias_ref, seg_col_ref, seg_row_ref)
    load_out.wait()
    mixed_ref[...] = mm_t(low_ref[...], rows_view(w_out)).astype(bf16)
    pairs = width // LANES

    @pl.loop(0, pairs)
    def _(at):
        query, key = qkv_ref[:, pair_lanes(at)], qkv_ref[:, pair_lanes(at + pairs)]
        value, grad = qkv_ref[:, pair_lanes(at + 2 * pairs)], mixed_ref[:, pair_lanes(at)]
        key_t = key.T
        d_key = jnp.zeros((tokens, LANES), f32)
        d_value = jnp.zeros((tokens, LANES), f32)
        d_query_t = []
        for head in range(2):
            query_head, grad_head = head_of(query, head), head_of(grad, head)
            lse = lse_ref[pl.ds(2 * at + head, 1), :]
            tiles = []
            for t in range(tokens // TILE):
                q_rows = slice(t * TILE, (t + 1) * TILE)
                scores = mm_t(key, query_head[q_rows]) + bias_ref[:, q_rows]
                probs = jnp.exp(scores - lse[:, q_rows])
                grad_probs = mm_t(value, grad_head[q_rows])
                inner = jnp.sum(probs * grad_probs, axis=0, keepdims=True)
                d_scores = (probs * (grad_probs - inner)).astype(bf16)
                d_value = d_value + mm(probs.astype(bf16), grad_head[q_rows])
                d_key = d_key + mm(d_scores, query_head[q_rows])
                tiles.append(mm(key_t[head * HEAD_DIM : (head + 1) * HEAD_DIM], d_scores))
            d_query_t.append(jnp.concatenate(tiles, axis=1))
        d_query = jnp.concatenate(d_query_t, axis=0) * HEAD_DIM**-0.5
        dqkv_ref[:, pair_lanes(at)] = d_query.astype(bf16).T
        dqkv_ref[:, pair_lanes(at + pairs)] = d_key.astype(bf16)
        dqkv_ref[:, pair_lanes(at + 2 * pairs)] = d_value.astype(bf16)

    load_qkv.wait()
    grad_norm = mm_t(dqkv_ref[...], rows_view(w_qkv))
    grad_entry = grad_ref[...] + norm_back(grad_norm, entry_ref[...], gain_ref[...])
    slot_total = prompt_ref.shape[0]
    onehot_t = (
        slot_row_ref[...] == lax.broadcasted_iota(jnp.int32, (slot_total, tokens), 0)
    ).astype(bf16)
    high = grad_entry.astype(bf16)
    low = (grad_entry - high.astype(f32)).astype(bf16)
    prompt_ref[...] = mm(onehot_t, high) + mm(onehot_t, low)
    out_ref[...] = jnp.where(slot_col_ref[...] < slot_total, 0.0, grad_entry)


def mlp_forward_body(static, *refs):
    count, ringed = static
    pieces, refs = refs[:count], refs[count:]
    middle_ref, gain_ref = refs[:2]
    hidden_ref, slope_ref = refs[2:4]
    w_up, w_down, norm_ref, active_ref, sem_a, sem_b = refs[4:]
    units = slope_ref.shape[1]
    width = middle_ref.shape[1]
    cut = units // (1 if count == 1 else 2)
    load_up = weight_copies(pieces, 0, cut, w_up, sem_a, ringed).start()
    load_down = weight_copies(pieces, cut, cut, w_down, sem_b, ringed).start()
    norm_ref[...] = (norm_stats(middle_ref[...])[0] * gain_ref[...]).astype(bf16)
    load_up.wait()

    @pl.loop(0, units // TILE)
    def _(at):
        columns = column_tile(at)
        before = mm(norm_ref[...], rows_view(w_up, columns))
        phi_sum, phi = gelu_parts(before)
        active_ref[:, columns] = (before * phi_sum).astype(bf16)
        slope_ref[:, columns] = (phi_sum + before * phi).astype(bf16)

    load_down.wait()
    branch = mm_t(active_ref[...], rows_view(w_down))
    hidden_ref[...] = (middle_ref[...] + branch).astype(hidden_ref.dtype)


def mlp_backward_body(static, *refs):
    count, ringed = static
    pieces, refs = refs[:count], refs[count:]
    grad_ref, middle_ref, slope_ref, gain_ref = refs[:4]
    (out_ref,) = refs[4:5]
    w_up, w_down, low_ref, before_ref, sem_a, sem_b = refs[5:]
    units = slope_ref.shape[1]
    width = middle_ref.shape[1]
    cut = units // (1 if count == 1 else 2)
    load_down = weight_copies(pieces, cut, cut, w_down, sem_b, ringed).start()
    load_up = weight_copies(pieces, 0, cut, w_up, sem_a, ringed).start()
    low_ref[...] = grad_ref[...].astype(bf16)
    load_down.wait()

    @pl.loop(0, units // TILE)
    def _(at):
        columns = column_tile(at)
        grad_active = mm(low_ref[...], rows_view(w_down, columns))
        before_ref[:, columns] = (grad_active * slope_ref[:, columns].astype(f32)).astype(bf16)

    load_up.wait()
    grad_norm = mm_t(before_ref[...], rows_view(w_up))
    back = norm_back(grad_norm, middle_ref[...], gain_ref[...])
    out_ref[...] = grad_ref[...].astype(f32) + back


def shape(dims, dtype):
    return jax.ShapeDtypeStruct(dims, dtype)


def run(body, static, pieces, inputs, outputs, scratch, flops, name):
    whole = pl.BlockSpec(memory_space=pltpu.VMEM)
    away = pl.BlockSpec(memory_space=pl.ANY)
    moved = sum(math.prod(a.shape) * a.dtype.itemsize for a in (*pieces, *inputs, *outputs))
    return pl.pallas_call(
        partial(body, (len(pieces), *static)),
        out_shape=outputs,
        in_specs=[away] * len(pieces) + [whole] * len(inputs),
        out_specs=[whole] * len(outputs),
        scratch_shapes=scratch,
        compiler_params=pltpu.CompilerParams(vmem_limit_bytes=VMEM_BYTES),
        cost_estimate=pl.CostEstimate(flops=flops, transcendentals=0, bytes_accessed=moved),
        name=name,
    )(*pieces, *inputs)


def piece_sems(pieces, ringed):
    count = len(pieces) * (pieces[0].shape[0] if ringed and len(pieces) > 1 else 1)
    return pltpu.SemaphoreType.DMA((count,))


def attn_forward(pieces, ringed, layer_at, slot_total, x, riders, marks, gain):
    tokens, width = x.shape
    pairs = width // LANES
    devices = math.prod(axis_sizes())
    takes_riders = riders is None
    outputs = (
        shape((tokens, width), f32),
        shape((tokens, 3 * width), bf16),
        shape((2 * pairs, tokens), f32),
        shape((tokens, width), f32),
    )
    inputs = (x, marks["slot_col"], marks["base"], marks["seg_col"], marks["seg_row"], gain)
    if takes_riders:
        outputs += (shape((devices, 8 * pairs, LANES), bf16),)
    else:
        inputs += (riders,)
    scratch = [
        weight_scratch(pieces, width, 3 * width),
        weight_scratch(pieces, width, width),
        pltpu.VMEM((tokens, width), bf16),
        pltpu.VMEM((tokens, width), bf16),
        pltpu.VMEM((tokens, tokens), f32),
        piece_sems(pieces, ringed),
        piece_sems(pieces, ringed),
        piece_sems(pieces, ringed),
    ]
    flops = 2 * tokens * width * (4 * width + 2 * tokens)
    static = (ringed, layer_at, slot_total, takes_riders)
    found = run(
        attn_forward_body, static, pieces, inputs, outputs, scratch, flops, "attn_forward"
    )
    return found if takes_riders else (*found, riders)


def attn_backward(pieces, ringed, grad, entry, qkv, lse, marks, gain, slot_total):
    tokens, width = entry.shape
    outputs = (shape((tokens, width), f32), shape((slot_total, width), f32))
    scratch = [
        weight_scratch(pieces, width, 3 * width),
        weight_scratch(pieces, width, width),
        pltpu.VMEM((tokens, width), bf16),
        pltpu.VMEM((tokens, width), bf16),
        pltpu.VMEM((tokens, 3 * width), bf16),
        pltpu.VMEM((tokens, tokens), f32),
        piece_sems(pieces, ringed),
        piece_sems(pieces, ringed),
    ]
    flops = 2 * tokens * width * (4 * width + 5 * tokens)
    inputs = (
        grad,
        entry,
        qkv,
        lse,
        marks["slot_col"],
        marks["slot_row"],
        marks["seg_col"],
        marks["seg_row"],
        gain,
    )
    return run(
        attn_backward_body, (ringed,), pieces, inputs, outputs, scratch, flops, "attn_backward"
    )


def mlp_forward(pieces, ringed, middle, gain, units, dtype):
    tokens, width = middle.shape
    outputs = (shape((tokens, width), dtype), shape((tokens, units), bf16))
    scratch = [
        weight_scratch(pieces, width, units),
        weight_scratch(pieces, width, units),
        pltpu.VMEM((tokens, width), bf16),
        pltpu.VMEM((tokens, units), bf16),
        piece_sems(pieces, ringed),
        piece_sems(pieces, ringed),
    ]
    flops = 4 * tokens * width * units
    return run(
        mlp_forward_body, (ringed,), pieces, (middle, gain), outputs, scratch, flops, "mlp_forward"
    )


def mlp_backward(pieces, ringed, grad, middle, slope, gain):
    tokens, width = middle.shape
    units = slope.shape[1]
    scratch = [
        weight_scratch(pieces, width, units),
        weight_scratch(pieces, width, units),
        pltpu.VMEM((tokens, width), bf16),
        pltpu.VMEM((tokens, units), bf16),
        piece_sems(pieces, ringed),
        piece_sems(pieces, ringed),
    ]
    flops = 4 * tokens * width * units
    inputs = (grad, middle, slope, gain)
    outputs = (shape((tokens, width), f32),)
    return run(
        mlp_backward_body, (ringed,), pieces, inputs, outputs, scratch, flops, "mlp_backward"
    )[0]


def axis_sizes():
    return tuple(lax.axis_size(axis) for axis in ALL)


def is_block():
    return axis_sizes() == (4, 2, 2, 2)


def flip(value, axis):
    return lax.ppermute(value, axis, [(0, 1), (1, 0)])


def turn(value, core_of_x):
    moves = []
    z_size, x_size, core_size, y_size = axis_sizes()
    for z in range(z_size):
        for x in range(x_size):
            for core in range(core_size):
                for y in range(y_size):
                    at = ((z * x_size + x) * core_size + core) * y_size + y
                    along_x = core == core_of_x
                    to_x, to_y = (1 - x, y) if along_x else (x, 1 - y)
                    moves.append((at, ((z * x_size + to_x) * core_size + core) * y_size + to_y))
    return lax.ppermute(value, ALL, moves)


def ring_z(value):
    size = lax.axis_size("z")
    parts = [value]
    for step in range(1, size):
        parts.append(lax.ppermute(value, "z", [(i, (i + step) % size) for i in range(size)]))
    return jnp.stack(parts)


def to_all(along_z):
    first = turn(along_z, 0)
    second = turn(along_z, 1)
    third = turn(first, 1)
    own = [along_z, first, second, third]
    return own + [flip(piece, "core") for piece in own]


def total_over(value):
    if not is_block():
        return lax.psum(value, ALL)
    core = lax.axis_index("core")
    low = value.astype(bf16)
    mine = jnp.where(core == 0, value[0], value[1])
    theirs = jnp.where(core == 0, low[1], low[0])
    total = mine + flip(theirs, "core").astype(f32)
    for axis in ("x", "y"):
        total = total + flip(total.astype(bf16), axis).astype(f32)
    for pairs in ([(0, 1), (1, 0), (2, 3), (3, 2)], [(0, 2), (2, 0), (1, 3), (3, 1)]):
        total = total + lax.ppermute(total.astype(bf16), "z", pairs).astype(f32)
    other = flip(total.astype(bf16), "core").astype(f32)
    return jnp.stack([jnp.where(core == 0, total, other), jnp.where(core == 0, other, total)])


def halves(values):
    high = values.astype(bf16)
    return high, (values - high.astype(f32)).astype(bf16)


def window_rows(count, width):
    step = math.gcd(count, width)
    return -(-(width - step + count) // width)


def prompt_window(prompts, width):
    count = prompts.shape[0]
    assert window_rows(count, width) <= 4
    shift = lax.axis_index(ALL) * count % width
    flat = lax.dynamic_update_slice(jnp.zeros((4 * width,), f32), prompts, (shift,))
    rows = flat.reshape(4, width // LANES, LANES).transpose(1, 0, 2)
    return jnp.concatenate(halves(rows), axis=1).reshape(-1, LANES)


def window_slots(count, width, layers):
    holders = math.prod(axis_sizes()) // layers
    base = jnp.arange(holders, dtype=jnp.int32) * count // width
    both = base[:, None] + jnp.arange(8, dtype=jnp.int32)[None, :] % 4
    return both.reshape(1, -1)


def gather_block(attn_parts, mlp_parts, window, layers):
    attn_width = attn_parts[0].shape[1]
    start = jnp.concatenate([attn_parts[0], window], axis=1)
    pieces = [to_all(ring_z(start)), to_all(lax.all_gather(mlp_parts[0], "z"))]
    for layer_at in range(1, layers):
        both = jnp.concatenate([attn_parts[layer_at], mlp_parts[layer_at]], axis=1)
        along = lax.all_gather(both, "z")
        pieces.append(to_all(along[..., :attn_width]))
        pieces.append(to_all(along[..., attn_width:]))
    return pieces, [True] + [False] * (2 * layers - 1)


def gather_any(qkv, out, up, down):
    seq = ("z", "x", "core")
    pieces = []
    for layer_at in range(qkv.shape[0]):
        attn = jnp.concatenate([qkv[layer_at], out[layer_at]], axis=1)
        pieces.append([lax.all_gather(attn, seq, tiled=True)])
        mlp = []
        for part in (up[layer_at], down[layer_at].T):
            part = lax.all_gather(part, "y", axis=1, tiled=True)
            mlp.append(lax.all_gather(part, seq, tiled=True))
        pieces.append([jnp.concatenate(mlp, axis=1)])
    return pieces, [False] * len(pieces)


def per_device(
    patches,
    segments,
    prompt_slots,
    norm_gains,
    qkv_weight,
    out_weight,
    up_weight,
    down_weight,
    cotangent,
    prompts,
    first_moment,
    second_moment,
    adam_betas,
    learn_rate,
):
    layers, _, width = norm_gains.shape
    tokens = patches.shape[0]
    units = up_weight.shape[2] * lax.axis_size("y")
    total_prompts = prompts.shape[0] * math.prod(axis_sizes())
    slot_total = total_prompts // (layers * width)
    window = prompt_window(prompts, width)
    if is_block():
        y_size, y_at = lax.axis_size("y"), lax.axis_index("y")
        rows = qkv_weight.shape[1]
        cut, out_cut = qkv_weight.shape[2] // y_size, width // y_size
        attn_parts, mlp_parts = [], []
        for layer_at in range(layers):
            qkv = lax.dynamic_slice(qkv_weight[layer_at], (0, y_at * cut), (rows, cut))
            out = lax.dynamic_slice(out_weight[layer_at], (0, y_at * out_cut), (rows, out_cut))
            attn_parts.append(jnp.concatenate([qkv, out], axis=1))
            mlp_parts.append(
                jnp.concatenate([up_weight[layer_at], down_weight[layer_at].T], axis=1)
            )
        pieces, ringed = gather_block(attn_parts, mlp_parts, window, layers)
        riders = None
    else:
        pieces, ringed = gather_any(qkv_weight, out_weight, up_weight, down_weight)
        riders = lax.all_gather(window, ALL)

    marks = {
        "base": window_slots(prompts.shape[0], width, layers),
        "slot_col": prompt_slots.reshape(tokens, 1),
        "slot_row": prompt_slots.reshape(1, tokens),
        "seg_col": segments.reshape(tokens, 1),
        "seg_row": segments.reshape(1, tokens),
    }
    gains = norm_gains.reshape(2 * layers, 1, width)
    hidden = patches
    kept = []
    for layer_at in range(layers):
        attn, mlp = 2 * layer_at, 2 * layer_at + 1
        entry, qkv, lse, middle, riders = attn_forward(
            pieces[attn],
            ringed[attn],
            layer_at,
            slot_total,
            hidden,
            riders,
            marks,
            gains[attn],
        )
        dtype = bf16 if layer_at == layers - 1 else f32
        hidden, slope = mlp_forward(pieces[mlp], ringed[mlp], middle, gains[mlp], units, dtype)
        kept.append((entry, qkv, lse, middle, slope))
    block_output = hidden
    gradient = cotangent
    layer_grads = []
    for layer_at in reversed(range(layers)):
        attn, mlp = 2 * layer_at, 2 * layer_at + 1
        entry, qkv, lse, middle, slope = kept[layer_at]
        gradient = mlp_backward(pieces[mlp], ringed[mlp], gradient, middle, slope, gains[mlp])
        gradient, layer_grad = attn_backward(
            pieces[attn], ringed[attn], gradient, entry, qkv, lse, marks, gains[attn], slot_total
        )
        layer_grads.append(layer_grad)

    prompt_grad = total_over(jnp.stack(layer_grads[::-1]))
    grad_norm = jnp.sqrt(jnp.sum(prompt_grad * prompt_grad))
    clip_limit = clip_ratio * math.sqrt(total_prompts)
    own_grads = lax.dynamic_slice(
        prompt_grad.reshape(-1), (lax.axis_index(ALL) * prompts.shape[0],), prompts.shape
    )
    clipped = own_grads * jnp.minimum(1.0, clip_limit / (grad_norm + 1e-06))
    beta_one = adam_betas[0]
    beta_two = adam_betas[1]
    step_value = float(ADAM_STEP)
    new_first = beta_one * first_moment + (1.0 - beta_one) * clipped
    new_second = beta_two * second_moment + (1.0 - beta_two) * clipped * clipped
    first_hat = new_first / (1.0 - beta_one**step_value)
    second_hat = new_second / (1.0 - beta_two**step_value)
    new_prompts = prompts - learn_rate[0] * (
        first_hat / (jnp.sqrt(second_hat) + adam_eps) + decay_rate * prompts
    )
    return (block_output, gradient, new_prompts, new_first, new_second, grad_norm.reshape(1))


def solution(mesh):
    seq_size, mlp_size = mesh.shape["seq"], mesh.shape["mlp"]
    grid = Mesh(mesh.devices.reshape(seq_size // 4, 2, 2, mlp_size), ALL)
    seq, mlp = ("z", "x", "core"), "y"
    in_specs = (
        P(ALL, None),
        P(ALL),
        P(ALL),
        P(),
        P(None, seq, None),
        P(None, seq, None),
        P(None, seq, mlp),
        P(None, mlp, seq),
        P(ALL, None),
        P(ALL),
        P(ALL),
        P(ALL),
        P(),
        P(),
    )
    out_specs = (P(ALL, None), P(ALL, None), P(ALL), P(ALL), P(ALL), P())
    return jax.shard_map(
        per_device, mesh=grid, in_specs=in_specs, out_specs=out_specs, check_vma=False
    )
```

```python
import math
from functools import partial

import jax
import jax.numpy as jnp
from jax import lax
from jax.experimental import pallas as pl
from jax.experimental.pallas import tpu as pltpu
from jax.sharding import Mesh
from jax.sharding import PartitionSpec as P

HEADS = 12
HEAD_DIM = 64
ADAM_STEP = 2

ln_eps = 1e-06
masked_score = -1e30
clip_ratio = 0.05
adam_eps = 1e-08
decay_rate = 0.1
ALL = ("z", "x", "core", "y")
f32 = jnp.float32
bf16 = jnp.bfloat16
LANES = 128
TILE = 256
VMEM_BYTES = 56 * 2**20

TAIL_SLOPE = 0.275
TAIL_POLY = (
    0.10971068582446765,
    0.1096543595961662,
    0.10219045697718625,
    0.07893593678575173,
    0.08800740710695068,
    -0.03516190352887128,
    0.13017028940734943,
    -0.11067510560848658,
    0.027167870070925505,
)


def mm(a, b):
    return jnp.dot(a, b, preferred_element_type=f32)


def mm_t(a, b):
    return lax.dot_general(a, b, (((1,), (1,)), ((), ())), preferred_element_type=f32)


def gelu_parts(v):
    a = jnp.abs(v)
    bell = jnp.exp(v * v * -0.5)
    t = 1.0 / (1.0 + TAIL_SLOPE * a)
    poly = jnp.full_like(v, TAIL_POLY[-1])
    for factor in TAIL_POLY[-2::-1]:
        poly = poly * t + factor
    tail = poly * t * bell
    return jnp.where(v >= 0.0, 1.0 - tail, tail), bell * (1.0 / math.sqrt(2.0 * math.pi))


def norm_stats(values):
    center = values - jnp.mean(values, axis=-1, keepdims=True)
    rstd = lax.rsqrt(jnp.mean(center * center, axis=-1, keepdims=True) + ln_eps)
    return center * rstd, rstd


def norm_back(grad, values, gain_row):
    unit, rstd = norm_stats(values)
    grad = grad * gain_row
    mean_grad = jnp.mean(grad, axis=-1, keepdims=True)
    mean_dot = jnp.mean(grad * unit, axis=-1, keepdims=True)
    return rstd * (grad - mean_grad - unit * mean_dot)


class Copies:
    def __init__(self, pairs, sems):
        self.copies = [
            pltpu.make_async_copy(source, target, sems.at[i])
            for i, (source, target) in enumerate(pairs)
        ]

    def start(self):
        for copy in self.copies:
            copy.start()
        return self

    def wait(self):
        for copy in self.copies:
            copy.wait()


def shards(refs, late):
    z, x, core, y = (lax.axis_index(axis) for axis in ALL)
    size = refs[0].shape[0]
    found = []
    for i, ref in enumerate(refs):
        c = core ^ (i // 4)
        for lead in range(size):
            step, back = (lead, i % 4) if late else (i % 4, lead)
            to_x, to_y = ((x, y), (x ^ 1 ^ c, y ^ c), (x ^ c, y ^ 1 ^ c), (x ^ 1, y ^ 1))[step]
            found.append((ref, lead, ((z - back) & (size - 1), to_x, c, to_y)))
    return found


def weight_copies(refs, column, width, dest, sems, late=False):
    if len(refs) == 1:
        y_size = dest.shape[-1] // width
        columns = pl.ds(column * y_size, dest.shape[-1])
        return Copies([(refs[0].at[:, columns], dest)], sems)
    rows = refs[0].shape[1]
    pairs = []
    for ref, lead, (z, x, core, y) in shards(refs, late):
        to_rows = pl.ds(pl.multiple_of((x * 2 + core) * rows, 16), rows)
        to_columns = pl.ds(pl.multiple_of(y * width, LANES), width)
        source = ref.at[lead, :, pl.ds(column, width)]
        pairs.append((source, dest.at[z, to_rows, to_columns]))
    return Copies(pairs, sems)


def rider_copies(refs, column, dest, sems):
    pairs = []
    for ref, lead, (z, x, core, y) in shards(refs, False):
        source = ref.at[lead, :, pl.ds(column, LANES)]
        pairs.append((source, dest.at[((z * 2 + x) * 2 + core) * 2 + y]))
    return Copies(pairs, sems)


def rows_view(ref, columns=None):
    value = ref[...] if columns is None else ref[..., columns]
    return value.reshape(-1, value.shape[-1])


def head_of(pair, head):
    lane = lax.broadcasted_iota(jnp.int32, pair.shape, 1)
    keep = (lane < HEAD_DIM) if head == 0 else (lane >= HEAD_DIM)
    return jnp.where(keep, pair, jnp.zeros_like(pair))


def fill_bias(bias_ref, seg_col_ref, seg_row_ref):
    bias_ref[...] = jnp.where(seg_col_ref[...] == seg_row_ref[...], 0.0, masked_score)


def copy_out(source, target, sem):
    copy = pltpu.make_async_copy(source, target, sem)
    copy.start()
    return copy


def attention(qkv_ref, bias_ref, mixed_ref, lse_ref):
    tokens, width = mixed_ref.shape
    pairs = width // LANES
    lane = lax.broadcasted_iota(jnp.int32, (tokens, LANES), 1)
    low = lane < HEAD_DIM
    lse = jnp.zeros((tokens, LANES), f32)
    for at in range(pairs):
        query, key, value = (
            qkv_ref[:, i * width + at * LANES : i * width + (at + 1) * LANES] for i in range(3)
        )
        ones = jnp.ones_like(value)
        values = (jnp.where(low, value, ones), jnp.where(low, ones, value))
        parts, tops = [], []
        for head in range(2):
            scores = mm_t(head_of(query, head), key) + bias_ref[...]
            top = jnp.max(scores, axis=1, keepdims=True)
            parts.append(mm(jnp.exp(scores - top).astype(bf16), values[head]))
            tops.append(top)
        total = pltpu.roll(jnp.where(low, parts[1], parts[0]), HEAD_DIM, 1)
        mixed = jnp.where(low, parts[0], parts[1]) / total
        mixed_ref[:, at * LANES : (at + 1) * LANES] = mixed.astype(bf16)
        pair_lse = jnp.where(low, tops[0], tops[1]) + jnp.log(total)
        lse = jnp.where((lane & (HEAD_DIM - 1)) == at, pair_lse, lse)
    lse_ref[...] = lse.T


def attention_back(qkv_ref, mixed_ref, lse_ref, bias_ref, dqkv_ref):
    tokens, width = mixed_ref.shape
    pairs = width // LANES
    for at in range(pairs):
        places = [slice(i * width + at * LANES, i * width + (at + 1) * LANES) for i in range(3)]
        query, key, value = (qkv_ref[:, place] for place in places)
        grad = mixed_ref[:, at * LANES : (at + 1) * LANES]
        found = [None, None, None]
        for head in range(2):
            query_head, key_head, grad_head = (head_of(v, head) for v in (query, key, grad))
            row = head * HEAD_DIM + at
            scores = mm_t(key, query_head) + bias_ref[...]
            probs = jnp.exp(scores - lse_ref[row : row + 1, :])
            grad_probs = mm_t(value, grad_head)
            inner = jnp.sum(probs * grad_probs, axis=0, keepdims=True)
            d_scores = (probs * (grad_probs - inner)).astype(bf16)
            for i, part in enumerate(
                (
                    mm(d_scores.T, key_head),
                    mm(d_scores, query_head),
                    mm(probs.astype(bf16), grad_head),
                )
            ):
                found[i] = part if head == 0 else found[i] + part
        found[0] = found[0] * HEAD_DIM**-0.5
        for place, part in zip(places, found):
            dqkv_ref[:, place] = part.astype(bf16)


def attn_forward_body(plan, *refs):
    count, layer_at, slot_total, takes_riders, has_down = plan
    pieces, refs = refs[:count], refs[count:]
    if has_down:
        (middle_in, active_in), refs = refs[:2], refs[2:]
    else:
        x_ref, refs = refs[0], refs[1:]
    slot_ref, base_ref, seg_col_ref, seg_row_ref, gain_ref = refs[:5]
    refs = refs[5:]
    if not takes_riders:
        rider_ref, refs = refs[0], refs[1:]
    mixed_ref, lse_ref, entry_out, qkv_out, weight_out = refs[:5]
    refs = refs[5:]
    if takes_riders:
        (rider_out, rider_ref), refs = (refs[0], refs[1]), refs[2:]
    if has_down:
        (down_out, w_down, middle_ref, active_ref, sem_down), refs = refs[:5], refs[5:]
    w_qkv, norm_ref, bias_ref, entry_ref, qkv_ref, sem_a, sem_b, sem_c = refs
    tokens, width = mixed_ref.shape
    parts = 1 if count <= 2 else 2
    cut = 3 * width // parts
    qkv_pieces, column = pieces, 0
    copies = []
    if has_down:
        units = active_ref.shape[1]
        load_middle = copy_out(middle_in, middle_ref, sem_c.at[3])
        load_active = copy_out(active_in, active_ref, sem_c.at[4])
        down_pieces = pieces
        if parts == 1:
            down_pieces, qkv_pieces = pieces[:1], pieces[1:]
        else:
            column = units // parts
        load_down = weight_copies(down_pieces, 0, units // parts, w_down, sem_down).start()
    if takes_riders:
        load_riders = rider_copies(pieces, cut, rider_ref, sem_b).start()
    load_qkv = weight_copies(qkv_pieces, column, cut, w_qkv, sem_a).start()
    fill_bias(bias_ref, seg_col_ref, seg_row_ref)
    slots = slot_ref[...]
    onehot = (slots == base_ref[...]).astype(bf16)
    is_prompt = slots < slot_total
    if takes_riders:
        load_riders.wait()
        copies.append(copy_out(rider_ref, rider_out, sem_c.at[3]))
    holders = base_ref.shape[1] // 8
    windows = rider_ref[layer_at * holders : (layer_at + 1) * holders].astype(f32)
    if has_down:
        load_middle.wait()
        load_active.wait()
        load_down.wait()
        copies.append(copy_out(w_down, down_out, sem_c.at[3]))
        entry_ref[...] = middle_ref[...] + mm_t(active_ref[...], rows_view(w_down))
        x_ref = entry_ref
    for at in range(width // LANES):
        lanes = slice(at * LANES, (at + 1) * LANES)
        part = windows[:, at * 8 : (at + 1) * 8, :].reshape(-1, LANES)
        inject = mm(onehot, part.astype(bf16))
        entry_ref[:, lanes] = jnp.where(is_prompt, inject, x_ref[:, lanes].astype(f32))
    copies.append(copy_out(entry_ref, entry_out, sem_c.at[0]))
    norm_ref[...] = (norm_stats(entry_ref[...])[0] * gain_ref[...]).astype(bf16)
    load_qkv.wait()
    copies.append(copy_out(w_qkv, weight_out, sem_c.at[1]))
    for at in range(3 * width // TILE):
        columns = slice(at * TILE, (at + 1) * TILE)
        out = mm(norm_ref[...], rows_view(w_qkv, columns))
        if at < width // TILE:
            out = out.astype(bf16).astype(f32) * HEAD_DIM**-0.5
        qkv_ref[:, columns] = out.astype(bf16)
    copies.append(copy_out(qkv_ref, qkv_out, sem_c.at[2]))
    attention(qkv_ref, bias_ref, mixed_ref, lse_ref)
    for copy in copies:
        copy.wait()


def mlp_up_body(count, *refs):
    pieces, refs = refs[:count], refs[count:]
    entry_in, mixed_ref, gain_ref = refs[:3]
    middle_out, slope_out, out_out, up_out, active_out = refs[3:8]
    w_out, w_up, norm_ref, middle_ref, active_ref, slope_ref, sem_a, sem_b, sem_d = refs[8:]
    units = slope_ref.shape[1]
    width = middle_ref.shape[1]
    parts = 1 if count == 1 else 2
    load_entry = copy_out(entry_in, middle_ref, sem_d.at[0])
    load_out = weight_copies(pieces, 0, width // parts, w_out, sem_a).start()
    load_up = weight_copies(pieces, width // parts, units // parts, w_up, sem_b).start()
    load_entry.wait()
    load_out.wait()
    middle_ref[...] = middle_ref[...] + mm(mixed_ref[...], rows_view(w_out))
    copies = [copy_out(middle_ref, middle_out, sem_d.at[0])]
    copies.append(copy_out(w_out, out_out, sem_d.at[1]))
    norm_ref[...] = (norm_stats(middle_ref[...])[0] * gain_ref[...]).astype(bf16)
    load_up.wait()
    copies.append(copy_out(w_up, up_out, sem_d.at[2]))
    for at in range(units // TILE):
        columns = slice(at * TILE, (at + 1) * TILE)
        before = mm(norm_ref[...], rows_view(w_up, columns))
        phi_sum, phi = gelu_parts(before)
        active_ref[:, columns] = (before * phi_sum).astype(bf16)
        slope_ref[:, columns] = (phi_sum + before * phi).astype(bf16)
    copies.append(copy_out(slope_ref, slope_out, sem_d.at[3]))
    copies.append(copy_out(active_ref, active_out, sem_d.at[4]))
    for copy in copies:
        copy.wait()


STATE = ("slope", "middle", "qkv", "lse", "entry")
WEIGHTS = ("down", "up", "out", "qkv_weight")


def backward_body(layers, count, late, *refs):
    down_pieces, refs = refs[:count], refs[count:]
    sources = []
    for layer_at in range(layers):
        names = STATE + (WEIGHTS if layer_at < layers - 1 else WEIGHTS[1:])
        sources.append(dict(zip(names, refs)))
        refs = refs[len(names) :]
    active_in, refs = refs[0], refs[1:]
    cotangent_ref, slot_col_ref, slot_row_ref, seg_col_ref, seg_row_ref, gain_ref = refs[:6]
    out_ref, prompt_ref, block_ref = refs[6:9]
    refs = refs[9:]
    held = dict(zip(STATE + WEIGHTS, refs))
    refs = refs[len(held) :]
    active_ref, low_ref, before_ref, grad_ref, mixed_ref, dqkv_ref, bias_ref = refs[:7]
    sem, sem_down = refs[7:]
    order = list(held)
    units = active_ref.shape[1]
    tokens, width = grad_ref.shape

    class Fetch:
        def __init__(self, name, layer_at):
            if name == "down" and layer_at == layers - 1:
                cut = units // (1 if count == 1 else 2)
                self.copies = weight_copies(down_pieces, 0, cut, held[name], sem_down, late).copies
            else:
                source, at = sources[layer_at][name], order.index(name)
                self.copies = [pltpu.make_async_copy(source, held[name], sem.at[at])]
            for copy in self.copies:
                copy.start()

        def wait(self):
            for copy in self.copies:
                copy.wait()

    names = ("down", "slope", "up", "middle", "out", "qkv", "lse", "qkv_weight", "entry")
    load_active = None
    coming = {}
    for name in names:
        coming[name] = Fetch(name, layers - 1)
        if name == "slope":
            load_active = copy_out(active_in, active_ref, sem.at[len(order)])
    fill_bias(bias_ref, seg_col_ref, seg_row_ref)
    low_ref[...] = cotangent_ref[...]
    slot_total = prompt_ref.shape[1]
    is_prompt = slot_col_ref[...] < slot_total
    onehot_t = (
        slot_row_ref[...] == lax.broadcasted_iota(jnp.int32, (slot_total, tokens), 0)
    ).astype(bf16)

    for layer_at in reversed(range(layers)):
        top = layer_at == layers - 1

        def refill(*names):
            if layer_at > 0:
                for name in names:
                    coming[name] = Fetch(name, layer_at - 1)

        coming["down"].wait()
        coming["slope"].wait()
        for at in range(units // TILE):
            columns = slice(at * TILE, (at + 1) * TILE)
            grad_active = mm(low_ref[...], rows_view(held["down"], columns))
            slope = held["slope"][:, columns].astype(f32)
            before_ref[:, columns] = (grad_active * slope).astype(bf16)
        coming["middle"].wait()
        if top:
            load_active.wait()
            branch = mm_t(active_ref[...], rows_view(held["down"]))
            block_ref[...] = (held["middle"][...] + branch).astype(bf16)
        refill("down", "slope")
        coming["up"].wait()
        grad_norm = mm_t(before_ref[...], rows_view(held["up"]))
        refill("up")
        back = norm_back(grad_norm, held["middle"][...], gain_ref[2 * layer_at + 1])
        grad = cotangent_ref[...].astype(f32) if top else grad_ref[...]
        grad_middle = grad + back
        grad_ref[...] = grad_middle
        low_ref[...] = grad_middle.astype(bf16)
        refill("middle")
        coming["out"].wait()
        mixed_ref[...] = mm_t(low_ref[...], rows_view(held["out"])).astype(bf16)
        refill("out")
        coming["qkv"].wait()
        coming["lse"].wait()
        attention_back(held["qkv"], mixed_ref, held["lse"], bias_ref, dqkv_ref)
        refill("qkv", "lse")
        coming["qkv_weight"].wait()
        grad_norm = mm_t(dqkv_ref[...], rows_view(held["qkv_weight"]))
        refill("qkv_weight")
        coming["entry"].wait()
        back = norm_back(grad_norm, held["entry"][...], gain_ref[2 * layer_at])
        grad_entry = grad_ref[...] + back
        refill("entry")
        high, low = halves(grad_entry)
        prompt_ref[layer_at] = mm(onehot_t, high) + mm(onehot_t, low)
        passed = jnp.where(is_prompt, 0.0, grad_entry)
        if layer_at > 0:
            grad_ref[...] = passed
            low_ref[...] = passed.astype(bf16)
        else:
            out_ref[...] = passed


def halves(values):
    high = values.astype(bf16)
    return high, (values - high.astype(f32)).astype(bf16)


def shape(dims, dtype):
    return jax.ShapeDtypeStruct(dims, dtype)


def skipping(body, inputs, outputs, passed):
    def kernel(*refs):
        ends = inputs, inputs + passed, inputs + passed + outputs, inputs + 2 * passed + outputs
        return body(*refs[: ends[0]], *refs[ends[1] : ends[2]], *refs[ends[3] :])

    return kernel


def run(body, away, near, outputs, outputs_away, scratch, flops, name, through=()):
    vmem = pl.BlockSpec(memory_space=pltpu.VMEM)
    anywhere = pl.BlockSpec(memory_space=pl.ANY)
    results = (*outputs, *outputs_away)
    moved = sum(math.prod(a.shape) * a.dtype.itemsize for a in (*away, *near, *results))
    taken = len(away) + len(near)
    return pl.pallas_call(
        skipping(body, taken, len(results), len(through)),
        out_shape=(*results, *(shape(a.shape, a.dtype) for a in through)),
        in_specs=[anywhere] * len(away) + [vmem] * len(near) + [anywhere] * len(through),
        out_specs=[vmem] * len(outputs) + [anywhere] * (len(outputs_away) + len(through)),
        input_output_aliases={taken + i: len(results) + i for i in range(len(through))},
        scratch_shapes=scratch,
        compiler_params=pltpu.CompilerParams(vmem_limit_bytes=VMEM_BYTES),
        cost_estimate=pl.CostEstimate(flops=flops, transcendentals=0, bytes_accessed=moved),
        name=name,
    )(*away, *near, *through)


def piece_sems(pieces):
    count = 1 if len(pieces) <= 2 else len(pieces) * 4
    return pltpu.SemaphoreType.DMA((count,))


def weight_shape(pieces, width, columns):
    return (width, columns) if len(pieces) <= 2 else (4, width // 4, columns)


def attn_forward(pieces, layer_at, slot_total, x, below, riders, marks, gain, through=()):
    tokens = marks["seg_row"].shape[1]
    width = gain.shape[1]
    takes_riders, has_down = riders is None, below is not None
    weight = weight_shape(pieces, width, 3 * width)
    near_out = (shape((tokens, width), bf16), shape((LANES, tokens), f32))
    away_out = (
        shape((tokens, width), f32),
        shape((tokens, 3 * width), bf16),
        shape(weight, bf16),
    )
    away = tuple(pieces)
    near = (marks["slot_col"], marks["base"], marks["seg_col"], marks["seg_row"], gain)
    scratch = []
    if not takes_riders:
        near += (riders,)
    else:
        rider_shape = (math.prod(axis_sizes()), 8 * width // LANES, LANES)
        away_out += (shape(rider_shape, bf16),)
        scratch.append(pltpu.VMEM(rider_shape, bf16))
    if has_down:
        units = below["active"].shape[1]
        away += (below["middle"], below["active"])
        down = weight_shape(pieces, width, units)
        away_out += (shape(down, bf16),)
        scratch += [
            pltpu.VMEM(down, bf16),
            pltpu.VMEM((tokens, width), f32),
            pltpu.VMEM((tokens, units), bf16),
            piece_sems(pieces),
        ]
    else:
        near = (x, *near)
    scratch += [
        pltpu.VMEM(weight, bf16),
        pltpu.VMEM((tokens, width), bf16),
        pltpu.VMEM((tokens, tokens), f32),
        pltpu.VMEM((tokens, width), f32),
        pltpu.VMEM((tokens, 3 * width), bf16),
        piece_sems(pieces),
        piece_sems(pieces),
        pltpu.SemaphoreType.DMA((5,)),
    ]
    flops = 2 * tokens * width * (7 * width + 2 * tokens)
    body = partial(attn_forward_body, (len(pieces), layer_at, slot_total, takes_riders, has_down))
    found = run(body, away, near, near_out, away_out, scratch, flops, "attn_forward", through)
    names = ("mixed", "lse", "entry", "qkv", "qkv_weight")
    layer = dict(zip(names, found))
    found = found[5:]
    if takes_riders:
        riders, found = found[0], found[1:]
    if has_down:
        below["down"], found = found[0], found[1:]
    return layer, riders, found


def mlp_up(pieces, layer, gain, units, through=()):
    tokens, width = layer["mixed"].shape
    out_shape, up_shape = (weight_shape(pieces, width, n) for n in (width, units))
    results = {
        "middle": shape((tokens, width), f32),
        "slope": shape((tokens, units), bf16),
        "out": shape(out_shape, bf16),
        "up": shape(up_shape, bf16),
        "active": shape((tokens, units), bf16),
    }
    scratch = [
        pltpu.VMEM(out_shape, bf16),
        pltpu.VMEM(up_shape, bf16),
        pltpu.VMEM((tokens, width), bf16),
        pltpu.VMEM((tokens, width), f32),
        pltpu.VMEM((tokens, units), bf16),
        pltpu.VMEM((tokens, units), bf16),
        piece_sems(pieces),
        piece_sems(pieces),
        pltpu.SemaphoreType.DMA((5,)),
    ]
    flops = 2 * tokens * width * (units + width)
    away = (*pieces, layer["entry"])
    near = (layer["mixed"], gain)
    body = partial(mlp_up_body, len(pieces))
    away_out = tuple(results.values())
    found = run(body, away, near, (), away_out, scratch, flops, "mlp_up", through)
    layer.update(zip(results, found))
    return found[len(results) :]


def backward(down_pieces, late, kept, cotangent, marks, gains, slot_total):
    layers = len(kept)
    tokens, width = cotangent.shape
    units = kept[0]["slope"].shape[1]
    away = list(down_pieces)
    for layer_at, layer in enumerate(kept):
        names = STATE + (WEIGHTS if layer_at < layers - 1 else WEIGHTS[1:])
        away += [layer[name] for name in names]
    away.append(kept[-1]["active"])
    near = (
        cotangent,
        marks["slot_col"],
        marks["slot_row"],
        marks["seg_col"],
        marks["seg_row"],
        gains,
    )
    outputs = (
        shape((tokens, width), f32),
        shape((layers, slot_total, width), f32),
        shape((tokens, width), bf16),
    )
    held = [kept[0][name] for name in STATE + WEIGHTS]
    scratch = [pltpu.VMEM(a.shape, a.dtype) for a in held]
    scratch += [
        pltpu.VMEM((tokens, units), bf16),
        pltpu.VMEM((tokens, width), bf16),
        pltpu.VMEM((tokens, units), bf16),
        pltpu.VMEM((tokens, width), f32),
        pltpu.VMEM((tokens, width), bf16),
        pltpu.VMEM((tokens, 3 * width), bf16),
        pltpu.VMEM((tokens, tokens), f32),
        pltpu.SemaphoreType.DMA((len(held) + 1,)),
        piece_sems(down_pieces),
    ]
    flops = 2 * layers * tokens * width * (4 * width + 3 * units + 5 * tokens)
    body = partial(backward_body, layers, len(down_pieces), late)
    return run(body, away, near, outputs, (), scratch, flops, "backward")


def axis_sizes():
    return tuple(lax.axis_size(axis) for axis in ALL)


def is_block():
    return axis_sizes() == (4, 2, 2, 2)


def flip(value, axis):
    return lax.ppermute(value, axis, [(0, 1), (1, 0)])


def turn(value, core_of_x):
    moves = []
    z_size, x_size, core_size, y_size = axis_sizes()
    for z in range(z_size):
        for x in range(x_size):
            for core in range(core_size):
                for y in range(y_size):
                    at = ((z * x_size + x) * core_size + core) * y_size + y
                    along_x = core == core_of_x
                    to_x, to_y = (1 - x, y) if along_x else (x, 1 - y)
                    moves.append((at, ((z * x_size + to_x) * core_size + core) * y_size + to_y))
    return lax.ppermute(value, ALL, moves)


def behind(value, *earlier):
    for array in earlier:
        corner = array[(0,) * array.ndim].astype(f32)
        value = value + (corner * 0.0).astype(value.dtype)
    return value


class Gather:
    def __init__(self, shard, late=False):
        self.own, self.late = shard, late

    def ring(self, *earlier):
        size = lax.axis_size("z")
        own = behind(self.own, *earlier)
        self.ringed = [own] + [
            lax.ppermute(own, "z", [(i, (i + step) % size) for i in range(size)])
            for step in range(1, size)
        ]

    def turns(self, *earlier):
        own = self.own if self.late else behind(jnp.stack(self.ringed), *earlier)
        self.turned = [own, turn(own, 0), turn(own, 1)]

    def third_turn(self):
        self.turned.append(turn(self.turned[1], 1))

    def pieces(self):
        parts = self.ringed if self.late else self.turned
        return parts + [flip(part, "core") for part in parts]


def total_over(value):
    if not is_block():
        return lax.psum(value, ALL)
    core = lax.axis_index("core")
    low = value.astype(bf16)
    mine = jnp.where(core == 0, value[0], value[1])
    theirs = jnp.where(core == 0, low[1], low[0])
    total = mine + flip(theirs, "core").astype(f32)
    for axis in ("x", "y"):
        total = total + flip(total.astype(bf16), axis).astype(f32)
    for pairs in ([(0, 1), (1, 0), (2, 3), (3, 2)], [(0, 2), (2, 0), (1, 3), (3, 1)]):
        total = total + lax.ppermute(total.astype(bf16), "z", pairs).astype(f32)
    other = flip(total.astype(bf16), "core").astype(f32)
    return jnp.stack([jnp.where(core == 0, total, other), jnp.where(core == 0, other, total)])


def window_rows(count, width):
    step = math.gcd(count, width)
    return -(-(width - step + count) // width)


def prompt_window(prompts, width):
    count = prompts.shape[0]
    assert window_rows(count, width) <= 4
    shift = lax.axis_index(ALL) * count % width
    flat = lax.dynamic_update_slice(jnp.zeros((4 * width,), f32), prompts, (shift,))
    rows = flat.reshape(4, width // LANES, LANES).transpose(1, 0, 2)
    return jnp.concatenate(halves(rows), axis=1).reshape(-1, LANES)


def window_slots(count, width, layers):
    holders = math.prod(axis_sizes()) // layers
    base = jnp.arange(holders, dtype=jnp.int32) * count // width
    both = base[:, None] + jnp.arange(8, dtype=jnp.int32)[None, :] % 4
    return both.reshape(1, -1)


def gather_any(qkv, out, up, down):
    seq = ("z", "x", "core")
    layers = qkv.shape[0]
    qkvs = [lax.all_gather(qkv[layer_at], seq, tiled=True) for layer_at in range(layers)]
    groups = [[qkvs[0]]]
    for layer_at in range(layers):
        whole_up = lax.all_gather(up[layer_at], "y", axis=1, tiled=True)
        out_up = jnp.concatenate([out[layer_at], whole_up], axis=1)
        groups.append([lax.all_gather(out_up, seq, tiled=True)])
        whole_down = lax.all_gather(down[layer_at].T, "y", axis=1, tiled=True)
        groups.append([lax.all_gather(whole_down, seq, tiled=True)] + qkvs[layer_at + 1 :][:1])
    return groups


def block_groups(qkv_weight, out_weight, up_weight, down_weight, window):
    y_size, y_at = lax.axis_size("y"), lax.axis_index("y")
    layers, rows, qkv_width = qkv_weight.shape
    cut, out_cut = qkv_width // y_size, out_weight.shape[2] // y_size
    qkv = lax.dynamic_slice(qkv_weight, (0, 0, y_at * cut), (layers, rows, cut))
    out = lax.dynamic_slice(out_weight, (0, 0, y_at * out_cut), (layers, rows, out_cut))
    groups = [jnp.concatenate([qkv[0], window], axis=1)]
    for layer_at in range(layers):
        groups.append(jnp.concatenate([out[layer_at], up_weight[layer_at]], axis=1))
        down = down_weight[layer_at].T
        if layer_at < layers - 1:
            down = jnp.concatenate([down, qkv[layer_at + 1]], axis=1)
        groups.append(down)
    return groups


def per_device(
    patches,
    segments,
    prompt_slots,
    norm_gains,
    qkv_weight,
    out_weight,
    up_weight,
    down_weight,
    cotangent,
    prompts,
    first_moment,
    second_moment,
    adam_betas,
    learn_rate,
):
    layers, _, width = norm_gains.shape
    tokens = patches.shape[0]
    units = up_weight.shape[2] * lax.axis_size("y")
    total_prompts = prompts.shape[0] * math.prod(axis_sizes())
    slot_total = total_prompts // (layers * width)
    window = prompt_window(prompts, width)
    marks = {
        "base": window_slots(prompts.shape[0], width, layers),
        "slot_col": prompt_slots.reshape(tokens, 1),
        "slot_row": prompt_slots.reshape(1, tokens),
        "seg_col": segments.reshape(tokens, 1),
        "seg_row": segments.reshape(1, tokens),
    }
    gains = norm_gains.reshape(2 * layers, 1, width)
    kept = []
    pieces = []
    state = {"riders": None}

    def forward_step(at, through=()):
        layer_at, part = divmod(at, 2)
        if part == 1:
            through = mlp_up(pieces[at], kept[layer_at], gains[2 * layer_at + 1], units, through)
            return kept[layer_at]["middle"], through
        layer, state["riders"], through = attn_forward(
            pieces[at],
            layer_at,
            slot_total,
            patches if layer_at == 0 else None,
            kept[layer_at - 1] if layer_at > 0 else None,
            state["riders"],
            marks,
            gains[2 * layer_at],
            through,
        )
        kept.append(layer)
        return layer["mixed"], through

    block = is_block()
    if block:
        groups = block_groups(qkv_weight, out_weight, up_weight, down_weight, window)
        last = len(groups) - 1
        gathers = [Gather(shard, late=i == last) for i, shard in enumerate(groups)]
        late = gathers[last]
        gathers[0].ring()
        late.turns()
        late.third_turn()
        gathers[0].turns()
        gathers[0].third_turn()
        gathers[1].ring(gathers[0].ringed[3])
        gathers[1].turns()
        gathers[1].third_turn()
        gathers[2].ring(gathers[1].ringed[3])
        gathers[2].turns()
        gathers[2].third_turn()
        late.own = jnp.stack(late.turned)
        for at in range(last):
            pieces.append(gathers[at].pieces())
            ahead = gathers[at + 3 :][:1]
            _, through = forward_step(at, tuple(gather.own for gather in ahead))
            for gather, own in zip(ahead, through):
                gather.own = own
                gather.ring()
                if not gather.late:
                    gather.turns()
                    gather.third_turn()
        pieces.append(late.pieces())
    else:
        state["riders"] = lax.all_gather(window, ALL)
        pieces = gather_any(qkv_weight, out_weight, up_weight, down_weight)
        for at in range(2 * layers):
            forward_step(at)

    gradient, layer_grads, block_output = backward(
        pieces[-1], block, kept, cotangent, marks, gains, slot_total
    )

    prompt_grad = total_over(layer_grads)
    grad_norm = jnp.sqrt(jnp.sum(prompt_grad * prompt_grad))
    clip_limit = clip_ratio * math.sqrt(total_prompts)
    own_grads = lax.dynamic_slice(
        prompt_grad.reshape(-1), (lax.axis_index(ALL) * prompts.shape[0],), prompts.shape
    )
    clipped = own_grads * jnp.minimum(1.0, clip_limit / (grad_norm + 1e-06))
    beta_one = adam_betas[0]
    beta_two = adam_betas[1]
    step_value = float(ADAM_STEP)
    new_first = beta_one * first_moment + (1.0 - beta_one) * clipped
    new_second = beta_two * second_moment + (1.0 - beta_two) * clipped * clipped
    first_hat = new_first / (1.0 - beta_one**step_value)
    second_hat = new_second / (1.0 - beta_two**step_value)
    new_prompts = prompts - learn_rate[0] * (
        first_hat / (jnp.sqrt(second_hat) + adam_eps) + decay_rate * prompts
    )
    return (block_output, gradient, new_prompts, new_first, new_second, grad_norm.reshape(1))


def solution(mesh):
    seq_size, mlp_size = mesh.shape["seq"], mesh.shape["mlp"]
    grid = Mesh(mesh.devices.reshape(seq_size // 4, 2, 2, mlp_size), ALL)
    seq, mlp = ("z", "x", "core"), "y"
    in_specs = (
        P(ALL, None),
        P(ALL),
        P(ALL),
        P(),
        P(None, seq, None),
        P(None, seq, None),
        P(None, seq, mlp),
        P(None, mlp, seq),
        P(ALL, None),
        P(ALL),
        P(ALL),
        P(ALL),
        P(),
        P(),
    )
    out_specs = (P(ALL, None), P(ALL, None), P(ALL), P(ALL), P(ALL), P())
    return jax.shard_map(
        per_device, mesh=grid, in_specs=in_specs, out_specs=out_specs, check_vma=False
    )
```

```python
import math
from functools import partial

import jax
import jax.numpy as jnp
import numpy as np
from jax import lax
from jax.experimental import pallas as pl
from jax.experimental.pallas import tpu as pltpu
from jax.sharding import Mesh
from jax.sharding import PartitionSpec as P

HEADS = 12
HEAD_DIM = 64
ADAM_STEP = 2

ln_eps = 1e-06
masked_score = -1e30
clip_ratio = 0.05
adam_eps = 1e-08
decay_rate = 0.1
ALL = ("z", "x", "core", "y")
f32 = jnp.float32
bf16 = jnp.bfloat16
LANES = 128
TILE = 256
FORWARD_VMEM = 30 * 2**20
BACKWARD_VMEM = 56 * 2**20

TAIL_SLOPE = 0.275
TAIL_POLY = (
    0.10971068582446765,
    0.1096543595961662,
    0.10219045697718625,
    0.07893593678575173,
    0.08800740710695068,
    -0.03516190352887128,
    0.13017028940734943,
    -0.11067510560848658,
    0.027167870070925505,
)


def mm(a, b):
    return jnp.dot(a, b, preferred_element_type=f32)


def mm_t(a, b):
    return lax.dot_general(a, b, (((1,), (1,)), ((), ())), preferred_element_type=f32)


def gelu_parts(v):
    a = jnp.abs(v)
    bell = jnp.exp(v * v * -0.5)
    t = 1.0 / (1.0 + TAIL_SLOPE * a)
    poly = jnp.full_like(v, TAIL_POLY[-1])
    for factor in TAIL_POLY[-2::-1]:
        poly = poly * t + factor
    tail = poly * t * bell
    return jnp.where(v >= 0.0, 1.0 - tail, tail), bell * (1.0 / math.sqrt(2.0 * math.pi))


def norm_stats(values):
    center = values - jnp.mean(values, axis=-1, keepdims=True)
    rstd = lax.rsqrt(jnp.mean(center * center, axis=-1, keepdims=True) + ln_eps)
    return center * rstd, rstd


def norm_back(grad, values, gain_row):
    unit, rstd = norm_stats(values)
    grad = grad * gain_row
    mean_grad = jnp.mean(grad, axis=-1, keepdims=True)
    mean_dot = jnp.mean(grad * unit, axis=-1, keepdims=True)
    return rstd * (grad - mean_grad - unit * mean_dot)


class Copies:
    def __init__(self, pairs, sems):
        self.copies = [
            pltpu.make_async_copy(source, target, sems.at[i])
            for i, (source, target) in enumerate(pairs)
        ]

    def start(self):
        for copy in self.copies:
            copy.start()
        return self

    def wait(self):
        for copy in self.copies:
            copy.wait()


def shards(refs):
    z, x, core, y = (lax.axis_index(axis) for axis in ALL)
    found = []
    for i, ref in enumerate(refs):
        c = core ^ i
        for step in range(4):
            to_x, to_y = ((x, y), (x ^ 1 ^ c, y ^ c), (x ^ c, y ^ 1 ^ c), (x ^ 1, y ^ 1))[step]
            for back in range(4):
                found.append((ref.at[step // 2, step % 2, back], (z ^ back, to_x, c, to_y)))
    return found


def weight_copies(refs, column, width, dest, sems):
    if refs[0].ndim == 2:
        y_size = dest.shape[-1] // width
        columns = pl.ds(column * y_size, dest.shape[-1])
        return Copies([(refs[0].at[:, columns], dest)], sems)
    rows = refs[0].shape[-2]
    pairs = []
    for ref, (z, x, core, y) in shards(refs):
        to_rows = pl.ds(pl.multiple_of((x * 2 + core) * rows, 16), rows)
        to_columns = pl.ds(pl.multiple_of(y * width, LANES), width)
        pairs.append((ref.at[:, pl.ds(column, width)], dest.at[z, to_rows, to_columns]))
    return Copies(pairs, sems)


def rider_copies(refs, column, dest, sems):
    pairs = []
    for ref, (z, x, core, y) in shards(refs):
        source = ref.at[:, pl.ds(column, LANES)]
        pairs.append((source, dest.at[((z * 2 + x) * 2 + core) * 2 + y]))
    return Copies(pairs, sems)


def rows_view(ref, columns=None):
    value = ref[...] if columns is None else ref[..., columns]
    return value.reshape(-1, value.shape[-1])


def head_of(pair, head):
    lane = lax.broadcasted_iota(jnp.int32, pair.shape, 1)
    keep = (lane < HEAD_DIM) if head == 0 else (lane >= HEAD_DIM)
    return jnp.where(keep, pair, jnp.zeros_like(pair))


def as_column(row):
    return jnp.broadcast_to(row.astype(f32), (8, row.shape[1])).T[:, :1]


def fill_bias(bias_ref, seg_ref):
    seg = seg_ref[...]
    bias_ref[...] = jnp.where(as_column(seg) == seg.astype(f32), 0.0, masked_score)


def copy_out(source, target, sem):
    copy = pltpu.make_async_copy(source, target, sem)
    copy.start()
    return copy


def attention(qkv_ref, bias_ref, mixed_ref, lse_ref):
    tokens, width = mixed_ref.shape
    pairs = width // LANES
    lane = lax.broadcasted_iota(jnp.int32, (tokens, LANES), 1)
    low = lane < HEAD_DIM
    lse = jnp.zeros((tokens, LANES), f32)
    for at in range(pairs):
        query, key, value = (
            qkv_ref[:, i * width + at * LANES : i * width + (at + 1) * LANES] for i in range(3)
        )
        ones = jnp.ones_like(value)
        values = (jnp.where(low, value, ones), jnp.where(low, ones, value))
        parts, tops = [], []
        for head in range(2):
            scores = mm_t(head_of(query, head), key) + bias_ref[...]
            top = jnp.max(scores, axis=1, keepdims=True)
            parts.append(mm(jnp.exp(scores - top).astype(bf16), values[head]))
            tops.append(top)
        total = pltpu.roll(jnp.where(low, parts[1], parts[0]), HEAD_DIM, 1)
        mixed = jnp.where(low, parts[0], parts[1]) / total
        mixed_ref[:, at * LANES : (at + 1) * LANES] = mixed.astype(bf16)
        pair_lse = jnp.where(low, tops[0], tops[1]) + jnp.log(total)
        lse = jnp.where((lane & (HEAD_DIM - 1)) == at, pair_lse, lse)
    lse_ref[...] = lse.T


def attention_back(qkv_ref, mixed_ref, lse_ref, bias_ref, dqkv_ref):
    tokens, width = mixed_ref.shape
    pairs = width // LANES
    for at in range(pairs):
        places = [slice(i * width + at * LANES, i * width + (at + 1) * LANES) for i in range(3)]
        query, key, value = (qkv_ref[:, place] for place in places)
        grad = mixed_ref[:, at * LANES : (at + 1) * LANES]
        found = [None, None, None]
        for head in range(2):
            query_head, key_head, grad_head = (head_of(v, head) for v in (query, key, grad))
            row = head * HEAD_DIM + at
            scores = mm_t(key, query_head) + bias_ref[...]
            probs = jnp.exp(scores - lse_ref[row : row + 1, :])
            grad_probs = mm_t(value, grad_head)
            inner = jnp.sum(probs * grad_probs, axis=0, keepdims=True)
            d_scores = (probs * (grad_probs - inner)).astype(bf16)
            for i, part in enumerate(
                (
                    mm(d_scores.T, key_head),
                    mm(d_scores, query_head),
                    mm(probs.astype(bf16), grad_head),
                )
            ):
                found[i] = part if head == 0 else found[i] + part
        found[0] = found[0] * HEAD_DIM**-0.5
        for place, part in zip(places, found):
            dqkv_ref[:, place] = part.astype(bf16)


def attn_forward_body(plan, *refs):
    count, layer_at, slot_total, takes_riders, has_down = plan
    pieces, refs = refs[:count], refs[count:]
    if has_down:
        (middle_in, active_in), refs = refs[:2], refs[2:]
    else:
        x_ref, refs = refs[0], refs[1:]
    slot_ref, base_ref, seg_ref, gain_ref = refs[:4]
    refs = refs[4:]
    if not takes_riders:
        rider_ref, refs = refs[0], refs[1:]
    mixed_ref, lse_ref, entry_out, qkv_out, weight_out = refs[:5]
    refs = refs[5:]
    if takes_riders:
        (rider_out, rider_ref), refs = (refs[0], refs[1]), refs[2:]
    if has_down:
        (down_out, w_down, middle_ref, active_ref, sem_down), refs = refs[:5], refs[5:]
    w_qkv, norm_ref, bias_ref, entry_ref, qkv_ref, sem_a, sem_b, sem_c = refs
    tokens, width = mixed_ref.shape
    parts = 1 if pieces[0].ndim == 2 else 2
    cut = 3 * width // parts
    qkv_pieces, column = pieces, 0
    copies = []
    if has_down:
        units = active_ref.shape[1]
        load_middle = copy_out(middle_in, middle_ref, sem_c.at[3])
        load_active = copy_out(active_in, active_ref, sem_c.at[4])
        down_pieces = pieces
        if parts == 1:
            down_pieces, qkv_pieces = pieces[:1], pieces[1:]
        else:
            column = units // parts
        load_down = weight_copies(down_pieces, 0, units // parts, w_down, sem_down).start()
    if takes_riders:
        load_riders = rider_copies(pieces, cut, rider_ref, sem_b).start()
    load_qkv = weight_copies(qkv_pieces, column, cut, w_qkv, sem_a).start()
    fill_bias(bias_ref, seg_ref)
    slots = as_column(slot_ref[...])
    onehot = (slots == base_ref[...]).astype(bf16)
    is_prompt = slots < slot_total
    if takes_riders:
        load_riders.wait()
        copies.append(copy_out(rider_ref, rider_out, sem_c.at[3]))
    holders = base_ref.shape[1] // 8
    windows = rider_ref[layer_at * holders : (layer_at + 1) * holders].astype(f32)
    if has_down:
        load_middle.wait()
        load_active.wait()
        load_down.wait()
        copies.append(copy_out(w_down, down_out, sem_c.at[3]))
        entry_ref[...] = middle_ref[...] + mm_t(active_ref[...], rows_view(w_down))
        x_ref = entry_ref
    for at in range(width // LANES):
        lanes = slice(at * LANES, (at + 1) * LANES)
        part = windows[:, at * 8 : (at + 1) * 8, :].reshape(-1, LANES)
        inject = mm(onehot, part.astype(bf16))
        entry_ref[:, lanes] = jnp.where(is_prompt, inject, x_ref[:, lanes].astype(f32))
    copies.append(copy_out(entry_ref, entry_out, sem_c.at[0]))
    norm_ref[...] = (norm_stats(entry_ref[...])[0] * gain_ref[layer_at, :1]).astype(bf16)
    load_qkv.wait()
    copies.append(copy_out(w_qkv, weight_out, sem_c.at[1]))
    for at in range(3 * width // TILE):
        columns = slice(at * TILE, (at + 1) * TILE)
        out = mm(norm_ref[...], rows_view(w_qkv, columns))
        if at < width // TILE:
            out = out.astype(bf16).astype(f32) * HEAD_DIM**-0.5
        qkv_ref[:, columns] = out.astype(bf16)
    copies.append(copy_out(qkv_ref, qkv_out, sem_c.at[2]))
    attention(qkv_ref, bias_ref, mixed_ref, lse_ref)
    for copy in copies:
        copy.wait()


def mlp_up_body(count, layer_at, *refs):
    pieces, refs = refs[:count], refs[count:]
    entry_in, mixed_ref, gain_ref = refs[:3]
    middle_out, slope_out, out_out, up_out, active_out = refs[3:8]
    w_out, w_up, norm_ref, middle_ref, active_ref, slope_ref, sem_a, sem_b, sem_d = refs[8:]
    units = slope_ref.shape[1]
    width = middle_ref.shape[1]
    parts = 1 if pieces[0].ndim == 2 else 2
    load_entry = copy_out(entry_in, middle_ref, sem_d.at[0])
    load_out = weight_copies(pieces, 0, width // parts, w_out, sem_a).start()
    load_up = weight_copies(pieces, width // parts, units // parts, w_up, sem_b).start()
    load_entry.wait()
    load_out.wait()
    middle_ref[...] = middle_ref[...] + mm(mixed_ref[...], rows_view(w_out))
    copies = [copy_out(middle_ref, middle_out, sem_d.at[0])]
    copies.append(copy_out(w_out, out_out, sem_d.at[1]))
    norm_ref[...] = (norm_stats(middle_ref[...])[0] * gain_ref[layer_at, 1:]).astype(bf16)
    load_up.wait()
    copies.append(copy_out(w_up, up_out, sem_d.at[2]))
    for at in range(units // TILE):
        columns = slice(at * TILE, (at + 1) * TILE)
        before = mm(norm_ref[...], rows_view(w_up, columns))
        phi_sum, phi = gelu_parts(before)
        active_ref[:, columns] = (before * phi_sum).astype(bf16)
        slope_ref[:, columns] = (phi_sum + before * phi).astype(bf16)
    copies.append(copy_out(slope_ref, slope_out, sem_d.at[3]))
    copies.append(copy_out(active_ref, active_out, sem_d.at[4]))
    for copy in copies:
        copy.wait()


STATE = ("slope", "middle", "qkv", "lse", "entry")
WEIGHTS = ("down", "up", "out", "qkv_weight")


def backward_body(layers, count, *refs):
    down_pieces, refs = refs[:count], refs[count:]
    sources = []
    for layer_at in range(layers):
        names = STATE + (WEIGHTS if layer_at < layers - 1 else WEIGHTS[1:])
        sources.append(dict(zip(names, refs)))
        refs = refs[len(names) :]
    active_in, refs = refs[0], refs[1:]
    cotangent_ref, slot_ref, seg_ref, gain_ref = refs[:4]
    out_ref, prompt_ref, block_ref = refs[4:7]
    refs = refs[7:]
    held = dict(zip(STATE + WEIGHTS, refs))
    refs = refs[len(held) :]
    active_ref, low_ref, before_ref, grad_ref, mixed_ref, dqkv_ref, bias_ref = refs[:7]
    sem, sem_down = refs[7:]
    order = list(held)
    units = active_ref.shape[1]
    tokens, width = grad_ref.shape

    class Fetch:
        def __init__(self, name, layer_at):
            if name == "down" and layer_at == layers - 1:
                cut = units // (1 if down_pieces[0].ndim == 2 else 2)
                self.copies = weight_copies(down_pieces, 0, cut, held[name], sem_down).copies
            else:
                source, at = sources[layer_at][name], order.index(name)
                self.copies = [pltpu.make_async_copy(source, held[name], sem.at[at])]
            for copy in self.copies:
                copy.start()

        def wait(self):
            for copy in self.copies:
                copy.wait()

    names = ("down", "slope", "up", "middle", "out", "qkv", "lse", "qkv_weight", "entry")
    load_active = None
    coming = {}
    for name in names:
        coming[name] = Fetch(name, layers - 1)
        if name == "slope":
            load_active = copy_out(active_in, active_ref, sem.at[len(order)])
    fill_bias(bias_ref, seg_ref)
    low_ref[...] = cotangent_ref[...]
    slot_total = prompt_ref.shape[1]
    is_prompt = as_column(slot_ref[...]) < slot_total
    onehot_t = (
        slot_ref[...] == lax.broadcasted_iota(jnp.int32, (slot_total, tokens), 0)
    ).astype(bf16)

    for layer_at in reversed(range(layers)):
        top = layer_at == layers - 1

        def refill(*names):
            if layer_at > 0:
                for name in names:
                    coming[name] = Fetch(name, layer_at - 1)

        coming["down"].wait()
        coming["slope"].wait()
        for at in range(units // TILE):
            columns = slice(at * TILE, (at + 1) * TILE)
            grad_active = mm(low_ref[...], rows_view(held["down"], columns))
            slope = held["slope"][:, columns].astype(f32)
            before_ref[:, columns] = (grad_active * slope).astype(bf16)
        coming["middle"].wait()
        if top:
            load_active.wait()
            branch = mm_t(active_ref[...], rows_view(held["down"]))
            block_ref[...] = (held["middle"][...] + branch).astype(bf16)
        refill("down", "slope")
        coming["up"].wait()
        grad_norm = mm_t(before_ref[...], rows_view(held["up"]))
        refill("up")
        back = norm_back(grad_norm, held["middle"][...], gain_ref[layer_at, 1:])
        grad = cotangent_ref[...].astype(f32) if top else grad_ref[...]
        grad_middle = grad + back
        grad_ref[...] = grad_middle
        low_ref[...] = grad_middle.astype(bf16)
        refill("middle")
        coming["out"].wait()
        mixed_ref[...] = mm_t(low_ref[...], rows_view(held["out"])).astype(bf16)
        refill("out")
        coming["qkv"].wait()
        coming["lse"].wait()
        attention_back(held["qkv"], mixed_ref, held["lse"], bias_ref, dqkv_ref)
        refill("qkv", "lse")
        coming["qkv_weight"].wait()
        grad_norm = mm_t(dqkv_ref[...], rows_view(held["qkv_weight"]))
        refill("qkv_weight")
        coming["entry"].wait()
        back = norm_back(grad_norm, held["entry"][...], gain_ref[layer_at, :1])
        grad_entry = grad_ref[...] + back
        refill("entry")
        high, low = halves(grad_entry)
        prompt_ref[layer_at] = mm(onehot_t, high) + mm(onehot_t, low)
        passed = jnp.where(is_prompt, 0.0, grad_entry)
        if layer_at > 0:
            grad_ref[...] = passed
            low_ref[...] = passed.astype(bf16)
        else:
            out_ref[...] = passed


def halves(values):
    high = values.astype(bf16)
    return high, (values - high.astype(f32)).astype(bf16)


def shape(dims, dtype):
    return jax.ShapeDtypeStruct(dims, dtype)


def skipping(body, taken, needed, results):
    def kernel(*refs):
        ends = taken + needed, taken + needed + results
        body(*refs[:taken], *refs[ends[0] : ends[1]], *refs[ends[1] + 1 :])
        refs[ends[1]][...] = jnp.zeros((1, 1), f32)

    return kernel


def run(body, away, near, outputs, outputs_away, scratch, flops, name, needs=(), vmem=FORWARD_VMEM):
    here = pl.BlockSpec(memory_space=pltpu.VMEM)
    anywhere = pl.BlockSpec(memory_space=pl.ANY)
    results = (*outputs, *outputs_away)
    moved = sum(math.prod(a.shape) * a.dtype.itemsize for a in (*away, *near, *results))
    return pl.pallas_call(
        skipping(body, len(away) + len(near), len(needs), len(results)),
        out_shape=(*results, shape((1, 1), f32)),
        in_specs=[anywhere] * len(away) + [here] * len(near) + [anywhere] * len(needs),
        out_specs=[here] * len(outputs) + [anywhere] * len(outputs_away) + [here],
        scratch_shapes=scratch,
        compiler_params=pltpu.CompilerParams(vmem_limit_bytes=vmem),
        cost_estimate=pl.CostEstimate(flops=flops, transcendentals=0, bytes_accessed=moved),
        name=name,
    )(*away, *near, *needs)


def zero_body(*refs):
    refs[-1][...] = jnp.zeros((1, 1), f32)


def zero_after(values):
    return pl.pallas_call(
        zero_body,
        out_shape=shape((1, 1), f32),
        in_specs=[pl.BlockSpec(memory_space=pl.ANY)] * len(values),
        out_specs=pl.BlockSpec(memory_space=pltpu.VMEM),
        compiler_params=pltpu.CompilerParams(vmem_limit_bytes=2**20),
        cost_estimate=pl.CostEstimate(flops=0, transcendentals=0, bytes_accessed=4),
        name="zero_after",
    )(*values)


def piece_sems(pieces):
    count = 1 if pieces[0].ndim == 2 else 32
    return pltpu.SemaphoreType.DMA((count,))


def weight_shape(pieces, width, columns):
    return (width, columns) if pieces[0].ndim == 2 else (4, width // 4, columns)


def attn_forward(pieces, layer_at, slot_total, x, below, riders, marks, gains, needs=()):
    tokens = marks["seg"].shape[1]
    width = gains.shape[2]
    takes_riders, has_down = riders is None, below is not None
    weight = weight_shape(pieces, width, 3 * width)
    near_out = (shape((tokens, width), bf16), shape((LANES, tokens), f32))
    away_out = (
        shape((tokens, width), f32),
        shape((tokens, 3 * width), bf16),
        shape(weight, bf16),
    )
    away = tuple(pieces)
    near = (marks["slot"], marks["base"], marks["seg"], gains)
    scratch = []
    if not takes_riders:
        near += (riders,)
    else:
        rider_shape = (math.prod(axis_sizes()), 8 * width // LANES, LANES)
        away_out += (shape(rider_shape, bf16),)
        scratch.append(pltpu.VMEM(rider_shape, bf16))
    if has_down:
        units = below["active"].shape[1]
        away += (below["middle"], below["active"])
        down = weight_shape(pieces, width, units)
        away_out += (shape(down, bf16),)
        scratch += [
            pltpu.VMEM(down, bf16),
            pltpu.VMEM((tokens, width), f32),
            pltpu.VMEM((tokens, units), bf16),
            piece_sems(pieces),
        ]
    else:
        near = (x, *near)
    scratch += [
        pltpu.VMEM(weight, bf16),
        pltpu.VMEM((tokens, width), bf16),
        pltpu.VMEM((tokens, tokens), f32),
        pltpu.VMEM((tokens, width), f32),
        pltpu.VMEM((tokens, 3 * width), bf16),
        piece_sems(pieces),
        piece_sems(pieces),
        pltpu.SemaphoreType.DMA((5,)),
    ]
    flops = 2 * tokens * width * (7 * width + 2 * tokens)
    body = partial(attn_forward_body, (len(pieces), layer_at, slot_total, takes_riders, has_down))
    found = run(body, away, near, near_out, away_out, scratch, flops, "attn_forward", needs)
    names = ("mixed", "lse", "entry", "qkv", "qkv_weight")
    layer = dict(zip(names, found))
    found = found[5:]
    if takes_riders:
        riders, found = found[0], found[1:]
    if has_down:
        below["down"], found = found[0], found[1:]
    return layer, riders, found[0]


def mlp_up(pieces, layer_at, layer, gains, units, needs=()):
    tokens, width = layer["mixed"].shape
    out_shape, up_shape = (weight_shape(pieces, width, n) for n in (width, units))
    results = {
        "middle": shape((tokens, width), f32),
        "slope": shape((tokens, units), bf16),
        "out": shape(out_shape, bf16),
        "up": shape(up_shape, bf16),
        "active": shape((tokens, units), bf16),
    }
    scratch = [
        pltpu.VMEM(out_shape, bf16),
        pltpu.VMEM(up_shape, bf16),
        pltpu.VMEM((tokens, width), bf16),
        pltpu.VMEM((tokens, width), f32),
        pltpu.VMEM((tokens, units), bf16),
        pltpu.VMEM((tokens, units), bf16),
        piece_sems(pieces),
        piece_sems(pieces),
        pltpu.SemaphoreType.DMA((5,)),
    ]
    flops = 2 * tokens * width * (units + width)
    away = (*pieces, layer["entry"])
    near = (layer["mixed"], gains)
    body = partial(mlp_up_body, len(pieces), layer_at)
    away_out = tuple(results.values())
    found = run(body, away, near, (), away_out, scratch, flops, "mlp_up", needs)
    layer.update(zip(results, found))
    return found[-1]


def backward(down_pieces, kept, cotangent, marks, gains, slot_total):
    layers = len(kept)
    tokens, width = cotangent.shape
    units = kept[0]["slope"].shape[1]
    away = list(down_pieces)
    for layer_at, layer in enumerate(kept):
        names = STATE + (WEIGHTS if layer_at < layers - 1 else WEIGHTS[1:])
        away += [layer[name] for name in names]
    away.append(kept[-1]["active"])
    near = (cotangent, marks["slot"], marks["seg"], gains)
    outputs = (
        shape((tokens, width), f32),
        shape((layers, slot_total, width), f32),
        shape((tokens, width), bf16),
    )
    held = [kept[0][name] for name in STATE + WEIGHTS]
    scratch = [pltpu.VMEM(a.shape, a.dtype) for a in held]
    scratch += [
        pltpu.VMEM((tokens, units), bf16),
        pltpu.VMEM((tokens, width), bf16),
        pltpu.VMEM((tokens, units), bf16),
        pltpu.VMEM((tokens, width), f32),
        pltpu.VMEM((tokens, width), bf16),
        pltpu.VMEM((tokens, 3 * width), bf16),
        pltpu.VMEM((tokens, tokens), f32),
        pltpu.SemaphoreType.DMA((len(held) + 1,)),
        piece_sems(down_pieces),
    ]
    flops = 2 * layers * tokens * width * (4 * width + 3 * units + 5 * tokens)
    body = partial(backward_body, layers, len(down_pieces))
    return run(body, away, near, outputs, (), scratch, flops, "backward", vmem=BACKWARD_VMEM)[:3]


def axis_sizes():
    return tuple(lax.axis_size(axis) for axis in ALL)


def is_block():
    return axis_sizes() == (4, 2, 2, 2)


def flip(value, axis):
    return lax.ppermute(value, axis, [(0, 1), (1, 0)])


def turn(value, core_of_x):
    moves = []
    z_size, x_size, core_size, y_size = axis_sizes()
    for z in range(z_size):
        for x in range(x_size):
            for core in range(core_size):
                for y in range(y_size):
                    at = ((z * x_size + x) * core_size + core) * y_size + y
                    along_x = core == core_of_x
                    to_x, to_y = (1 - x, y) if along_x else (x, 1 - y)
                    moves.append((at, ((z * x_size + to_x) * core_size + core) * y_size + to_y))
    return lax.ppermute(value, ALL, moves)


def swap_z(value, distance):
    return lax.ppermute(value, "z", [(i, i ^ distance) for i in range(lax.axis_size("z"))])


class Steps:
    def __init__(self):
        self.zero = None

    def needs(self):
        return [] if self.zero is None else [self.zero]

    def behind(self, value):
        return value if self.zero is None else value + self.zero[0, 0].astype(value.dtype)

    def join(self, parts):
        return self.behind(jnp.stack(parts))

    def wait(self, arrays):
        self.zero = zero_after([*arrays, *self.needs()])


class Gather:
    def __init__(self, steps, shard):
        self.steps, self.own = steps, shard

    def start_ring(self):
        own = self.steps.behind(self.own)
        self.parts = [own] + [swap_z(own, i) for i in (1, 2, 3)]
        return self.parts[1:]

    def first_turn(self):
        self.parts = [self.steps.join(self.parts)]
        self.parts.append(turn(self.parts[0], 0))
        return self.parts[1:]

    def second_turn(self):
        self.parts = [self.steps.join(self.parts)]
        self.parts.append(turn(self.parts[0], 1))
        return self.parts[1:]

    def last_turn(self):
        whole = self.steps.join(self.parts)
        self.pieces = [whole, flip(whole, "core")]
        return []


def total_over(value):
    if not is_block():
        return lax.psum(value, ALL)
    core = lax.axis_index("core")
    low = value.astype(bf16)
    mine = jnp.where(core == 0, value[0], value[1])
    theirs = jnp.where(core == 0, low[1], low[0])
    total = mine + flip(theirs, "core").astype(f32)
    for axis in ("x", "y"):
        total = total + flip(total.astype(bf16), axis).astype(f32)
    for pairs in ([(0, 1), (1, 0), (2, 3), (3, 2)], [(0, 2), (2, 0), (1, 3), (3, 1)]):
        total = total + lax.ppermute(total.astype(bf16), "z", pairs).astype(f32)
    other = flip(total.astype(bf16), "core").astype(f32)
    return jnp.stack([jnp.where(core == 0, total, other), jnp.where(core == 0, other, total)])


def window_rows(count, width):
    step = math.gcd(count, width)
    return -(-(width - step + count) // width)


def prompt_window(prompts, width):
    count = prompts.shape[0]
    assert window_rows(count, width) <= 4
    shift = lax.axis_index(ALL) * count % width
    flat = lax.dynamic_update_slice(jnp.zeros((4 * width,), f32), prompts, (shift,))
    rows = flat.reshape(4, width // LANES, LANES).transpose(1, 0, 2)
    return jnp.concatenate(halves(rows), axis=1).reshape(-1, LANES)


def window_slots(count, width, layers):
    holders = math.prod(axis_sizes()) // layers
    base = np.arange(holders, dtype=np.int32) * count // width
    both = base[:, None] + np.arange(8, dtype=np.int32)[None, :] % 4
    return jnp.asarray(both.reshape(1, -1), f32)


def gather_any(qkv, out, up, down):
    seq = ("z", "x", "core")
    layers = qkv.shape[0]
    qkvs = [lax.all_gather(qkv[layer_at], seq, tiled=True) for layer_at in range(layers)]
    groups = [[qkvs[0]]]
    for layer_at in range(layers):
        whole_up = lax.all_gather(up[layer_at], "y", axis=1, tiled=True)
        out_up = jnp.concatenate([out[layer_at], whole_up], axis=1)
        groups.append([lax.all_gather(out_up, seq, tiled=True)])
        whole_down = lax.all_gather(down[layer_at].T, "y", axis=1, tiled=True)
        groups.append([lax.all_gather(whole_down, seq, tiled=True)] + qkvs[layer_at + 1 :][:1])
    return groups


def block_groups(qkv_weight, out_weight, up_weight, down_weight, window):
    y_size, y_at = lax.axis_size("y"), lax.axis_index("y")
    layers, rows, qkv_width = qkv_weight.shape
    cut, out_cut = qkv_width // y_size, out_weight.shape[2] // y_size
    qkv = lax.dynamic_slice(qkv_weight, (0, 0, y_at * cut), (layers, rows, cut))
    out = lax.dynamic_slice(out_weight, (0, 0, y_at * out_cut), (layers, rows, out_cut))
    groups = [jnp.concatenate([qkv[0], window], axis=1)]
    for layer_at in range(layers):
        groups.append(jnp.concatenate([out[layer_at], up_weight[layer_at]], axis=1))
        down = down_weight[layer_at].T
        if layer_at < layers - 1:
            down = jnp.concatenate([down, qkv[layer_at + 1]], axis=1)
        groups.append(down)
    return groups


def per_device(
    patches,
    segments,
    prompt_slots,
    norm_gains,
    qkv_weight,
    out_weight,
    up_weight,
    down_weight,
    cotangent,
    prompts,
    first_moment,
    second_moment,
    adam_betas,
    learn_rate,
):
    layers, _, width = norm_gains.shape
    tokens = patches.shape[0]
    units = up_weight.shape[2] * lax.axis_size("y")
    total_prompts = prompts.shape[0] * math.prod(axis_sizes())
    slot_total = total_prompts // (layers * width)
    window = prompt_window(prompts, width)
    marks = {
        "base": window_slots(prompts.shape[0], width, layers),
        "slot": prompt_slots.reshape(1, tokens),
        "seg": segments.reshape(1, tokens),
    }
    kept = []
    pieces = []
    state = {"riders": None}

    def forward_step(at, needs=()):
        layer_at, part = divmod(at, 2)
        if part == 1:
            return mlp_up(pieces[at], layer_at, kept[layer_at], norm_gains, units, needs)
        layer, state["riders"], zero = attn_forward(
            pieces[at],
            layer_at,
            slot_total,
            patches if layer_at == 0 else None,
            kept[layer_at - 1] if layer_at > 0 else None,
            state["riders"],
            marks,
            norm_gains,
            needs,
        )
        kept.append(layer)
        return zero

    block = is_block()
    if block:
        steps = Steps()
        groups = block_groups(qkv_weight, out_weight, up_weight, down_weight, window)
        gathers = [Gather(steps, shard) for shard in groups]

        def kernel(at):
            pieces.append(gathers[at].pieces)
            steps.zero = forward_step(at, steps.needs())

        ring, first, second, last = (
            Gather.start_ring,
            Gather.first_turn,
            Gather.second_turn,
            Gather.last_turn,
        )
        for moves, beside in (
            ([(ring, 0)], None),
            ([(first, 0)], None),
            ([(second, 0), (ring, 1)], None),
            ([(last, 0), (first, 1), (ring, 2)], 0),
            ([(second, 1), (first, 2), (ring, 3)], None),
            ([(last, 1), (second, 2), (first, 3), (ring, 4)], 1),
            ([(last, 2), (second, 3), (first, 4)], 2),
            ([(last, 3), (second, 4)], 3),
            ([(last, 4)], None),
        ):
            coming = [array for move, at in moves for array in move(gathers[at])]
            if beside is not None:
                kernel(beside)
            if coming:
                steps.wait(coming)
        pieces.append(gathers[4].pieces)
    else:
        state["riders"] = lax.all_gather(window, ALL)
        pieces = gather_any(qkv_weight, out_weight, up_weight, down_weight)
        for at in range(2 * layers):
            forward_step(at)

    gradient, layer_grads, block_output = backward(
        pieces[-1], kept, cotangent, marks, norm_gains, slot_total
    )

    prompt_grad = total_over(layer_grads)
    grad_norm = jnp.sqrt(jnp.sum(prompt_grad * prompt_grad))
    clip_limit = clip_ratio * math.sqrt(total_prompts)
    own_grads = lax.dynamic_slice(
        prompt_grad.reshape(-1), (lax.axis_index(ALL) * prompts.shape[0],), prompts.shape
    )
    clipped = own_grads * jnp.minimum(1.0, clip_limit / (grad_norm + 1e-06))
    beta_one = adam_betas[0]
    beta_two = adam_betas[1]
    step_value = float(ADAM_STEP)
    new_first = beta_one * first_moment + (1.0 - beta_one) * clipped
    new_second = beta_two * second_moment + (1.0 - beta_two) * clipped * clipped
    first_hat = new_first / (1.0 - beta_one**step_value)
    second_hat = new_second / (1.0 - beta_two**step_value)
    new_prompts = prompts - learn_rate[0] * (
        first_hat / (jnp.sqrt(second_hat) + adam_eps) + decay_rate * prompts
    )
    return (block_output, gradient, new_prompts, new_first, new_second, grad_norm.reshape(1))


def solution(mesh):
    seq_size, mlp_size = mesh.shape["seq"], mesh.shape["mlp"]
    grid = Mesh(mesh.devices.reshape(seq_size // 4, 2, 2, mlp_size), ALL)
    seq, mlp = ("z", "x", "core"), "y"
    in_specs = (
        P(ALL, None),
        P(ALL),
        P(ALL),
        P(),
        P(None, seq, None),
        P(None, seq, None),
        P(None, seq, mlp),
        P(None, mlp, seq),
        P(ALL, None),
        P(ALL),
        P(ALL),
        P(ALL),
        P(),
        P(),
    )
    out_specs = (P(ALL, None), P(ALL, None), P(ALL), P(ALL), P(ALL), P())
    return jax.shard_map(
        per_device, mesh=grid, in_specs=in_specs, out_specs=out_specs, check_vma=False
    )
```

```python
import math
from functools import partial

import jax
import jax.numpy as jnp
import numpy as np
from jax import lax
from jax.experimental import pallas as pl
from jax.experimental.pallas import tpu as pltpu
from jax.sharding import Mesh
from jax.sharding import PartitionSpec as P

HEADS = 12
HEAD_DIM = 64
ADAM_STEP = 2

ln_eps = 1e-06
masked_score = -1e30
clip_ratio = 0.05
adam_eps = 1e-08
decay_rate = 0.1
ALL = ("z", "x", "core", "y")
f32 = jnp.float32
bf16 = jnp.bfloat16
LANES = 128
TILE = 256
FORWARD_VMEM = 30 * 2**20
BACKWARD_VMEM = 41 * 2**20

TAIL_SLOPE = 0.275
TAIL_POLY = (
    0.10971068582446765,
    0.1096543595961662,
    0.10219045697718625,
    0.07893593678575173,
    0.08800740710695068,
    -0.03516190352887128,
    0.13017028940734943,
    -0.11067510560848658,
    0.027167870070925505,
)


def mm(a, b):
    return jnp.dot(a, b, preferred_element_type=f32)


def mm_t(a, b):
    return lax.dot_general(a, b, (((1,), (1,)), ((), ())), preferred_element_type=f32)


def gelu_parts(v):
    a = jnp.abs(v)
    bell = jnp.exp(v * v * -0.5)
    t = 1.0 / (1.0 + TAIL_SLOPE * a)
    poly = jnp.full_like(v, TAIL_POLY[-1])
    for factor in TAIL_POLY[-2::-1]:
        poly = poly * t + factor
    tail = poly * t * bell
    return jnp.where(v >= 0.0, 1.0 - tail, tail), bell * (1.0 / math.sqrt(2.0 * math.pi))


def norm_stats(values):
    center = values - jnp.mean(values, axis=-1, keepdims=True)
    rstd = lax.rsqrt(jnp.mean(center * center, axis=-1, keepdims=True) + ln_eps)
    return center * rstd, rstd


def norm_back(grad, values, gain_row):
    unit, rstd = norm_stats(values)
    grad = grad * gain_row
    mean_grad = jnp.mean(grad, axis=-1, keepdims=True)
    mean_dot = jnp.mean(grad * unit, axis=-1, keepdims=True)
    return rstd * (grad - mean_grad - unit * mean_dot)


class Copies:
    def __init__(self, pairs, sems):
        self.copies = [
            pltpu.make_async_copy(source, target, sems.at[i])
            for i, (source, target) in enumerate(pairs)
        ]

    def start(self):
        for copy in self.copies:
            copy.start()
        return self

    def wait(self):
        for copy in self.copies:
            copy.wait()


def shards(refs, late):
    z, x, core, y = (lax.axis_index(axis) for axis in ALL)
    found = []
    for i, ref in enumerate(refs):
        c = core ^ i
        for step in range(4):
            to_x, to_y = ((x, y), (x ^ 1 ^ c, y ^ c), (x ^ c, y ^ 1 ^ c), (x ^ 1, y ^ 1))[step]
            for back in range(4):
                at = (step // 2, step % 2)
                at = (back, *at) if late else (*at, back)
                found.append((ref.at[at], (z ^ back, to_x, c, to_y)))
    return found


def weight_copies(refs, column, width, dest, sems, late=False):
    if refs[0].ndim == 2:
        y_size = dest.shape[-1] // width
        columns = pl.ds(column * y_size, dest.shape[-1])
        return Copies([(refs[0].at[:, columns], dest)], sems)
    rows = refs[0].shape[-2]
    pairs = []
    for ref, (z, x, core, y) in shards(refs, late):
        to_rows = pl.ds(pl.multiple_of((x * 2 + core) * rows, 16), rows)
        to_columns = pl.ds(pl.multiple_of(y * width, LANES), width)
        pairs.append((ref.at[:, pl.ds(column, width)], dest.at[z, to_rows, to_columns]))
    return Copies(pairs, sems)


def rider_copies(refs, column, dest, sems):
    pairs = []
    for ref, (z, x, core, y) in shards(refs, False):
        source = ref.at[:, pl.ds(column, LANES)]
        pairs.append((source, dest.at[((z * 2 + x) * 2 + core) * 2 + y]))
    return Copies(pairs, sems)


def rows_view(ref, columns=None):
    value = ref[...] if columns is None else ref[..., columns]
    return value.reshape(-1, value.shape[-1])


def head_of(pair, head):
    lane = lax.broadcasted_iota(jnp.int32, pair.shape, 1)
    keep = (lane < HEAD_DIM) if head == 0 else (lane >= HEAD_DIM)
    return jnp.where(keep, pair, jnp.zeros_like(pair))


def as_column(row):
    return jnp.broadcast_to(row.astype(f32), (8, row.shape[1])).T[:, :1]


def fill_bias(bias_ref, seg_ref):
    seg = seg_ref[...]
    bias_ref[...] = jnp.where(as_column(seg) == seg.astype(f32), 0.0, masked_score)


def copy_out(source, target, sem):
    copy = pltpu.make_async_copy(source, target, sem)
    copy.start()
    return copy


def attention(qkv_ref, bias_ref, mixed_ref, lse_ref):
    tokens, width = mixed_ref.shape
    pairs = width // LANES
    lane = lax.broadcasted_iota(jnp.int32, (tokens, LANES), 1)
    low = lane < HEAD_DIM
    lse = jnp.zeros((tokens, LANES), f32)
    for at in range(pairs):
        query, key, value = (
            qkv_ref[:, i * width + at * LANES : i * width + (at + 1) * LANES] for i in range(3)
        )
        ones = jnp.ones_like(value)
        values = (jnp.where(low, value, ones), jnp.where(low, ones, value))
        parts, tops = [], []
        for head in range(2):
            scores = mm_t(head_of(query, head), key) + bias_ref[...]
            top = jnp.max(scores, axis=1, keepdims=True)
            parts.append(mm(jnp.exp(scores - top).astype(bf16), values[head]))
            tops.append(top)
        total = pltpu.roll(jnp.where(low, parts[1], parts[0]), HEAD_DIM, 1)
        mixed = jnp.where(low, parts[0], parts[1]) / total
        mixed_ref[:, at * LANES : (at + 1) * LANES] = mixed.astype(bf16)
        pair_lse = jnp.where(low, tops[0], tops[1]) + jnp.log(total)
        lse = jnp.where((lane & (HEAD_DIM - 1)) == at, pair_lse, lse)
    lse_ref[...] = lse.T


def attention_back(qkv_ref, mixed_ref, lse_ref, bias_ref, dqkv_ref):
    tokens, width = mixed_ref.shape
    pairs = width // LANES
    for at in range(pairs):
        places = [slice(i * width + at * LANES, i * width + (at + 1) * LANES) for i in range(3)]
        query, key, value = (qkv_ref[:, place] for place in places)
        grad = mixed_ref[:, at * LANES : (at + 1) * LANES]
        found = [None, None, None]
        for head in range(2):
            query_head, key_head, grad_head = (head_of(v, head) for v in (query, key, grad))
            row = head * HEAD_DIM + at
            scores = mm_t(key, query_head) + bias_ref[...]
            probs = jnp.exp(scores - lse_ref[row : row + 1, :])
            grad_probs = mm_t(value, grad_head)
            inner = jnp.sum(probs * grad_probs, axis=0, keepdims=True)
            d_scores = (probs * (grad_probs - inner)).astype(bf16)
            for i, part in enumerate(
                (
                    mm(d_scores.T, key_head),
                    mm(d_scores, query_head),
                    mm(probs.astype(bf16), grad_head),
                )
            ):
                found[i] = part if head == 0 else found[i] + part
        found[0] = found[0] * HEAD_DIM**-0.5
        for place, part in zip(places, found):
            dqkv_ref[:, place] = part.astype(bf16)


def attn_forward_body(plan, *refs):
    count, layer_at, slot_total, takes_riders, has_down = plan
    pieces, refs = refs[:count], refs[count:]
    if has_down:
        (middle_in, active_in), refs = refs[:2], refs[2:]
    else:
        x_ref, refs = refs[0], refs[1:]
    slot_ref, base_ref, seg_ref, gain_ref = refs[:4]
    refs = refs[4:]
    if not takes_riders:
        rider_ref, refs = refs[0], refs[1:]
    mixed_ref, lse_ref, entry_out, qkv_out, weight_out = refs[:5]
    refs = refs[5:]
    if takes_riders:
        (rider_out, rider_ref), refs = (refs[0], refs[1]), refs[2:]
    if has_down:
        (down_out, w_down, middle_ref, active_ref, sem_down), refs = refs[:5], refs[5:]
    w_qkv, norm_ref, bias_ref, entry_ref, qkv_ref, sem_a, sem_b, sem_c = refs
    tokens, width = mixed_ref.shape
    parts = 1 if pieces[0].ndim == 2 else 2
    cut = 3 * width // parts
    qkv_pieces, column = pieces, 0
    copies = []
    if has_down:
        units = active_ref.shape[1]
        load_middle = copy_out(middle_in, middle_ref, sem_c.at[3])
        load_active = copy_out(active_in, active_ref, sem_c.at[4])
        down_pieces = pieces
        if parts == 1:
            down_pieces, qkv_pieces = pieces[:1], pieces[1:]
        else:
            column = units // parts
        load_down = weight_copies(down_pieces, 0, units // parts, w_down, sem_down).start()
    if takes_riders:
        load_riders = rider_copies(pieces, cut, rider_ref, sem_b).start()
    load_qkv = weight_copies(qkv_pieces, column, cut, w_qkv, sem_a).start()
    fill_bias(bias_ref, seg_ref)
    slots = as_column(slot_ref[...])
    onehot = (slots == base_ref[...]).astype(bf16)
    is_prompt = slots < slot_total
    if takes_riders:
        load_riders.wait()
        copies.append(copy_out(rider_ref, rider_out, sem_c.at[3]))
    holders = base_ref.shape[1] // 8
    windows = rider_ref[layer_at * holders : (layer_at + 1) * holders].astype(f32)
    if has_down:
        load_middle.wait()
        load_active.wait()
        load_down.wait()
        copies.append(copy_out(w_down, down_out, sem_c.at[3]))
        entry_ref[...] = middle_ref[...] + mm_t(active_ref[...], rows_view(w_down))
        x_ref = entry_ref
    for at in range(width // LANES):
        lanes = slice(at * LANES, (at + 1) * LANES)
        part = windows[:, at * 8 : (at + 1) * 8, :].reshape(-1, LANES)
        inject = mm(onehot, part.astype(bf16))
        entry_ref[:, lanes] = jnp.where(is_prompt, inject, x_ref[:, lanes].astype(f32))
    copies.append(copy_out(entry_ref, entry_out, sem_c.at[0]))
    norm_ref[...] = (norm_stats(entry_ref[...])[0] * gain_ref[layer_at, :1]).astype(bf16)
    load_qkv.wait()
    copies.append(copy_out(w_qkv, weight_out, sem_c.at[1]))
    for at in range(3 * width // TILE):
        columns = slice(at * TILE, (at + 1) * TILE)
        out = mm(norm_ref[...], rows_view(w_qkv, columns))
        if at < width // TILE:
            out = out.astype(bf16).astype(f32) * HEAD_DIM**-0.5
        qkv_ref[:, columns] = out.astype(bf16)
    copies.append(copy_out(qkv_ref, qkv_out, sem_c.at[2]))
    attention(qkv_ref, bias_ref, mixed_ref, lse_ref)
    for copy in copies:
        copy.wait()


def mlp_up_body(layer_at, top, *refs):
    count = 1 if refs[0].ndim == 2 else 2
    pieces, refs = refs[:count], refs[count:]
    entry_in, mixed_ref, gain_ref = refs[:3]
    refs = refs[3:]
    if top:
        (middle_ref, slope_ref, active_ref), refs = refs[:3], refs[3:]
        w_out, w_up, norm_ref, sem_a, sem_b, sem_d = refs
    else:
        middle_out, slope_out, out_out, up_out, active_out = refs[:5]
        w_out, w_up, norm_ref, sem_a, sem_b, sem_d, middle_ref, slope_ref, active_ref = refs[5:]
    units = slope_ref.shape[1]
    width = middle_ref.shape[1]
    load_entry = copy_out(entry_in, middle_ref, sem_d.at[0])
    load_out = weight_copies(pieces, 0, width // count, w_out, sem_a).start()
    load_up = weight_copies(pieces, width // count, units // count, w_up, sem_b).start()
    load_entry.wait()
    load_out.wait()
    middle_ref[...] = middle_ref[...] + mm(mixed_ref[...], rows_view(w_out))
    copies = []
    if not top:
        copies.append(copy_out(middle_ref, middle_out, sem_d.at[0]))
        copies.append(copy_out(w_out, out_out, sem_d.at[1]))
    norm_ref[...] = (norm_stats(middle_ref[...])[0] * gain_ref[layer_at, 1:]).astype(bf16)
    load_up.wait()
    if not top:
        copies.append(copy_out(w_up, up_out, sem_d.at[2]))
    for at in range(units // TILE):
        columns = slice(at * TILE, (at + 1) * TILE)
        before = mm(norm_ref[...], rows_view(w_up, columns))
        phi_sum, phi = gelu_parts(before)
        active_ref[:, columns] = (before * phi_sum).astype(bf16)
        slope_ref[:, columns] = (phi_sum + before * phi).astype(bf16)
    if not top:
        copies.append(copy_out(slope_ref, slope_out, sem_d.at[3]))
        copies.append(copy_out(active_ref, active_out, sem_d.at[4]))
    for copy in copies:
        copy.wait()


STATE = ("slope", "middle", "qkv", "lse", "entry")
WEIGHTS = ("down", "up", "out", "qkv_weight")
TOP = (*STATE, "qkv_weight")


def backward_body(layers, counts, *refs):
    down_pieces, refs = refs[: counts[0]], refs[counts[0] :]
    up_pieces, refs = refs[: counts[1]], refs[counts[1] :]
    sources = []
    for layer_at in range(layers):
        names = STATE + WEIGHTS if layer_at < layers - 1 else TOP
        sources.append(dict(zip(names, refs)))
        refs = refs[len(names) :]
    active_in, cotangent_ref, slot_ref, seg_ref, gain_ref = refs[:5]
    out_ref, prompt_ref, block_ref = refs[5:8]
    refs = refs[8:]
    held = dict(zip(STATE + WEIGHTS, refs))
    refs = refs[len(held) :]
    low_ref, before_ref, grad_ref, mixed_ref, dqkv_ref, bias_ref = refs[:6]
    sem, sem_down, sem_up, sem_out = refs[6:]
    order = list(held)
    tokens, width = grad_ref.shape
    units = before_ref.shape[1]
    parts = 1 if down_pieces[0].ndim == 2 else 2
    top_weights = {
        "down": (down_pieces, 0, units // parts, sem_down, True),
        "up": (up_pieces, width // parts, units // parts, sem_up, False),
        "out": (up_pieces, 0, width // parts, sem_out, False),
    }

    class Fetch:
        def __init__(self, name, layer_at):
            if layer_at == layers - 1 and name in top_weights:
                refs, column, count, sems, late = top_weights[name]
                self.copies = weight_copies(refs, column, count, held[name], sems, late).copies
            else:
                source, at = sources[layer_at][name], order.index(name)
                self.copies = [pltpu.make_async_copy(source, held[name], sem.at[at])]
            for copy in self.copies:
                copy.start()

        def wait(self):
            for copy in self.copies:
                copy.wait()

    coming = {}

    def fetch(layer_at, *names):
        for name in names if layer_at >= 0 else ():
            coming[name] = Fetch(name, layer_at)

    def arrived(*names):
        for name in names:
            if name in coming:
                coming.pop(name).wait()

    load_active = copy_out(active_in, before_ref, sem.at[len(order)])
    fetch(layers - 1, "down", "middle", "slope")
    fill_bias(bias_ref, seg_ref)
    low_ref[...] = cotangent_ref[...]
    slot_total = prompt_ref.shape[1]
    is_prompt = as_column(slot_ref[...]) < slot_total
    onehot_t = (
        slot_ref[...] == lax.broadcasted_iota(jnp.int32, (slot_total, tokens), 0)
    ).astype(bf16)

    for layer_at in reversed(range(layers)):
        top = layer_at == layers - 1

        below = layer_at - 1
        arrived("down")
        fetch(layer_at, "up")
        if top:
            arrived("middle")
            load_active.wait()
            branch = mm_t(before_ref[...], rows_view(held["down"]))
            block_ref[...] = (held["middle"][...] + branch).astype(bf16)
        arrived("slope")
        for at in range(units // TILE):
            columns = slice(at * TILE, (at + 1) * TILE)
            grad_active = mm(low_ref[...], rows_view(held["down"], columns))
            slope = held["slope"][:, columns].astype(f32)
            before_ref[:, columns] = (grad_active * slope).astype(bf16)
        arrived("up", "middle")
        fetch(layer_at, "out", "qkv", "lse")
        grad_norm = mm_t(before_ref[...], rows_view(held["up"]))
        back = norm_back(grad_norm, held["middle"][...], gain_ref[layer_at, 1:])
        grad = cotangent_ref[...].astype(f32) if top else grad_ref[...]
        grad_middle = grad + back
        grad_ref[...] = grad_middle
        low_ref[...] = grad_middle.astype(bf16)
        arrived("out", "qkv", "lse")
        fetch(layer_at, "qkv_weight", "entry")
        fetch(below, "down", "slope", "middle")
        mixed_ref[...] = mm_t(low_ref[...], rows_view(held["out"])).astype(bf16)
        attention_back(held["qkv"], mixed_ref, held["lse"], bias_ref, dqkv_ref)
        arrived("qkv_weight", "entry")
        grad_norm = mm_t(dqkv_ref[...], rows_view(held["qkv_weight"]))
        back = norm_back(grad_norm, held["entry"][...], gain_ref[layer_at, :1])
        grad_entry = grad_ref[...] + back
        high, low = halves(grad_entry)
        prompt_ref[layer_at] = mm(onehot_t, high) + mm(onehot_t, low)
        passed = jnp.where(is_prompt, 0.0, grad_entry)
        if layer_at > 0:
            grad_ref[...] = passed
            low_ref[...] = passed.astype(bf16)
        else:
            out_ref[...] = passed


def halves(values):
    high = values.astype(bf16)
    return high, (values - high.astype(f32)).astype(bf16)


def shape(dims, dtype):
    return jax.ShapeDtypeStruct(dims, dtype)


def skipping(body, taken, needed, results):
    def kernel(*refs):
        ends = taken + needed, taken + needed + results
        body(*refs[:taken], *refs[ends[0] : ends[1]], *refs[ends[1] + 1 :])
        refs[ends[1]][...] = jnp.zeros((1, 1), f32)

    return kernel


def run(body, away, near, outputs, outputs_away, scratch, flops, name, needs=(), vmem=FORWARD_VMEM):
    here = pl.BlockSpec(memory_space=pltpu.VMEM)
    hbm = pl.BlockSpec(memory_space=pltpu.HBM)
    anywhere = pl.BlockSpec(memory_space=pl.ANY)
    results = (*outputs, *outputs_away)
    moved = sum(math.prod(a.shape) * a.dtype.itemsize for a in (*away, *near, *results))
    return pl.pallas_call(
        skipping(body, len(away) + len(near), len(needs), len(results)),
        out_shape=(*results, shape((1, 1), f32)),
        in_specs=[anywhere] * len(away) + [here] * len(near) + [anywhere] * len(needs),
        out_specs=[here] * len(outputs) + [hbm] * len(outputs_away) + [here],
        scratch_shapes=scratch,
        compiler_params=pltpu.CompilerParams(vmem_limit_bytes=vmem),
        cost_estimate=pl.CostEstimate(flops=flops, transcendentals=0, bytes_accessed=moved),
        name=name,
    )(*away, *near, *needs)


def zero_body(*refs):
    refs[-1][...] = jnp.zeros((1, 1), f32)


def zero_after(values):
    return pl.pallas_call(
        zero_body,
        out_shape=shape((1, 1), f32),
        in_specs=[pl.BlockSpec(memory_space=pl.ANY)] * len(values),
        out_specs=pl.BlockSpec(memory_space=pltpu.VMEM),
        compiler_params=pltpu.CompilerParams(vmem_limit_bytes=2**20),
        cost_estimate=pl.CostEstimate(flops=0, transcendentals=0, bytes_accessed=4),
        name="zero_after",
    )(*values)


def piece_sems(pieces):
    count = 1 if pieces[0].ndim == 2 else 32
    return pltpu.SemaphoreType.DMA((count,))


def weight_shape(pieces, width, columns):
    return (width, columns) if pieces[0].ndim == 2 else (4, width // 4, columns)


def attn_forward(pieces, layer_at, slot_total, x, below, riders, marks, gains, needs=()):
    tokens = marks["seg"].shape[1]
    width = gains.shape[2]
    takes_riders, has_down = riders is None, below is not None
    weight = weight_shape(pieces, width, 3 * width)
    near_out = (shape((tokens, width), bf16), shape((LANES, tokens), f32))
    away_out = (
        shape((tokens, width), f32),
        shape((tokens, 3 * width), bf16),
        shape(weight, bf16),
    )
    away = tuple(pieces)
    near = (marks["slot"], marks["base"], marks["seg"], gains)
    scratch = []
    if not takes_riders:
        near += (riders,)
    else:
        rider_shape = (math.prod(axis_sizes()), 8 * width // LANES, LANES)
        away_out += (shape(rider_shape, bf16),)
        scratch.append(pltpu.VMEM(rider_shape, bf16))
    if has_down:
        units = below["active"].shape[1]
        away += (below["middle"], below["active"])
        down = weight_shape(pieces, width, units)
        away_out += (shape(down, bf16),)
        scratch += [
            pltpu.VMEM(down, bf16),
            pltpu.VMEM((tokens, width), f32),
            pltpu.VMEM((tokens, units), bf16),
            piece_sems(pieces),
        ]
    else:
        near = (x, *near)
    scratch += [
        pltpu.VMEM(weight, bf16),
        pltpu.VMEM((tokens, width), bf16),
        pltpu.VMEM((tokens, tokens), f32),
        pltpu.VMEM((tokens, width), f32),
        pltpu.VMEM((tokens, 3 * width), bf16),
        piece_sems(pieces),
        piece_sems(pieces),
        pltpu.SemaphoreType.DMA((5,)),
    ]
    flops = 2 * tokens * width * (7 * width + 2 * tokens)
    body = partial(attn_forward_body, (len(pieces), layer_at, slot_total, takes_riders, has_down))
    found = run(body, away, near, near_out, away_out, scratch, flops, "attn_forward", needs)
    names = ("mixed", "lse", "entry", "qkv", "qkv_weight")
    layer = dict(zip(names, found))
    found = found[5:]
    if takes_riders:
        riders, found = found[0], found[1:]
    if has_down:
        below["down"], found = found[0], found[1:]
    return layer, riders, found[0]


def mlp_up(pieces, layer_at, layer, gains, units, top, needs=()):
    tokens, width = layer["mixed"].shape
    out_shape, up_shape = (weight_shape(pieces, width, n) for n in (width, units))
    state = {
        "middle": shape((tokens, width), f32),
        "slope": shape((tokens, units), bf16),
        "active": shape((tokens, units), bf16),
    }
    scratch = [
        pltpu.VMEM(out_shape, bf16),
        pltpu.VMEM(up_shape, bf16),
        pltpu.VMEM((tokens, width), bf16),
        piece_sems(pieces),
        piece_sems(pieces),
        pltpu.SemaphoreType.DMA((5,)),
    ]
    if top:
        results, outputs, away_out = state, tuple(state.values()), ()
    else:
        weights = {"out": shape(out_shape, bf16), "up": shape(up_shape, bf16)}
        names = ("middle", "slope", "out", "up", "active")
        results = {name: {**state, **weights}[name] for name in names}
        outputs, away_out = (), tuple(results.values())
        scratch += [pltpu.VMEM(a.shape, a.dtype) for a in state.values()]
    flops = 2 * tokens * width * (units + width)
    away = (*pieces, layer["entry"])
    near = (layer["mixed"], gains)
    body = partial(mlp_up_body, layer_at, top)
    found = run(body, away, near, outputs, away_out, scratch, flops, "mlp_up", needs)
    layer.update(zip(results, found))
    return found[-1]


def backward(down_pieces, up_pieces, kept, cotangent, marks, gains, slot_total):
    layers = len(kept)
    tokens, width = cotangent.shape
    units = kept[0]["slope"].shape[1]
    away = [*down_pieces, *up_pieces]
    for layer_at, layer in enumerate(kept):
        away += [layer[name] for name in (STATE + WEIGHTS if layer_at < layers - 1 else TOP)]
    away.append(kept[-1]["active"])
    near = (cotangent, marks["slot"], marks["seg"], gains)
    outputs = (
        shape((tokens, width), f32),
        shape((layers, slot_total, width), f32),
        shape((tokens, width), bf16),
    )
    held = [kept[0][name] for name in STATE + WEIGHTS]
    scratch = [pltpu.VMEM(a.shape, a.dtype) for a in held]
    scratch += [
        pltpu.VMEM((tokens, width), bf16),
        pltpu.VMEM((tokens, units), bf16),
        pltpu.VMEM((tokens, width), f32),
        pltpu.VMEM((tokens, width), bf16),
        pltpu.VMEM((tokens, 3 * width), bf16),
        pltpu.VMEM((tokens, tokens), f32),
        pltpu.SemaphoreType.DMA((len(held) + 1,)),
        piece_sems(down_pieces),
        piece_sems(up_pieces),
        piece_sems(up_pieces),
    ]
    flops = 2 * layers * tokens * width * (4 * width + 3 * units + 5 * tokens)
    body = partial(backward_body, layers, (len(down_pieces), len(up_pieces)))
    found = run(body, away, near, outputs, (), scratch, flops, "backward", vmem=BACKWARD_VMEM)
    return found[:3]


def axis_sizes():
    return tuple(lax.axis_size(axis) for axis in ALL)


def is_block():
    return axis_sizes() == (4, 2, 2, 2)


def flip(value, axis):
    return lax.ppermute(value, axis, [(0, 1), (1, 0)])


def move_all(value, to):
    sizes = axis_sizes()
    moves = []
    for at in np.ndindex(*sizes):
        moves.append(tuple(int(np.ravel_multi_index(place, sizes)) for place in (at, to(*at))))
    return lax.ppermute(value, ALL, moves)


def turn(value, core_of_x):
    return move_all(
        value,
        lambda z, x, core, y: (z, 1 - x, core, y) if core == core_of_x else (z, x, core, 1 - y),
    )


def near_xy(value, dx, dy):
    return move_all(value, lambda z, x, core, y: (z, x ^ dx, core, y ^ dy))


def swap_z(value, distance):
    return lax.ppermute(value, "z", [(i, i ^ distance) for i in range(lax.axis_size("z"))])


class Steps:
    def __init__(self):
        self.zero = None

    def needs(self):
        return [] if self.zero is None else [self.zero]

    def behind(self, value):
        return value if self.zero is None else value + self.zero[0, 0].astype(value.dtype)

    def join(self, parts):
        return self.behind(jnp.stack(parts))

    def wait(self, arrays):
        self.zero = zero_after([*arrays, *self.needs()])


class Gather:
    def __init__(self, steps, shard):
        self.steps, self.own = steps, shard

    def start_ring(self):
        own = self.steps.behind(self.own)
        self.parts = [own] + [swap_z(own, i) for i in (1, 2, 3)]
        return self.parts[1:]

    def first_turn(self):
        self.parts = [self.steps.join(self.parts)]
        self.parts.append(turn(self.parts[0], 0))
        return self.parts[1:]

    def second_turn(self):
        self.parts = [self.steps.join(self.parts)]
        self.parts.append(turn(self.parts[0], 1))
        return self.parts[1:]

    def last_turn(self):
        whole = self.steps.join(self.parts)
        self.pieces = [whole, flip(whole, "core")]
        return []


class LateGather(Gather):
    def late_first(self):
        self.parts = [self.steps.behind(self.own)]
        self.parts.append(turn(self.parts[0], 0))
        return self.parts[1:]

    def late_ring(self, distances):
        if len(self.parts) == 2:
            self.parts = [self.steps.join(self.parts)]
        own = self.parts[0]
        self.parts += [swap_z(own, i) for i in distances]
        return self.parts[-len(distances) :]


def total_over(value):
    if not is_block():
        return lax.psum(value, ALL)
    core = lax.axis_index("core")
    low = value.astype(bf16)
    mine = jnp.where(core == 0, value[0], value[1])
    theirs = jnp.where(core == 0, low[1], low[0])
    total = mine + flip(theirs, "core").astype(f32)
    low = total.astype(bf16)
    total = total + sum(near_xy(low, *to).astype(f32) for to in ((1, 0), (0, 1), (1, 1)))
    low = total.astype(bf16)
    total = total + sum(swap_z(low, distance).astype(f32) for distance in (1, 2, 3))
    other = flip(total.astype(bf16), "core").astype(f32)
    return jnp.stack([jnp.where(core == 0, total, other), jnp.where(core == 0, other, total)])


def window_rows(count, width):
    step = math.gcd(count, width)
    return -(-(width - step + count) // width)


def prompt_window(prompts, width):
    count = prompts.shape[0]
    assert window_rows(count, width) <= 4
    shift = lax.axis_index(ALL) * count % width
    flat = lax.dynamic_update_slice(jnp.zeros((4 * width,), f32), prompts, (shift,))
    rows = flat.reshape(4, width // LANES, LANES).transpose(1, 0, 2)
    return jnp.concatenate(halves(rows), axis=1).reshape(-1, LANES)


def window_slots(count, width, layers):
    holders = math.prod(axis_sizes()) // layers
    base = np.arange(holders, dtype=np.int32) * count // width
    both = base[:, None] + np.arange(8, dtype=np.int32)[None, :] % 4
    return jnp.asarray(both.reshape(1, -1), f32)


def gather_any(qkv, out, up, down):
    seq = ("z", "x", "core")
    layers = qkv.shape[0]
    qkvs = [lax.all_gather(qkv[layer_at], seq, tiled=True) for layer_at in range(layers)]
    groups = [[qkvs[0]]]
    for layer_at in range(layers):
        whole_up = lax.all_gather(up[layer_at], "y", axis=1, tiled=True)
        out_up = jnp.concatenate([out[layer_at], whole_up], axis=1)
        groups.append([lax.all_gather(out_up, seq, tiled=True)])
        whole_down = lax.all_gather(down[layer_at].T, "y", axis=1, tiled=True)
        groups.append([lax.all_gather(whole_down, seq, tiled=True)] + qkvs[layer_at + 1 :][:1])
    return groups


def block_groups(qkv_weight, out_weight, up_weight, down_weight, window):
    y_size, y_at = lax.axis_size("y"), lax.axis_index("y")
    layers, rows, qkv_width = qkv_weight.shape
    cut, out_cut = qkv_width // y_size, out_weight.shape[2] // y_size
    qkv = lax.dynamic_slice(qkv_weight, (0, 0, y_at * cut), (layers, rows, cut))
    out = lax.dynamic_slice(out_weight, (0, 0, y_at * out_cut), (layers, rows, out_cut))
    groups = [jnp.concatenate([qkv[0], window], axis=1)]
    for layer_at in range(layers):
        groups.append(jnp.concatenate([out[layer_at], up_weight[layer_at]], axis=1))
        down = down_weight[layer_at].T
        if layer_at < layers - 1:
            down = jnp.concatenate([down, qkv[layer_at + 1]], axis=1)
        groups.append(down)
    return groups


def per_device(
    patches,
    segments,
    prompt_slots,
    norm_gains,
    qkv_weight,
    out_weight,
    up_weight,
    down_weight,
    cotangent,
    prompts,
    first_moment,
    second_moment,
    adam_betas,
    learn_rate,
):
    layers, _, width = norm_gains.shape
    tokens = patches.shape[0]
    units = up_weight.shape[2] * lax.axis_size("y")
    total_prompts = prompts.shape[0] * math.prod(axis_sizes())
    slot_total = total_prompts // (layers * width)
    window = prompt_window(prompts, width)
    marks = {
        "base": window_slots(prompts.shape[0], width, layers),
        "slot": prompt_slots.reshape(1, tokens),
        "seg": segments.reshape(1, tokens),
    }
    kept = []
    pieces = []
    state = {"riders": None}

    def forward_step(at, needs=()):
        layer_at, part = divmod(at, 2)
        if part == 1:
            top = layer_at == layers - 1
            return mlp_up(pieces[at], layer_at, kept[layer_at], norm_gains, units, top, needs)
        layer, state["riders"], zero = attn_forward(
            pieces[at],
            layer_at,
            slot_total,
            patches if layer_at == 0 else None,
            kept[layer_at - 1] if layer_at > 0 else None,
            state["riders"],
            marks,
            norm_gains,
            needs,
        )
        kept.append(layer)
        return zero

    block = is_block()
    if block:
        steps = Steps()
        groups = block_groups(qkv_weight, out_weight, up_weight, down_weight, window)
        *early, final = groups
        gathers = [Gather(steps, shard) for shard in early] + [LateGather(steps, final)]

        def kernel(at):
            pieces.append(gathers[at].pieces)
            steps.zero = forward_step(at, steps.needs())

        ring, first, second, last = (
            Gather.start_ring,
            Gather.first_turn,
            Gather.second_turn,
            Gather.last_turn,
        )
        late_first = LateGather.late_first
        late_ring = LateGather.late_ring
        for moves, beside in (
            ([(ring, 0)], None),
            ([(first, 0), (late_first, 4)], None),
            ([(second, 0), (second, 4), (ring, 1)], None),
            ([(last, 0), (first, 1), (ring, 2)], 0),
            ([(second, 1), (first, 2), (ring, 3)], None),
            ([(last, 1), (second, 2), (first, 3), (partial(late_ring, distances=(1, 2)), 4)], 1),
            ([(last, 2), (second, 3), (partial(late_ring, distances=(3,)), 4)], 2),
            ([(last, 3), (last, 4)], 3),
        ):
            coming = [array for move, at in moves for array in move(gathers[at])]
            if beside is not None:
                kernel(beside)
            if coming:
                steps.wait(coming)
        pieces.append(gathers[4].pieces)
    else:
        state["riders"] = lax.all_gather(window, ALL)
        pieces = gather_any(qkv_weight, out_weight, up_weight, down_weight)
        for at in range(2 * layers):
            forward_step(at)

    gradient, layer_grads, block_output = backward(
        pieces[-1], pieces[-2], kept, cotangent, marks, norm_gains, slot_total
    )

    prompt_grad = total_over(layer_grads)
    grad_norm = jnp.sqrt(jnp.sum(prompt_grad * prompt_grad))
    clip_limit = clip_ratio * math.sqrt(total_prompts)
    own_grads = lax.dynamic_slice(
        prompt_grad.reshape(-1), (lax.axis_index(ALL) * prompts.shape[0],), prompts.shape
    )
    clipped = own_grads * jnp.minimum(1.0, clip_limit / (grad_norm + 1e-06))
    beta_one = adam_betas[0]
    beta_two = adam_betas[1]
    step_value = float(ADAM_STEP)
    new_first = beta_one * first_moment + (1.0 - beta_one) * clipped
    new_second = beta_two * second_moment + (1.0 - beta_two) * clipped * clipped
    first_hat = new_first / (1.0 - beta_one**step_value)
    second_hat = new_second / (1.0 - beta_two**step_value)
    new_prompts = prompts - learn_rate[0] * (
        first_hat / (jnp.sqrt(second_hat) + adam_eps) + decay_rate * prompts
    )
    return (block_output, gradient, new_prompts, new_first, new_second, grad_norm.reshape(1))


def solution(mesh):
    seq_size, mlp_size = mesh.shape["seq"], mesh.shape["mlp"]
    grid = Mesh(mesh.devices.reshape(seq_size // 4, 2, 2, mlp_size), ALL)
    seq, mlp = ("z", "x", "core"), "y"
    in_specs = (
        P(ALL, None),
        P(ALL),
        P(ALL),
        P(),
        P(None, seq, None),
        P(None, seq, None),
        P(None, seq, mlp),
        P(None, mlp, seq),
        P(ALL, None),
        P(ALL),
        P(ALL),
        P(ALL),
        P(),
        P(),
    )
    out_specs = (P(ALL, None), P(ALL, None), P(ALL), P(ALL), P(ALL), P())
    return jax.shard_map(
        per_device, mesh=grid, in_specs=in_specs, out_specs=out_specs, check_vma=False
    )
```

```python
import math
from functools import partial

import jax
import jax.numpy as jnp
import numpy as np
from jax import lax
from jax.experimental import pallas as pl
from jax.experimental.pallas import tpu as pltpu
from jax.sharding import Mesh
from jax.sharding import PartitionSpec as P

HEADS = 12
HEAD_DIM = 64
ADAM_STEP = 2

ln_eps = 1e-06
masked_score = -1e30
clip_ratio = 0.05
adam_eps = 1e-08
decay_rate = 0.1
ALL = ("z", "x", "core", "y")
f32 = jnp.float32
bf16 = jnp.bfloat16
LANES = 128
TILE = 256
FORWARD_VMEM = 30 * 2**20
BACKWARD_VMEM = 45 * 2**20

TAIL_SLOPE = 0.275
TAIL_POLY = (
    0.10971068582446765,
    0.1096543595961662,
    0.10219045697718625,
    0.07893593678575173,
    0.08800740710695068,
    -0.03516190352887128,
    0.13017028940734943,
    -0.11067510560848658,
    0.027167870070925505,
)


def mm(a, b):
    return jnp.dot(a, b, preferred_element_type=f32)


def mm_t(a, b):
    return lax.dot_general(a, b, (((1,), (1,)), ((), ())), preferred_element_type=f32)


def gelu_parts(v):
    a = jnp.abs(v)
    bell = jnp.exp2(v * v * (-0.5 * math.log2(math.e)))
    t = 1.0 / (1.0 + TAIL_SLOPE * a)
    poly = jnp.full_like(v, TAIL_POLY[-1])
    for factor in TAIL_POLY[-2::-1]:
        poly = poly * t + factor
    tail = poly * t * bell
    return jnp.where(v >= 0.0, 1.0 - tail, tail), bell * (1.0 / math.sqrt(2.0 * math.pi))


def norm_stats(values):
    center = values - jnp.mean(values, axis=-1, keepdims=True)
    rstd = lax.rsqrt(jnp.mean(center * center, axis=-1, keepdims=True) + ln_eps)
    return center * rstd, rstd


def norm_back(grad, values, gain_row):
    unit, rstd = norm_stats(values)
    grad = grad * gain_row
    mean_grad = jnp.mean(grad, axis=-1, keepdims=True)
    mean_dot = jnp.mean(grad * unit, axis=-1, keepdims=True)
    return rstd * (grad - mean_grad - unit * mean_dot)


class Copies:
    def __init__(self, pairs, sems):
        self.copies = [
            pltpu.make_async_copy(source, target, sems.at[i])
            for i, (source, target) in enumerate(pairs)
        ]

    def start(self):
        for copy in self.copies:
            copy.start()
        return self

    def wait(self):
        for copy in self.copies:
            copy.wait()


def shards(refs, late):
    z, x, core, y = (lax.axis_index(axis) for axis in ALL)
    found = []
    for i, ref in enumerate(refs):
        c = core ^ i
        for step in range(4):
            to_x, to_y = ((x, y), (x ^ 1 ^ c, y ^ c), (x ^ c, y ^ 1 ^ c), (x ^ 1, y ^ 1))[step]
            for back in range(4):
                at = (step // 2, step % 2)
                at = (back, *at) if late else (*at, back)
                found.append((ref.at[at], (z ^ back, to_x, c, to_y)))
    return found


def weight_copies(refs, column, width, dest, sems, late=False, first=0):
    if refs[0].ndim == 2:
        y_size = dest.shape[-1] // width
        columns = pl.ds(column * y_size, dest.shape[-1])
        return Copies([(refs[0].at[:, columns], dest)], sems)
    rows = refs[0].shape[-2]
    pairs = []
    for ref, (z, x, core, y) in shards(refs, late):
        to_rows = pl.ds(pl.multiple_of((x * 2 + core) * rows, 16), rows)
        to_columns = pl.ds(pl.multiple_of(y * (dest.shape[-1] // 2) + first, LANES), width)
        pairs.append((ref.at[:, pl.ds(column, width)], dest.at[z, to_rows, to_columns]))
    return Copies(pairs, sems)


def rider_copies(refs, column, dest, sems):
    pairs = []
    for ref, (z, x, core, y) in shards(refs, False):
        source = ref.at[:, pl.ds(column, LANES)]
        pairs.append((source, dest.at[((z * 2 + x) * 2 + core) * 2 + y]))
    return Copies(pairs, sems)


def rows_view(ref, columns=None):
    value = ref[...] if columns is None else ref[..., columns]
    return value.reshape(-1, value.shape[-1])


def head_of(pair, head):
    lane = lax.broadcasted_iota(jnp.int32, pair.shape, 1)
    keep = (lane < HEAD_DIM) if head == 0 else (lane >= HEAD_DIM)
    return jnp.where(keep, pair, jnp.zeros_like(pair))


def as_column(row):
    return jnp.broadcast_to(row.astype(f32), (8, row.shape[1])).T[:, :1]


def fill_bias(bias_ref, seg_ref):
    seg = seg_ref[...]
    bias_ref[...] = jnp.where(as_column(seg) == seg.astype(f32), 0.0, masked_score)


def copy_out(source, target, sem):
    copy = pltpu.make_async_copy(source, target, sem)
    copy.start()
    return copy


def attention(qkv_ref, bias_ref, mixed_ref, lse_ref):
    tokens, width = mixed_ref.shape
    pairs = width // LANES
    lane = lax.broadcasted_iota(jnp.int32, (tokens, LANES), 1)
    low = lane < HEAD_DIM
    lse = jnp.zeros((tokens, LANES), f32)
    for at in range(pairs):
        query, key, value = (
            qkv_ref[:, i * width + at * LANES : i * width + (at + 1) * LANES] for i in range(3)
        )
        ones = jnp.ones_like(value)
        values = (jnp.where(low, value, ones), jnp.where(low, ones, value))
        parts, tops = [], []
        for head in range(2):
            scores = mm_t(head_of(query, head), key) + bias_ref[...]
            top = jnp.max(scores, axis=1, keepdims=True)
            parts.append(mm(jnp.exp(scores - top).astype(bf16), values[head]))
            tops.append(top)
        total = pltpu.roll(jnp.where(low, parts[1], parts[0]), HEAD_DIM, 1)
        mixed = jnp.where(low, parts[0], parts[1]) / total
        mixed_ref[:, at * LANES : (at + 1) * LANES] = mixed.astype(bf16)
        pair_lse = jnp.where(low, tops[0], tops[1]) + jnp.log(total)
        lse = jnp.where((lane & (HEAD_DIM - 1)) == at, pair_lse, lse)
    lse_ref[...] = lse.T


def attention_back(qkv_ref, mixed_ref, lse_ref, bias_ref, dqkv_ref):
    tokens, width = mixed_ref.shape
    pairs = width // LANES
    for at in range(pairs):
        places = [slice(i * width + at * LANES, i * width + (at + 1) * LANES) for i in range(3)]
        query, key, value = (qkv_ref[:, place] for place in places)
        grad = mixed_ref[:, at * LANES : (at + 1) * LANES]
        found = [None, None, None]
        for head in range(2):
            query_head, key_head, grad_head = (head_of(v, head) for v in (query, key, grad))
            row = head * HEAD_DIM + at
            scores = mm_t(key, query_head) + bias_ref[...]
            probs = jnp.exp(scores - lse_ref[row : row + 1, :])
            grad_probs = mm_t(value, grad_head)
            inner = jnp.sum(probs * grad_probs, axis=0, keepdims=True)
            d_scores = (probs * (grad_probs - inner)).astype(bf16)
            for i, part in enumerate(
                (
                    mm(d_scores.T, key_head),
                    mm(d_scores, query_head),
                    mm(probs.astype(bf16), grad_head),
                )
            ):
                found[i] = part if head == 0 else found[i] + part
        found[0] = found[0] * HEAD_DIM**-0.5
        for place, part in zip(places, found):
            dqkv_ref[:, place] = part.astype(bf16)


def attn_forward_body(plan, *refs):
    count, layer_at, slot_total, takes_riders, has_down = plan
    pieces, refs = refs[:count], refs[count:]
    if has_down:
        (middle_in, active_in), refs = refs[:2], refs[2:]
    else:
        x_ref, refs = refs[0], refs[1:]
    slot_ref, base_ref, seg_ref, gain_ref = refs[:4]
    refs = refs[4:]
    if not takes_riders:
        rider_ref, refs = refs[0], refs[1:]
    mixed_ref, lse_ref, entry_out, qkv_out, weight_out = refs[:5]
    refs = refs[5:]
    if takes_riders:
        (rider_out, rider_ref), refs = (refs[0], refs[1]), refs[2:]
    if has_down:
        (down_out, w_down, middle_ref, active_ref, sem_down), refs = refs[:5], refs[5:]
    w_qkv, norm_ref, bias_ref, entry_ref, qkv_ref, sem_a, sem_b, sem_c = refs
    tokens, width = mixed_ref.shape
    parts = 1 if pieces[0].ndim == 2 else 2
    cut = 3 * width // parts
    qkv_pieces, column = pieces, 0
    copies = []
    if has_down:
        units = active_ref.shape[1]
        load_middle = copy_out(middle_in, middle_ref, sem_c.at[3])
        load_active = copy_out(active_in, active_ref, sem_c.at[4])
        down_pieces = pieces
        if parts == 1:
            down_pieces, qkv_pieces = pieces[:1], pieces[1:]
        else:
            column = units // parts
        load_down = weight_copies(down_pieces, 0, units // parts, w_down, sem_down).start()
    if takes_riders:
        load_riders = rider_copies(pieces, cut, rider_ref, sem_b).start()
    load_qkv = weight_copies(qkv_pieces, column, cut, w_qkv, sem_a)
    if not has_down:
        load_qkv.start()
    fill_bias(bias_ref, seg_ref)
    slots = as_column(slot_ref[...])
    onehot = (slots == base_ref[...]).astype(bf16)
    is_prompt = slots < slot_total
    if takes_riders:
        load_riders.wait()
        copies.append(copy_out(rider_ref, rider_out, sem_c.at[3]))
    holders = base_ref.shape[1] // 8
    windows = rider_ref[layer_at * holders : (layer_at + 1) * holders].astype(f32)
    if has_down:
        load_middle.wait()
        load_active.wait()
        load_down.wait()
        load_qkv.start()
        entry_ref[...] = middle_ref[...] + mm_t(active_ref[...], rows_view(w_down))
        x_ref = entry_ref
    for at in range(width // LANES):
        lanes = slice(at * LANES, (at + 1) * LANES)
        part = windows[:, at * 8 : (at + 1) * 8, :].reshape(-1, LANES)
        inject = mm(onehot, part.astype(bf16))
        entry_ref[:, lanes] = jnp.where(is_prompt, inject, x_ref[:, lanes].astype(f32))
    norm_ref[...] = (norm_stats(entry_ref[...])[0] * gain_ref[layer_at, :1]).astype(bf16)
    load_qkv.wait()
    copies.append(copy_out(entry_ref, entry_out, sem_c.at[0]))
    if has_down:
        copies.append(copy_out(w_down, down_out, sem_c.at[3]))
    copies.append(copy_out(w_qkv, weight_out, sem_c.at[1]))
    for at in range(3 * width // TILE):
        columns = slice(at * TILE, (at + 1) * TILE)
        out = mm(norm_ref[...], rows_view(w_qkv, columns))
        if at < width // TILE:
            out = out.astype(bf16).astype(f32) * HEAD_DIM**-0.5
        qkv_ref[:, columns] = out.astype(bf16)
    copies.append(copy_out(qkv_ref, qkv_out, sem_c.at[2]))
    attention(qkv_ref, bias_ref, mixed_ref, lse_ref)
    for copy in copies:
        copy.wait()


def mlp_up_body(layer_at, top, *refs):
    count = 1 if refs[0].ndim == 2 else 2
    pieces, refs = refs[:count], refs[count:]
    entry_in, mixed_ref, gain_ref = refs[:3]
    refs = refs[3:]
    if top:
        (middle_ref, slope_ref, active_ref), refs = refs[:3], refs[3:]
        w_out, w_up, norm_ref, sem_a, sem_b, sem_d = refs
    else:
        middle_out, slope_out, out_out, up_out, active_out = refs[:5]
        w_out, w_up, norm_ref, sem_a, sem_b, sem_d, middle_ref, slope_ref, active_ref = refs[5:]
    units = slope_ref.shape[1]
    width = middle_ref.shape[1]
    load_entry = copy_out(entry_in, middle_ref, sem_d.at[0])
    load_out = weight_copies(pieces, 0, width // count, w_out, sem_a).start()
    load_up = weight_copies(pieces, width // count, units // count, w_up, sem_b).start()
    load_entry.wait()
    load_out.wait()
    middle_ref[...] = middle_ref[...] + mm(mixed_ref[...], rows_view(w_out))
    copies = []
    if not top:
        copies.append(copy_out(middle_ref, middle_out, sem_d.at[0]))
        copies.append(copy_out(w_out, out_out, sem_d.at[1]))
    norm_ref[...] = (norm_stats(middle_ref[...])[0] * gain_ref[layer_at, 1:]).astype(bf16)
    load_up.wait()
    if not top:
        copies.append(copy_out(w_up, up_out, sem_d.at[2]))
    for at in range(units // TILE):
        columns = slice(at * TILE, (at + 1) * TILE)
        before = mm(norm_ref[...], rows_view(w_up, columns))
        phi_sum, phi = gelu_parts(before)
        active_ref[:, columns] = (before * phi_sum).astype(bf16)
        slope_ref[:, columns] = (phi_sum + before * phi).astype(bf16)
    if not top:
        copies.append(copy_out(slope_ref, slope_out, sem_d.at[3]))
        copies.append(copy_out(active_ref, active_out, sem_d.at[4]))
    for copy in copies:
        copy.wait()


def top_down_copies(down_pieces, up_pieces, dest, sem_down, sem_rest, width):
    units = dest.shape[-1]
    if down_pieces[0].ndim == 2:
        return weight_copies(down_pieces, 0, units, dest, sem_down).copies
    here = down_pieces[0].shape[-1]
    rest = units // 2 - here
    column = (width + units) // 2
    copies = weight_copies(down_pieces, 0, here, dest, sem_down, late=True).copies
    return copies + weight_copies(up_pieces, column, rest, dest, sem_rest, first=here).copies


STATE = ("slope", "middle", "qkv", "lse", "entry")
WEIGHTS = ("down", "up", "out", "qkv_weight")
TOP = (*STATE, "qkv_weight")


def backward_body(layers, counts, *refs):
    down_pieces, refs = refs[: counts[0]], refs[counts[0] :]
    up_pieces, refs = refs[: counts[1]], refs[counts[1] :]
    sources = []
    for layer_at in range(layers):
        names = STATE + WEIGHTS if layer_at < layers - 1 else TOP
        sources.append(dict(zip(names, refs)))
        refs = refs[len(names) :]
    active_in, cotangent_ref, slot_ref, seg_ref, gain_ref = refs[:5]
    (out_ref, prompt_ref, block_ref), refs = refs[5:8], refs[8:]
    held = dict(zip(STATE + WEIGHTS, refs))
    refs = refs[len(held) :]
    active_ref, low_ref, before_ref, grad_ref, mixed_ref, dqkv_ref, bias_ref = refs[:7]
    sem, sem_down, sem_rest, sem_up, sem_out = refs[7:]
    order = list(held)
    tokens, width = grad_ref.shape
    units = before_ref.shape[1]
    parts = 1 if down_pieces[0].ndim == 2 else 2
    top_weights = {
        "up": (up_pieces, width // parts, units // parts, sem_up),
        "out": (up_pieces, 0, width // parts, sem_out),
    }

    class Fetch:
        def __init__(self, name, layer_at):
            if layer_at == layers - 1 and name == "down":
                self.copies = top_down_copies(
                    down_pieces, up_pieces, held[name], sem_down, sem_rest, width
                )
            elif layer_at == layers - 1 and name in top_weights:
                refs, column, count, sems = top_weights[name]
                self.copies = weight_copies(refs, column, count, held[name], sems).copies
            else:
                source, at = sources[layer_at][name], order.index(name)
                self.copies = [pltpu.make_async_copy(source, held[name], sem.at[at])]
            for copy in self.copies:
                copy.start()

        def wait(self):
            for copy in self.copies:
                copy.wait()

    coming = {}

    def fetch(layer_at, *names):
        for name in names if layer_at >= 0 else ():
            coming[name] = Fetch(name, layer_at)

    def arrived(*names):
        for name in names:
            if name in coming:
                coming.pop(name).wait()

    fetch(layers - 1, "down", "slope")
    fill_bias(bias_ref, seg_ref)
    low_ref[...] = cotangent_ref[...]
    slot_total = prompt_ref.shape[1]
    is_prompt = as_column(slot_ref[...]) < slot_total
    onehot_t = (
        slot_ref[...] == lax.broadcasted_iota(jnp.int32, (slot_total, tokens), 0)
    ).astype(bf16)

    for layer_at in reversed(range(layers)):
        top = layer_at == layers - 1

        below = layer_at - 1
        arrived("down", "slope")
        fetch(layer_at, *(("up", "middle") if top else ("up",)))
        for at in range(units // TILE):
            columns = slice(at * TILE, (at + 1) * TILE)
            grad_active = mm(low_ref[...], rows_view(held["down"], columns))
            slope = held["slope"][:, columns].astype(f32)
            before_ref[:, columns] = (grad_active * slope).astype(bf16)
        arrived("up", "middle")
        if top:
            load_active = copy_out(active_in, active_ref, sem.at[len(order)])
        fetch(layer_at, "out", "qkv", "lse")
        grad_norm = mm_t(before_ref[...], rows_view(held["up"]))
        back = norm_back(grad_norm, held["middle"][...], gain_ref[layer_at, 1:])
        grad = cotangent_ref[...].astype(f32) if top else grad_ref[...]
        grad_middle = grad + back
        grad_ref[...] = grad_middle
        low_ref[...] = grad_middle.astype(bf16)
        arrived("out", "qkv", "lse")
        mixed_ref[...] = mm_t(low_ref[...], rows_view(held["out"])).astype(bf16)
        if top:
            load_active.wait()
            branch = mm_t(active_ref[...], rows_view(held["down"]))
            block_ref[...] = (held["middle"][...] + branch).astype(bf16)
        fetch(layer_at, "qkv_weight", "entry")
        fetch(below, "down", "slope", "middle")
        attention_back(held["qkv"], mixed_ref, held["lse"], bias_ref, dqkv_ref)
        arrived("qkv_weight", "entry")
        grad_norm = mm_t(dqkv_ref[...], rows_view(held["qkv_weight"]))
        back = norm_back(grad_norm, held["entry"][...], gain_ref[layer_at, :1])
        grad_entry = grad_ref[...] + back
        high, low = halves(grad_entry)
        prompt_ref[layer_at] = mm(onehot_t, high) + mm(onehot_t, low)
        passed = jnp.where(is_prompt, 0.0, grad_entry)
        if layer_at > 0:
            grad_ref[...] = passed
            low_ref[...] = passed.astype(bf16)
        else:
            out_ref[...] = passed


def halves(values):
    high = values.astype(bf16)
    return high, (values - high.astype(f32)).astype(bf16)


def shape(dims, dtype):
    return jax.ShapeDtypeStruct(dims, dtype)


def skipping(body, taken, needed, results):
    def kernel(*refs):
        ends = taken + needed, taken + needed + results
        body(*refs[:taken], *refs[ends[0] : ends[1]], *refs[ends[1] + 1 :])
        refs[ends[1]][...] = jnp.zeros((1, 1), f32)

    return kernel


def run(body, away, near, outputs, outputs_away, scratch, flops, name, needs=(), vmem=FORWARD_VMEM):
    here = pl.BlockSpec(memory_space=pltpu.VMEM)
    hbm = pl.BlockSpec(memory_space=pltpu.HBM)
    anywhere = pl.BlockSpec(memory_space=pl.ANY)
    results = (*outputs, *outputs_away)
    moved = sum(math.prod(a.shape) * a.dtype.itemsize for a in (*away, *near, *results))
    return pl.pallas_call(
        skipping(body, len(away) + len(near), len(needs), len(results)),
        out_shape=(*results, shape((1, 1), f32)),
        in_specs=[anywhere] * len(away) + [here] * len(near) + [anywhere] * len(needs),
        out_specs=[here] * len(outputs) + [hbm] * len(outputs_away) + [here],
        scratch_shapes=scratch,
        compiler_params=pltpu.CompilerParams(vmem_limit_bytes=vmem),
        cost_estimate=pl.CostEstimate(flops=flops, transcendentals=0, bytes_accessed=moved),
        name=name,
    )(*away, *near, *needs)


def zero_body(*refs):
    refs[-1][...] = jnp.zeros((1, 1), f32)


def zero_after(values):
    return pl.pallas_call(
        zero_body,
        out_shape=shape((1, 1), f32),
        in_specs=[pl.BlockSpec(memory_space=pl.ANY)] * len(values),
        out_specs=pl.BlockSpec(memory_space=pltpu.VMEM),
        compiler_params=pltpu.CompilerParams(vmem_limit_bytes=2**20),
        cost_estimate=pl.CostEstimate(flops=0, transcendentals=0, bytes_accessed=4),
        name="zero_after",
    )(*values)


def piece_sems(pieces):
    count = 1 if pieces[0].ndim == 2 else 32
    return pltpu.SemaphoreType.DMA((count,))


def weight_shape(pieces, width, columns):
    return (width, columns) if pieces[0].ndim == 2 else (4, width // 4, columns)


def attn_forward(pieces, layer_at, slot_total, x, below, riders, marks, gains, needs=()):
    tokens = marks["seg"].shape[1]
    width = gains.shape[2]
    takes_riders, has_down = riders is None, below is not None
    weight = weight_shape(pieces, width, 3 * width)
    near_out = (shape((tokens, width), bf16), shape((LANES, tokens), f32))
    away_out = (
        shape((tokens, width), f32),
        shape((tokens, 3 * width), bf16),
        shape(weight, bf16),
    )
    away = tuple(pieces)
    near = (marks["slot"], marks["base"], marks["seg"], gains)
    scratch = []
    if not takes_riders:
        near += (riders,)
    else:
        rider_shape = (math.prod(axis_sizes()), 8 * width // LANES, LANES)
        away_out += (shape(rider_shape, bf16),)
        scratch.append(pltpu.VMEM(rider_shape, bf16))
    if has_down:
        units = below["active"].shape[1]
        away += (below["middle"], below["active"])
        down = weight_shape(pieces, width, units)
        away_out += (shape(down, bf16),)
        scratch += [
            pltpu.VMEM(down, bf16),
            pltpu.VMEM((tokens, width), f32),
            pltpu.VMEM((tokens, units), bf16),
            piece_sems(pieces),
        ]
    else:
        near = (x, *near)
    scratch += [
        pltpu.VMEM(weight, bf16),
        pltpu.VMEM((tokens, width), bf16),
        pltpu.VMEM((tokens, tokens), f32),
        pltpu.VMEM((tokens, width), f32),
        pltpu.VMEM((tokens, 3 * width), bf16),
        piece_sems(pieces),
        piece_sems(pieces),
        pltpu.SemaphoreType.DMA((5,)),
    ]
    flops = 2 * tokens * width * (7 * width + 2 * tokens)
    body = partial(attn_forward_body, (len(pieces), layer_at, slot_total, takes_riders, has_down))
    found = run(body, away, near, near_out, away_out, scratch, flops, "attn_forward", needs)
    names = ("mixed", "lse", "entry", "qkv", "qkv_weight")
    layer = dict(zip(names, found))
    found = found[5:]
    if takes_riders:
        riders, found = found[0], found[1:]
    if has_down:
        below["down"], found = found[0], found[1:]
    return layer, riders, found[0]


def mlp_up(pieces, layer_at, layer, gains, units, top, needs=()):
    tokens, width = layer["mixed"].shape
    out_shape, up_shape = (weight_shape(pieces, width, n) for n in (width, units))
    state = {
        "middle": shape((tokens, width), f32),
        "slope": shape((tokens, units), bf16),
        "active": shape((tokens, units), bf16),
    }
    scratch = [
        pltpu.VMEM(out_shape, bf16),
        pltpu.VMEM(up_shape, bf16),
        pltpu.VMEM((tokens, width), bf16),
        piece_sems(pieces),
        piece_sems(pieces),
        pltpu.SemaphoreType.DMA((5,)),
    ]
    if top:
        results, outputs, away_out = state, tuple(state.values()), ()
    else:
        weights = {"out": shape(out_shape, bf16), "up": shape(up_shape, bf16)}
        names = ("middle", "slope", "out", "up", "active")
        results = {name: {**state, **weights}[name] for name in names}
        outputs, away_out = (), tuple(results.values())
        scratch += [pltpu.VMEM(a.shape, a.dtype) for a in state.values()]
    flops = 2 * tokens * width * (units + width)
    away = (*pieces, layer["entry"])
    near = (layer["mixed"], gains)
    body = partial(mlp_up_body, layer_at, top)
    found = run(body, away, near, outputs, away_out, scratch, flops, "mlp_up", needs)
    layer.update(zip(results, found))
    return found[-1]


def backward(down_pieces, up_pieces, kept, cotangent, marks, gains, slot_total):
    layers = len(kept)
    tokens, width = cotangent.shape
    units = kept[0]["slope"].shape[1]
    away = [*down_pieces, *up_pieces]
    for layer_at, layer in enumerate(kept):
        away += [layer[name] for name in (STATE + WEIGHTS if layer_at < layers - 1 else TOP)]
    away.append(kept[-1]["active"])
    near = (cotangent, marks["slot"], marks["seg"], gains)
    outputs = (
        shape((tokens, width), f32),
        shape((layers, slot_total, width), f32),
        shape((tokens, width), bf16),
    )
    held = [kept[0][name] for name in STATE + WEIGHTS]
    scratch = [pltpu.VMEM(a.shape, a.dtype) for a in held]
    scratch += [
        pltpu.VMEM((tokens, units), bf16),
        pltpu.VMEM((tokens, width), bf16),
        pltpu.VMEM((tokens, units), bf16),
        pltpu.VMEM((tokens, width), f32),
        pltpu.VMEM((tokens, width), bf16),
        pltpu.VMEM((tokens, 3 * width), bf16),
        pltpu.VMEM((tokens, tokens), f32),
        pltpu.SemaphoreType.DMA((len(held) + 1,)),
        piece_sems(down_pieces),
        piece_sems(up_pieces),
        piece_sems(up_pieces),
        piece_sems(up_pieces),
    ]
    flops = 2 * layers * tokens * width * (4 * width + 3 * units + 5 * tokens)
    body = partial(backward_body, layers, (len(down_pieces), len(up_pieces)))
    found = run(body, away, near, outputs, (), scratch, flops, "backward", vmem=BACKWARD_VMEM)
    return found[:3]


def axis_sizes():
    return tuple(lax.axis_size(axis) for axis in ALL)


def is_block():
    return axis_sizes() == (4, 2, 2, 2)


def flip(value, axis):
    return lax.ppermute(value, axis, [(0, 1), (1, 0)])


def move_all(value, to):
    sizes = axis_sizes()
    moves = []
    for at in np.ndindex(*sizes):
        moves.append(tuple(int(np.ravel_multi_index(place, sizes)) for place in (at, to(*at))))
    return lax.ppermute(value, ALL, moves)


def turn(value, core_of_x):
    return move_all(
        value,
        lambda z, x, core, y: (z, 1 - x, core, y) if core == core_of_x else (z, x, core, 1 - y),
    )


def near_xy(value, dx, dy):
    return move_all(value, lambda z, x, core, y: (z, x ^ dx, core, y ^ dy))


def swap_z(value, distance):
    return lax.ppermute(value, "z", [(i, i ^ distance) for i in range(lax.axis_size("z"))])


class Steps:
    def __init__(self):
        self.zero = None

    def needs(self):
        return [] if self.zero is None else [self.zero]

    def behind(self, value):
        return value if self.zero is None else value + self.zero[0, 0].astype(value.dtype)

    def join(self, parts):
        return self.behind(jnp.stack(parts))

    def wait(self, arrays):
        self.zero = zero_after([*arrays, *self.needs()])


class Gather:
    def __init__(self, steps, shard):
        self.steps, self.own = steps, shard

    def start_ring(self):
        own = self.steps.behind(self.own)
        self.parts = [own] + [swap_z(own, i) for i in (1, 2, 3)]
        return self.parts[1:]

    def first_turn(self):
        self.parts = [self.steps.join(self.parts)]
        self.parts.append(turn(self.parts[0], 0))
        return self.parts[1:]

    def second_turn(self):
        self.parts = [self.steps.join(self.parts)]
        self.parts.append(turn(self.parts[0], 1))
        return self.parts[1:]

    def last_turn(self):
        whole = self.steps.join(self.parts)
        self.pieces = [whole, flip(whole, "core")]
        return []


class LateGather(Gather):
    def late_first(self):
        self.parts = [self.steps.behind(self.own)]
        self.parts.append(turn(self.parts[0], 0))
        return self.parts[1:]

    def late_ring(self, distances):
        if len(self.parts) == 2:
            self.parts = [self.steps.join(self.parts)]
        own = self.parts[0]
        self.parts += [swap_z(own, i) for i in distances]
        return self.parts[-len(distances) :]


def total_over(value):
    if not is_block():
        return lax.psum(value, ALL)
    core = lax.axis_index("core")
    low = value.astype(bf16)
    mine = jnp.where(core == 0, value[0], value[1])
    theirs = jnp.where(core == 0, low[1], low[0])
    total = mine + flip(theirs, "core").astype(f32)
    low = total.astype(bf16)
    total = total + sum(near_xy(low, *to).astype(f32) for to in ((1, 0), (0, 1), (1, 1)))
    low = total.astype(bf16)
    total = total + sum(swap_z(low, distance).astype(f32) for distance in (1, 2, 3))
    other = flip(total.astype(bf16), "core").astype(f32)
    return jnp.stack([jnp.where(core == 0, total, other), jnp.where(core == 0, other, total)])


def window_rows(count, width):
    step = math.gcd(count, width)
    return -(-(width - step + count) // width)


def prompt_window(prompts, width):
    count = prompts.shape[0]
    assert window_rows(count, width) <= 4
    shift = lax.axis_index(ALL) * count % width
    flat = lax.dynamic_update_slice(jnp.zeros((4 * width,), f32), prompts, (shift,))
    rows = flat.reshape(4, width // LANES, LANES).transpose(1, 0, 2)
    return jnp.concatenate(halves(rows), axis=1).reshape(-1, LANES)


def window_slots(count, width, layers):
    holders = math.prod(axis_sizes()) // layers
    base = np.arange(holders, dtype=np.int32) * count // width
    both = base[:, None] + np.arange(8, dtype=np.int32)[None, :] % 4
    return jnp.asarray(both.reshape(1, -1), f32)


def gather_any(qkv, out, up, down):
    seq = ("z", "x", "core")
    layers = qkv.shape[0]
    qkvs = [lax.all_gather(qkv[layer_at], seq, tiled=True) for layer_at in range(layers)]
    groups = [[qkvs[0]]]
    for layer_at in range(layers):
        whole_up = lax.all_gather(up[layer_at], "y", axis=1, tiled=True)
        out_up = jnp.concatenate([out[layer_at], whole_up], axis=1)
        groups.append([lax.all_gather(out_up, seq, tiled=True)])
        whole_down = lax.all_gather(down[layer_at].T, "y", axis=1, tiled=True)
        groups.append([lax.all_gather(whole_down, seq, tiled=True)] + qkvs[layer_at + 1 :][:1])
    return groups


def block_groups(qkv_weight, out_weight, up_weight, down_weight, window):
    y_size, y_at = lax.axis_size("y"), lax.axis_index("y")
    layers, rows, qkv_width = qkv_weight.shape
    cut, out_cut = qkv_width // y_size, out_weight.shape[2] // y_size
    qkv = lax.dynamic_slice(qkv_weight, (0, 0, y_at * cut), (layers, rows, cut))
    out = lax.dynamic_slice(out_weight, (0, 0, y_at * out_cut), (layers, rows, out_cut))
    groups = [jnp.concatenate([qkv[0], window], axis=1)]
    for layer_at in range(layers):
        out_up = [out[layer_at], up_weight[layer_at]]
        down = down_weight[layer_at].T
        if layer_at < layers - 1:
            down = jnp.concatenate([down, qkv[layer_at + 1]], axis=1)
        else:
            late = down.shape[1] * 3 // 4
            out_up.append(down[:, late:])
            down = down[:, :late]
        groups += [jnp.concatenate(out_up, axis=1), down]
    return groups


def per_device(
    patches,
    segments,
    prompt_slots,
    norm_gains,
    qkv_weight,
    out_weight,
    up_weight,
    down_weight,
    cotangent,
    prompts,
    first_moment,
    second_moment,
    adam_betas,
    learn_rate,
):
    layers, _, width = norm_gains.shape
    tokens = patches.shape[0]
    units = up_weight.shape[2] * lax.axis_size("y")
    total_prompts = prompts.shape[0] * math.prod(axis_sizes())
    slot_total = total_prompts // (layers * width)
    window = prompt_window(prompts, width)
    marks = {
        "base": window_slots(prompts.shape[0], width, layers),
        "slot": prompt_slots.reshape(1, tokens),
        "seg": segments.reshape(1, tokens),
    }
    kept = []
    pieces = []
    state = {"riders": None}

    def forward_step(at, needs=()):
        layer_at, part = divmod(at, 2)
        if part == 1:
            top = layer_at == layers - 1
            return mlp_up(pieces[at], layer_at, kept[layer_at], norm_gains, units, top, needs)
        layer, state["riders"], zero = attn_forward(
            pieces[at],
            layer_at,
            slot_total,
            patches if layer_at == 0 else None,
            kept[layer_at - 1] if layer_at > 0 else None,
            state["riders"],
            marks,
            norm_gains,
            needs,
        )
        kept.append(layer)
        return zero

    block = is_block()
    if block:
        steps = Steps()
        groups = block_groups(qkv_weight, out_weight, up_weight, down_weight, window)
        *early, final = groups
        gathers = [Gather(steps, shard) for shard in early] + [LateGather(steps, final)]

        def kernel(at):
            pieces.append(gathers[at].pieces)
            steps.zero = forward_step(at, steps.needs())

        ring, first, second, last = (
            Gather.start_ring,
            Gather.first_turn,
            Gather.second_turn,
            Gather.last_turn,
        )
        late_first = LateGather.late_first
        late_ring = LateGather.late_ring
        for moves, beside in (
            ([(ring, 0)], None),
            ([(first, 0), (late_first, 4)], None),
            ([(second, 0), (second, 4), (ring, 1)], None),
            ([(last, 0), (first, 1), (ring, 2)], 0),
            ([(second, 1), (first, 2), (ring, 3)], None),
            ([(last, 1), (second, 2), (first, 3), (partial(late_ring, distances=(1, 2)), 4)], 1),
            ([(last, 2), (second, 3), (partial(late_ring, distances=(3,)), 4)], 2),
            ([(last, 3), (last, 4)], 3),
        ):
            coming = [array for move, at in moves for array in move(gathers[at])]
            if beside is not None:
                kernel(beside)
            if coming:
                steps.wait(coming)
        pieces.append(gathers[4].pieces)
    else:
        state["riders"] = lax.all_gather(window, ALL)
        pieces = gather_any(qkv_weight, out_weight, up_weight, down_weight)
        for at in range(2 * layers):
            forward_step(at)

    gradient, layer_grads, block_output = backward(
        pieces[-1], pieces[-2], kept, cotangent, marks, norm_gains, slot_total
    )

    prompt_grad = total_over(layer_grads)
    grad_norm = jnp.sqrt(jnp.sum(prompt_grad * prompt_grad))
    clip_limit = clip_ratio * math.sqrt(total_prompts)
    own_grads = lax.dynamic_slice(
        prompt_grad.reshape(-1), (lax.axis_index(ALL) * prompts.shape[0],), prompts.shape
    )
    clipped = own_grads * jnp.minimum(1.0, clip_limit / (grad_norm + 1e-06))
    beta_one = adam_betas[0]
    beta_two = adam_betas[1]
    step_value = float(ADAM_STEP)
    new_first = beta_one * first_moment + (1.0 - beta_one) * clipped
    new_second = beta_two * second_moment + (1.0 - beta_two) * clipped * clipped
    first_hat = new_first / (1.0 - beta_one**step_value)
    second_hat = new_second / (1.0 - beta_two**step_value)
    new_prompts = prompts - learn_rate[0] * (
        first_hat / (jnp.sqrt(second_hat) + adam_eps) + decay_rate * prompts
    )
    return (block_output, gradient, new_prompts, new_first, new_second, grad_norm.reshape(1))


def solution(mesh):
    seq_size, mlp_size = mesh.shape["seq"], mesh.shape["mlp"]
    grid = Mesh(mesh.devices.reshape(seq_size // 4, 2, 2, mlp_size), ALL)
    seq, mlp = ("z", "x", "core"), "y"
    in_specs = (
        P(ALL, None),
        P(ALL),
        P(ALL),
        P(),
        P(None, seq, None),
        P(None, seq, None),
        P(None, seq, mlp),
        P(None, mlp, seq),
        P(ALL, None),
        P(ALL),
        P(ALL),
        P(ALL),
        P(),
        P(),
    )
    out_specs = (P(ALL, None), P(ALL, None), P(ALL), P(ALL), P(ALL), P())
    return jax.shard_map(
        per_device, mesh=grid, in_specs=in_specs, out_specs=out_specs, check_vma=False
    )
```

```python
import math
from functools import partial

import jax
import jax.numpy as jnp
import numpy as np
from jax import lax
from jax.experimental import pallas as pl
from jax.experimental.pallas import tpu as pltpu
from jax.sharding import Mesh
from jax.sharding import PartitionSpec as P

HEADS = 12
HEAD_DIM = 64
ADAM_STEP = 2

ln_eps = 1e-06
masked_score = -1e30
clip_ratio = 0.05
adam_eps = 1e-08
decay_rate = 0.1
ALL = ("z", "x", "core", "y")
f32 = jnp.float32
bf16 = jnp.bfloat16
LANES = 128
TILE = 256
FORWARD_VMEM = 30 * 2**20
BACKWARD_VMEM = 45 * 2**20

TAIL_SLOPE = 0.275
TAIL_POLY = (
    0.10971068582446765,
    0.1096543595961662,
    0.10219045697718625,
    0.07893593678575173,
    0.08800740710695068,
    -0.03516190352887128,
    0.13017028940734943,
    -0.11067510560848658,
    0.027167870070925505,
)


def mm(a, b):
    return jnp.dot(a, b, preferred_element_type=f32)


def mm_t(a, b):
    return lax.dot_general(a, b, (((1,), (1,)), ((), ())), preferred_element_type=f32)


def gelu_parts(v):
    a = jnp.abs(v)
    bell = jnp.exp2(v * v * (-0.5 * math.log2(math.e)))
    t = 1.0 / (1.0 + TAIL_SLOPE * a)
    poly = jnp.full_like(v, TAIL_POLY[-1])
    for factor in TAIL_POLY[-2::-1]:
        poly = poly * t + factor
    tail = poly * t * bell
    return jnp.where(v >= 0.0, 1.0 - tail, tail), bell * (1.0 / math.sqrt(2.0 * math.pi))


def norm_stats(values):
    center = values - jnp.mean(values, axis=-1, keepdims=True)
    rstd = lax.rsqrt(jnp.mean(center * center, axis=-1, keepdims=True) + ln_eps)
    return center * rstd, rstd


def norm_back(grad, values, gain_row):
    unit, rstd = norm_stats(values)
    grad = grad * gain_row
    mean_grad = jnp.mean(grad, axis=-1, keepdims=True)
    mean_dot = jnp.mean(grad * unit, axis=-1, keepdims=True)
    return rstd * (grad - mean_grad - unit * mean_dot)


class Copies:
    def __init__(self, pairs, sems):
        self.copies = [
            pltpu.make_async_copy(source, target, sems.at[i])
            for i, (source, target) in enumerate(pairs)
        ]

    def start(self):
        for copy in self.copies:
            copy.start()
        return self

    def wait(self):
        for copy in self.copies:
            copy.wait()


def shards(refs, late):
    z, x, core, y = (lax.axis_index(axis) for axis in ALL)
    found = []
    for i, ref in enumerate(refs):
        c = core ^ i
        for step in range(4):
            to_x, to_y = ((x, y), (x ^ 1 ^ c, y ^ c), (x ^ c, y ^ 1 ^ c), (x ^ 1, y ^ 1))[step]
            for back in range(4):
                at = (step // 2, step % 2)
                at = (back, *at) if late else (*at, back)
                found.append((ref.at[at], (z ^ back, to_x, c, to_y)))
    return found


def weight_copies(refs, column, width, dest, sems, late=False, first=0):
    if refs[0].ndim == 2:
        y_size = dest.shape[-1] // width
        columns = pl.ds(column * y_size, dest.shape[-1])
        return Copies([(refs[0].at[:, columns], dest)], sems)
    rows = refs[0].shape[-2]
    pairs = []
    for ref, (z, x, core, y) in shards(refs, late):
        to_rows = pl.ds(pl.multiple_of((x * 2 + core) * rows, 16), rows)
        to_columns = pl.ds(pl.multiple_of(y * (dest.shape[-1] // 2) + first, LANES), width)
        pairs.append((ref.at[:, pl.ds(column, width)], dest.at[z, to_rows, to_columns]))
    return Copies(pairs, sems)


def rider_copies(refs, column, dest, sems):
    pairs = []
    for ref, (z, x, core, y) in shards(refs, False):
        source = ref.at[:, pl.ds(column, LANES)]
        pairs.append((source, dest.at[((z * 2 + x) * 2 + core) * 2 + y]))
    return Copies(pairs, sems)


def rows_view(ref, columns=None):
    value = ref[...] if columns is None else ref[..., columns]
    return value.reshape(-1, value.shape[-1])


def head_of(pair, head):
    lane = lax.broadcasted_iota(jnp.int32, pair.shape, 1)
    keep = (lane < HEAD_DIM) if head == 0 else (lane >= HEAD_DIM)
    return jnp.where(keep, pair, jnp.zeros_like(pair))


def as_column(row):
    return jnp.broadcast_to(row.astype(f32), (8, row.shape[1])).T[:, :1]


def fill_bias(bias_ref, seg_ref):
    seg = seg_ref[...]
    bias_ref[...] = jnp.where(as_column(seg) == seg.astype(f32), 0.0, masked_score)


def copy_out(source, target, sem):
    copy = pltpu.make_async_copy(source, target, sem)
    copy.start()
    return copy


def attention(qkv_ref, bias_ref, mixed_ref, lse_ref):
    tokens, width = mixed_ref.shape
    pairs = width // LANES
    lane = lax.broadcasted_iota(jnp.int32, (tokens, LANES), 1)
    low = lane < HEAD_DIM
    lse = jnp.zeros((tokens, LANES), f32)
    for at in range(pairs):
        query, key, value = (
            qkv_ref[:, i * width + at * LANES : i * width + (at + 1) * LANES] for i in range(3)
        )
        ones = jnp.ones_like(value)
        values = (jnp.where(low, value, ones), jnp.where(low, ones, value))
        parts, tops = [], []
        for head in range(2):
            scores = mm_t(head_of(query, head), key) + bias_ref[...]
            top = jnp.max(scores, axis=1, keepdims=True)
            parts.append(mm(jnp.exp(scores - top).astype(bf16), values[head]))
            tops.append(top)
        total = pltpu.roll(jnp.where(low, parts[1], parts[0]), HEAD_DIM, 1)
        mixed = jnp.where(low, parts[0], parts[1]) / total
        mixed_ref[:, at * LANES : (at + 1) * LANES] = mixed.astype(bf16)
        pair_lse = jnp.where(low, tops[0], tops[1]) + jnp.log(total)
        lse = jnp.where((lane & (HEAD_DIM - 1)) == at, pair_lse, lse)
    lse_ref[...] = lse.T


def attention_back(qkv_ref, mixed_ref, lse_ref, bias_ref, dqkv_ref):
    tokens, width = mixed_ref.shape
    pairs = width // LANES
    for at in range(pairs):
        places = [slice(i * width + at * LANES, i * width + (at + 1) * LANES) for i in range(3)]
        query, key, value = (qkv_ref[:, place] for place in places)
        grad = mixed_ref[:, at * LANES : (at + 1) * LANES]
        found = [None, None, None]
        for head in range(2):
            query_head, key_head, grad_head = (head_of(v, head) for v in (query, key, grad))
            row = head * HEAD_DIM + at
            scores = mm_t(key, query_head) + bias_ref[...]
            probs = jnp.exp(scores - lse_ref[row : row + 1, :])
            grad_probs = mm_t(value, grad_head)
            inner = jnp.sum(probs * grad_probs, axis=0, keepdims=True)
            d_scores = (probs * (grad_probs - inner)).astype(bf16)
            for i, part in enumerate(
                (
                    mm(d_scores.T, key_head),
                    mm(d_scores, query_head),
                    mm(probs.astype(bf16), grad_head),
                )
            ):
                found[i] = part if head == 0 else found[i] + part
        found[0] = found[0] * HEAD_DIM**-0.5
        for place, part in zip(places, found):
            dqkv_ref[:, place] = part.astype(bf16)


def attn_forward_body(plan, *refs):
    count, layer_at, slot_total, takes_riders, has_down = plan
    pieces, refs = refs[:count], refs[count:]
    if has_down:
        (middle_in, active_in), refs = refs[:2], refs[2:]
    else:
        x_ref, refs = refs[0], refs[1:]
    slot_ref, base_ref, seg_ref, gain_ref = refs[:4]
    refs = refs[4:]
    if not takes_riders:
        rider_ref, refs = refs[0], refs[1:]
    mixed_ref, lse_ref, entry_out, qkv_out, weight_out = refs[:5]
    refs = refs[5:]
    if takes_riders:
        (rider_out, rider_ref), refs = (refs[0], refs[1]), refs[2:]
    if has_down:
        (down_out, w_down, middle_ref, active_ref, sem_down), refs = refs[:5], refs[5:]
    w_qkv, norm_ref, bias_ref, entry_ref, qkv_ref, sem_a, sem_b, sem_c = refs
    tokens, width = mixed_ref.shape
    parts = 1 if pieces[0].ndim == 2 else 2
    cut = 3 * width // parts
    qkv_pieces, column = pieces, 0
    copies = []
    if has_down:
        units = active_ref.shape[1]
        load_middle = copy_out(middle_in, middle_ref, sem_c.at[3])
        load_active = copy_out(active_in, active_ref, sem_c.at[4])
        down_pieces = pieces
        if parts == 1:
            down_pieces, qkv_pieces = pieces[:1], pieces[1:]
        else:
            column = units // parts
        load_down = weight_copies(down_pieces, 0, units // parts, w_down, sem_down).start()
    if takes_riders:
        load_riders = rider_copies(pieces, cut, rider_ref, sem_b).start()
    load_qkv = weight_copies(qkv_pieces, column, cut, w_qkv, sem_a)
    if not has_down:
        load_qkv.start()
    fill_bias(bias_ref, seg_ref)
    slots = as_column(slot_ref[...])
    onehot = (slots == base_ref[...]).astype(bf16)
    is_prompt = slots < slot_total
    if takes_riders:
        load_riders.wait()
        copies.append(copy_out(rider_ref, rider_out, sem_c.at[3]))
    holders = base_ref.shape[1] // 8
    windows = rider_ref[layer_at * holders : (layer_at + 1) * holders].astype(f32)
    if has_down:
        load_middle.wait()
        load_active.wait()
        load_down.wait()
        load_qkv.start()
        entry_ref[...] = middle_ref[...] + mm_t(active_ref[...], rows_view(w_down))
        x_ref = entry_ref
    for at in range(width // LANES):
        lanes = slice(at * LANES, (at + 1) * LANES)
        part = windows[:, at * 8 : (at + 1) * 8, :].reshape(-1, LANES)
        inject = mm(onehot, part.astype(bf16))
        entry_ref[:, lanes] = jnp.where(is_prompt, inject, x_ref[:, lanes].astype(f32))
    norm_ref[...] = (norm_stats(entry_ref[...])[0] * gain_ref[layer_at, :1]).astype(bf16)
    load_qkv.wait()
    copies.append(copy_out(entry_ref, entry_out, sem_c.at[0]))
    if has_down:
        copies.append(copy_out(w_down, down_out, sem_c.at[3]))
    copies.append(copy_out(w_qkv, weight_out, sem_c.at[1]))
    for at in range(3 * width // TILE):
        columns = slice(at * TILE, (at + 1) * TILE)
        out = mm(norm_ref[...], rows_view(w_qkv, columns))
        if at < width // TILE:
            out = out.astype(bf16).astype(f32) * HEAD_DIM**-0.5
        qkv_ref[:, columns] = out.astype(bf16)
    copies.append(copy_out(qkv_ref, qkv_out, sem_c.at[2]))
    attention(qkv_ref, bias_ref, mixed_ref, lse_ref)
    for copy in copies:
        copy.wait()


def mlp_up_body(layer_at, top, *refs):
    count = 1 if refs[0].ndim == 2 else 2
    pieces, refs = refs[:count], refs[count:]
    entry_in, mixed_ref, gain_ref = refs[:3]
    refs = refs[3:]
    if top:
        (middle_ref, slope_ref, active_ref), refs = refs[:3], refs[3:]
        w_out, w_up, norm_ref, sem_a, sem_b, sem_d = refs
    else:
        middle_out, slope_out, out_out, up_out, active_out = refs[:5]
        w_out, w_up, norm_ref, sem_a, sem_b, sem_d, middle_ref, slope_ref, active_ref = refs[5:]
    units = slope_ref.shape[1]
    width = middle_ref.shape[1]
    load_entry = copy_out(entry_in, middle_ref, sem_d.at[0])
    load_out = weight_copies(pieces, 0, width // count, w_out, sem_a).start()
    load_up = weight_copies(pieces, width // count, units // count, w_up, sem_b).start()
    load_entry.wait()
    load_out.wait()
    middle_ref[...] = middle_ref[...] + mm(mixed_ref[...], rows_view(w_out))
    copies = []
    if not top:
        copies.append(copy_out(middle_ref, middle_out, sem_d.at[0]))
        copies.append(copy_out(w_out, out_out, sem_d.at[1]))
    norm_ref[...] = (norm_stats(middle_ref[...])[0] * gain_ref[layer_at, 1:]).astype(bf16)
    load_up.wait()
    if not top:
        copies.append(copy_out(w_up, up_out, sem_d.at[2]))
    for at in range(units // TILE):
        columns = slice(at * TILE, (at + 1) * TILE)
        before = mm(norm_ref[...], rows_view(w_up, columns))
        phi_sum, phi = gelu_parts(before)
        active_ref[:, columns] = (before * phi_sum).astype(bf16)
        slope_ref[:, columns] = (phi_sum + before * phi).astype(bf16)
    if not top:
        copies.append(copy_out(slope_ref, slope_out, sem_d.at[3]))
        copies.append(copy_out(active_ref, active_out, sem_d.at[4]))
    for copy in copies:
        copy.wait()


def top_down_copies(down_pieces, up_pieces, dest, sem_down, sem_rest, width):
    units = dest.shape[-1]
    if down_pieces[0].ndim == 2:
        return weight_copies(down_pieces, 0, units, dest, sem_down).copies
    here = down_pieces[0].shape[-1]
    rest = units // 2 - here
    column = (width + units) // 2
    copies = weight_copies(down_pieces, 0, here, dest, sem_down, late=True).copies
    return copies + weight_copies(up_pieces, column, rest, dest, sem_rest, first=here).copies


STATE = ("slope", "middle", "qkv", "lse", "entry")
WEIGHTS = ("down", "up", "out", "qkv_weight")
TOP = (*STATE, "qkv_weight")


def backward_body(layers, counts, *refs):
    down_pieces, refs = refs[: counts[0]], refs[counts[0] :]
    up_pieces, refs = refs[: counts[1]], refs[counts[1] :]
    sources = []
    for layer_at in range(layers):
        names = STATE + WEIGHTS if layer_at < layers - 1 else TOP
        sources.append(dict(zip(names, refs)))
        refs = refs[len(names) :]
    active_in, cotangent_ref, slot_ref, seg_ref, gain_ref = refs[:5]
    (out_ref, prompt_ref, block_ref), refs = refs[5:8], refs[8:]
    held = dict(zip(STATE + WEIGHTS, refs))
    refs = refs[len(held) :]
    active_ref, low_ref, before_ref, grad_ref, mixed_ref, dqkv_ref, bias_ref = refs[:7]
    sem, sem_down, sem_rest, sem_up, sem_out = refs[7:]
    order = list(held)
    tokens, width = grad_ref.shape
    units = before_ref.shape[1]
    parts = 1 if down_pieces[0].ndim == 2 else 2
    top_weights = {
        "up": (up_pieces, width // parts, units // parts, sem_up),
        "out": (up_pieces, 0, width // parts, sem_out),
    }

    class Fetch:
        def __init__(self, name, layer_at):
            if layer_at == layers - 1 and name == "down":
                self.copies = top_down_copies(
                    down_pieces, up_pieces, held[name], sem_down, sem_rest, width
                )
            elif layer_at == layers - 1 and name in top_weights:
                refs, column, count, sems = top_weights[name]
                self.copies = weight_copies(refs, column, count, held[name], sems).copies
            else:
                source, at = sources[layer_at][name], order.index(name)
                self.copies = [pltpu.make_async_copy(source, held[name], sem.at[at])]
            for copy in self.copies:
                copy.start()

        def wait(self):
            for copy in self.copies:
                copy.wait()

    coming = {}

    def fetch(layer_at, *names):
        for name in names if layer_at >= 0 else ():
            coming[name] = Fetch(name, layer_at)

    def arrived(*names):
        for name in names:
            if name in coming:
                coming.pop(name).wait()

    fetch(layers - 1, "down", "slope")
    fill_bias(bias_ref, seg_ref)
    low_ref[...] = cotangent_ref[...]
    slot_total = prompt_ref.shape[1]
    is_prompt = as_column(slot_ref[...]) < slot_total
    onehot_t = (
        slot_ref[...] == lax.broadcasted_iota(jnp.int32, (slot_total, tokens), 0)
    ).astype(bf16)

    for layer_at in reversed(range(layers)):
        top = layer_at == layers - 1

        below = layer_at - 1
        arrived("down", "slope")
        fetch(layer_at, *(("up", "middle") if top else ("up",)))
        for at in range(units // TILE):
            columns = slice(at * TILE, (at + 1) * TILE)
            grad_active = mm(low_ref[...], rows_view(held["down"], columns))
            slope = held["slope"][:, columns].astype(f32)
            before_ref[:, columns] = (grad_active * slope).astype(bf16)
        arrived("up", "middle")
        if top:
            load_active = copy_out(active_in, active_ref, sem.at[len(order)])
        fetch(layer_at, "out", "qkv", "lse")
        grad_norm = mm_t(before_ref[...], rows_view(held["up"]))
        back = norm_back(grad_norm, held["middle"][...], gain_ref[layer_at, 1:])
        grad = cotangent_ref[...].astype(f32) if top else grad_ref[...]
        grad_middle = grad + back
        grad_ref[...] = grad_middle
        low_ref[...] = grad_middle.astype(bf16)
        arrived("out", "qkv", "lse")
        mixed_ref[...] = mm_t(low_ref[...], rows_view(held["out"])).astype(bf16)
        if top:
            load_active.wait()
            branch = mm_t(active_ref[...], rows_view(held["down"]))
            block_ref[...] = (held["middle"][...] + branch).astype(bf16)
        fetch(layer_at, "qkv_weight", "entry")
        fetch(below, "down", "slope", "middle")
        attention_back(held["qkv"], mixed_ref, held["lse"], bias_ref, dqkv_ref)
        arrived("qkv_weight", "entry")
        grad_norm = mm_t(dqkv_ref[...], rows_view(held["qkv_weight"]))
        back = norm_back(grad_norm, held["entry"][...], gain_ref[layer_at, :1])
        grad_entry = grad_ref[...] + back
        high, low = halves(grad_entry)
        prompt_ref[layer_at] = mm(onehot_t, high) + mm(onehot_t, low)
        passed = jnp.where(is_prompt, 0.0, grad_entry)
        if layer_at > 0:
            grad_ref[...] = passed
            low_ref[...] = passed.astype(bf16)
        else:
            out_ref[...] = passed


def halves(values):
    high = values.astype(bf16)
    return high, (values - high.astype(f32)).astype(bf16)


def shape(dims, dtype):
    return jax.ShapeDtypeStruct(dims, dtype)


def run(body, away, near, outputs, outputs_away, scratch, flops, name, vmem=FORWARD_VMEM):
    here = pl.BlockSpec(memory_space=pltpu.VMEM)
    hbm = pl.BlockSpec(memory_space=pltpu.HBM)
    anywhere = pl.BlockSpec(memory_space=pl.ANY)
    results = (*outputs, *outputs_away)
    moved = sum(math.prod(a.shape) * a.dtype.itemsize for a in (*away, *near, *results))
    return pl.pallas_call(
        body,
        out_shape=results,
        in_specs=[anywhere] * len(away) + [here] * len(near),
        out_specs=[here] * len(outputs) + [hbm] * len(outputs_away),
        scratch_shapes=scratch,
        compiler_params=pltpu.CompilerParams(vmem_limit_bytes=vmem),
        cost_estimate=pl.CostEstimate(flops=flops, transcendentals=0, bytes_accessed=moved),
        name=name,
    )(*away, *near)


def zero_body(*refs):
    refs[-1][...] = jnp.zeros((1, 1), f32)


def zero_after(values):
    return pl.pallas_call(
        zero_body,
        out_shape=shape((1, 1), f32),
        in_specs=[pl.BlockSpec(memory_space=pl.ANY)] * len(values),
        out_specs=pl.BlockSpec(memory_space=pltpu.VMEM),
        compiler_params=pltpu.CompilerParams(vmem_limit_bytes=2**20),
        cost_estimate=pl.CostEstimate(flops=0, transcendentals=0, bytes_accessed=4),
        name="zero_after",
    )(*values)


def piece_sems(pieces):
    count = 1 if pieces[0].ndim == 2 else 32
    return pltpu.SemaphoreType.DMA((count,))


def weight_shape(pieces, width, columns):
    return (width, columns) if pieces[0].ndim == 2 else (4, width // 4, columns)


def attn_forward(pieces, layer_at, slot_total, x, below, riders, marks, gains):
    tokens = marks["seg"].shape[1]
    width = gains.shape[2]
    takes_riders, has_down = riders is None, below is not None
    weight = weight_shape(pieces, width, 3 * width)
    near_out = (shape((tokens, width), bf16), shape((LANES, tokens), f32))
    away_out = (
        shape((tokens, width), f32),
        shape((tokens, 3 * width), bf16),
        shape(weight, bf16),
    )
    away = tuple(pieces)
    near = (marks["slot"], marks["base"], marks["seg"], gains)
    scratch = []
    if not takes_riders:
        near += (riders,)
    else:
        rider_shape = (math.prod(axis_sizes()), 8 * width // LANES, LANES)
        away_out += (shape(rider_shape, bf16),)
        scratch.append(pltpu.VMEM(rider_shape, bf16))
    if has_down:
        units = below["active"].shape[1]
        away += (below["middle"], below["active"])
        down = weight_shape(pieces, width, units)
        away_out += (shape(down, bf16),)
        scratch += [
            pltpu.VMEM(down, bf16),
            pltpu.VMEM((tokens, width), f32),
            pltpu.VMEM((tokens, units), bf16),
            piece_sems(pieces),
        ]
    else:
        near = (x, *near)
    scratch += [
        pltpu.VMEM(weight, bf16),
        pltpu.VMEM((tokens, width), bf16),
        pltpu.VMEM((tokens, tokens), f32),
        pltpu.VMEM((tokens, width), f32),
        pltpu.VMEM((tokens, 3 * width), bf16),
        piece_sems(pieces),
        piece_sems(pieces),
        pltpu.SemaphoreType.DMA((5,)),
    ]
    flops = 2 * tokens * width * (7 * width + 2 * tokens)
    body = partial(attn_forward_body, (len(pieces), layer_at, slot_total, takes_riders, has_down))
    found = run(body, away, near, near_out, away_out, scratch, flops, "attn_forward")
    names = ("mixed", "lse", "entry", "qkv", "qkv_weight")
    layer = dict(zip(names, found))
    found = found[5:]
    if takes_riders:
        riders, found = found[0], found[1:]
    if has_down:
        below["down"], found = found[0], found[1:]
    return layer, riders


def mlp_up(pieces, layer_at, layer, gains, units, top):
    tokens, width = layer["mixed"].shape
    out_shape, up_shape = (weight_shape(pieces, width, n) for n in (width, units))
    state = {
        "middle": shape((tokens, width), f32),
        "slope": shape((tokens, units), bf16),
        "active": shape((tokens, units), bf16),
    }
    scratch = [
        pltpu.VMEM(out_shape, bf16),
        pltpu.VMEM(up_shape, bf16),
        pltpu.VMEM((tokens, width), bf16),
        piece_sems(pieces),
        piece_sems(pieces),
        pltpu.SemaphoreType.DMA((5,)),
    ]
    if top:
        results, outputs, away_out = state, tuple(state.values()), ()
    else:
        weights = {"out": shape(out_shape, bf16), "up": shape(up_shape, bf16)}
        names = ("middle", "slope", "out", "up", "active")
        results = {name: {**state, **weights}[name] for name in names}
        outputs, away_out = (), tuple(results.values())
        scratch += [pltpu.VMEM(a.shape, a.dtype) for a in state.values()]
    flops = 2 * tokens * width * (units + width)
    away = (*pieces, layer["entry"])
    near = (layer["mixed"], gains)
    body = partial(mlp_up_body, layer_at, top)
    found = run(body, away, near, outputs, away_out, scratch, flops, "mlp_up")
    layer.update(zip(results, found))


def backward(down_pieces, up_pieces, kept, cotangent, marks, gains, slot_total):
    layers = len(kept)
    tokens, width = cotangent.shape
    units = kept[0]["slope"].shape[1]
    away = [*down_pieces, *up_pieces]
    for layer_at, layer in enumerate(kept):
        away += [layer[name] for name in (STATE + WEIGHTS if layer_at < layers - 1 else TOP)]
    away.append(kept[-1]["active"])
    near = (cotangent, marks["slot"], marks["seg"], gains)
    outputs = (
        shape((tokens, width), f32),
        shape((layers, slot_total, width), f32),
        shape((tokens, width), bf16),
    )
    held = [kept[0][name] for name in STATE + WEIGHTS]
    scratch = [pltpu.VMEM(a.shape, a.dtype) for a in held]
    scratch += [
        pltpu.VMEM((tokens, units), bf16),
        pltpu.VMEM((tokens, width), bf16),
        pltpu.VMEM((tokens, units), bf16),
        pltpu.VMEM((tokens, width), f32),
        pltpu.VMEM((tokens, width), bf16),
        pltpu.VMEM((tokens, 3 * width), bf16),
        pltpu.VMEM((tokens, tokens), f32),
        pltpu.SemaphoreType.DMA((len(held) + 1,)),
        piece_sems(down_pieces),
        piece_sems(up_pieces),
        piece_sems(up_pieces),
        piece_sems(up_pieces),
    ]
    flops = 2 * layers * tokens * width * (4 * width + 3 * units + 5 * tokens)
    body = partial(backward_body, layers, (len(down_pieces), len(up_pieces)))
    return run(body, away, near, outputs, (), scratch, flops, "backward", vmem=BACKWARD_VMEM)


def axis_sizes():
    return tuple(lax.axis_size(axis) for axis in ALL)


def is_block():
    return axis_sizes() == (4, 2, 2, 2)


def flip(value, axis):
    return lax.ppermute(value, axis, [(0, 1), (1, 0)])


def move_all(value, to):
    sizes = axis_sizes()
    moves = []
    for at in np.ndindex(*sizes):
        moves.append(tuple(int(np.ravel_multi_index(place, sizes)) for place in (at, to(*at))))
    return lax.ppermute(value, ALL, moves)


def turn(value, core_of_x):
    return move_all(
        value,
        lambda z, x, core, y: (z, 1 - x, core, y) if core == core_of_x else (z, x, core, 1 - y),
    )


def near_xy(value, dx, dy):
    return move_all(value, lambda z, x, core, y: (z, x ^ dx, core, y ^ dy))


def swap_z(value, distance):
    return lax.ppermute(value, "z", [(i, i ^ distance) for i in range(lax.axis_size("z"))])


class Steps:
    def __init__(self):
        self.zero = None

    def behind(self, value):
        return value if self.zero is None else value + self.zero[0, 0].astype(value.dtype)

    def join(self, parts):
        return self.behind(jnp.stack(parts))

    def wait(self, arrays):
        self.zero = zero_after(arrays)


class Gather:
    def __init__(self, steps, shard):
        self.steps, self.own = steps, shard

    def start_ring(self):
        own = self.steps.behind(self.own)
        self.parts = [own] + [swap_z(own, i) for i in (1, 2, 3)]
        return self.parts[1:]

    def first_turn(self):
        self.parts = [self.steps.join(self.parts)]
        self.parts.append(turn(self.parts[0], 0))
        return self.parts[1:]

    def second_turn(self):
        self.parts = [self.steps.join(self.parts)]
        self.parts.append(turn(self.parts[0], 1))
        return self.parts[1:]

    def last_turn(self):
        whole = self.steps.join(self.parts)
        self.pieces = [whole, flip(whole, "core")]
        return []


class LateGather(Gather):
    def late_first(self):
        self.parts = [self.steps.behind(self.own)]
        self.parts.append(turn(self.parts[0], 0))
        return self.parts[1:]

    def late_ring(self, distances):
        if len(self.parts) == 2:
            self.parts = [self.steps.join(self.parts)]
        own = self.parts[0]
        self.parts += [swap_z(own, i) for i in distances]
        return self.parts[-len(distances) :]


def total_over(value):
    if not is_block():
        return lax.psum(value, ALL)
    core = lax.axis_index("core")
    low = value.astype(bf16)
    mine = jnp.where(core == 0, value[0], value[1])
    theirs = jnp.where(core == 0, low[1], low[0])
    total = mine + flip(theirs, "core").astype(f32)
    low = total.astype(bf16)
    total = total + sum(near_xy(low, *to).astype(f32) for to in ((1, 0), (0, 1), (1, 1)))
    low = total.astype(bf16)
    total = total + sum(swap_z(low, distance).astype(f32) for distance in (1, 2, 3))
    other = flip(total.astype(bf16), "core").astype(f32)
    return jnp.stack([jnp.where(core == 0, total, other), jnp.where(core == 0, other, total)])


def window_rows(count, width):
    step = math.gcd(count, width)
    return -(-(width - step + count) // width)


def prompt_window(prompts, width):
    count = prompts.shape[0]
    assert window_rows(count, width) <= 4
    shift = lax.axis_index(ALL) * count % width
    flat = lax.dynamic_update_slice(jnp.zeros((4 * width,), f32), prompts, (shift,))
    rows = flat.reshape(4, width // LANES, LANES).transpose(1, 0, 2)
    return jnp.concatenate(halves(rows), axis=1).reshape(-1, LANES)


def window_slots(count, width, layers):
    holders = math.prod(axis_sizes()) // layers
    base = np.arange(holders, dtype=np.int32) * count // width
    both = base[:, None] + np.arange(8, dtype=np.int32)[None, :] % 4
    return jnp.asarray(both.reshape(1, -1), f32)


def gather_any(qkv, out, up, down):
    seq = ("z", "x", "core")
    layers = qkv.shape[0]
    qkvs = [lax.all_gather(qkv[layer_at], seq, tiled=True) for layer_at in range(layers)]
    groups = [[qkvs[0]]]
    for layer_at in range(layers):
        whole_up = lax.all_gather(up[layer_at], "y", axis=1, tiled=True)
        out_up = jnp.concatenate([out[layer_at], whole_up], axis=1)
        groups.append([lax.all_gather(out_up, seq, tiled=True)])
        whole_down = lax.all_gather(down[layer_at].T, "y", axis=1, tiled=True)
        groups.append([lax.all_gather(whole_down, seq, tiled=True)] + qkvs[layer_at + 1 :][:1])
    return groups


def block_groups(qkv_weight, out_weight, up_weight, down_weight, window):
    y_size, y_at = lax.axis_size("y"), lax.axis_index("y")
    layers, rows, qkv_width = qkv_weight.shape
    cut, out_cut = qkv_width // y_size, out_weight.shape[2] // y_size
    qkv = lax.dynamic_slice(qkv_weight, (0, 0, y_at * cut), (layers, rows, cut))
    out = lax.dynamic_slice(out_weight, (0, 0, y_at * out_cut), (layers, rows, out_cut))
    groups = [jnp.concatenate([qkv[0], window], axis=1)]
    for layer_at in range(layers):
        out_up = [out[layer_at], up_weight[layer_at]]
        down = down_weight[layer_at].T
        if layer_at < layers - 1:
            down = jnp.concatenate([down, qkv[layer_at + 1]], axis=1)
        else:
            late = down.shape[1] * 3 // 4
            out_up.append(down[:, late:])
            down = down[:, :late]
        groups += [jnp.concatenate(out_up, axis=1), down]
    return groups


def per_device(
    patches,
    segments,
    prompt_slots,
    norm_gains,
    qkv_weight,
    out_weight,
    up_weight,
    down_weight,
    cotangent,
    prompts,
    first_moment,
    second_moment,
    adam_betas,
    learn_rate,
):
    layers, _, width = norm_gains.shape
    tokens = patches.shape[0]
    units = up_weight.shape[2] * lax.axis_size("y")
    total_prompts = prompts.shape[0] * math.prod(axis_sizes())
    slot_total = total_prompts // (layers * width)
    window = prompt_window(prompts, width)
    marks = {
        "base": window_slots(prompts.shape[0], width, layers),
        "slot": prompt_slots.reshape(1, tokens),
        "seg": segments.reshape(1, tokens),
    }
    kept = []
    pieces = []
    state = {"riders": None}

    def forward_step(at):
        layer_at, part = divmod(at, 2)
        if part == 1:
            top = layer_at == layers - 1
            mlp_up(pieces[at], layer_at, kept[layer_at], norm_gains, units, top)
            return
        layer, state["riders"] = attn_forward(
            pieces[at],
            layer_at,
            slot_total,
            patches if layer_at == 0 else None,
            kept[layer_at - 1] if layer_at > 0 else None,
            state["riders"],
            marks,
            norm_gains,
        )
        kept.append(layer)

    block = is_block()
    if block:
        steps = Steps()
        groups = block_groups(qkv_weight, out_weight, up_weight, down_weight, window)
        *early, final = groups
        gathers = [Gather(steps, shard) for shard in early] + [LateGather(steps, final)]

        def kernel(at):
            pieces.append(gathers[at].pieces)
            forward_step(at)
            return [kept[at // 2][("entry", "middle")[at % 2]]]

        ring, first, second, last = (
            Gather.start_ring,
            Gather.first_turn,
            Gather.second_turn,
            Gather.last_turn,
        )
        late_first = LateGather.late_first
        late_ring = LateGather.late_ring
        for moves, beside in (
            ([(ring, 0)], None),
            ([(first, 0), (late_first, 4)], None),
            ([(ring, 1), (second, 0), (second, 4)], None),
            ([(ring, 2), (last, 0), (first, 1)], 0),
            ([(ring, 3), (second, 1), (first, 2)], None),
            ([(last, 1), (second, 2), (first, 3), (partial(late_ring, distances=(1, 2)), 4)], 1),
            ([(last, 2), (second, 3), (partial(late_ring, distances=(3,)), 4)], 2),
            ([(last, 3), (last, 4)], 3),
        ):
            coming = [array for move, at in moves for array in move(gathers[at])]
            beside = [] if beside is None else kernel(beside)
            if coming:
                steps.wait(coming + beside)
        pieces.append(gathers[4].pieces)
    else:
        state["riders"] = lax.all_gather(window, ALL)
        pieces = gather_any(qkv_weight, out_weight, up_weight, down_weight)
        for at in range(2 * layers):
            forward_step(at)

    gradient, layer_grads, block_output = backward(
        pieces[-1], pieces[-2], kept, cotangent, marks, norm_gains, slot_total
    )

    prompt_grad = total_over(layer_grads)
    grad_norm = jnp.sqrt(jnp.sum(prompt_grad * prompt_grad))
    clip_limit = clip_ratio * math.sqrt(total_prompts)
    own_grads = lax.dynamic_slice(
        prompt_grad.reshape(-1), (lax.axis_index(ALL) * prompts.shape[0],), prompts.shape
    )
    clipped = own_grads * jnp.minimum(1.0, clip_limit / (grad_norm + 1e-06))
    beta_one = adam_betas[0]
    beta_two = adam_betas[1]
    step_value = float(ADAM_STEP)
    new_first = beta_one * first_moment + (1.0 - beta_one) * clipped
    new_second = beta_two * second_moment + (1.0 - beta_two) * clipped * clipped
    first_hat = new_first / (1.0 - beta_one**step_value)
    second_hat = new_second / (1.0 - beta_two**step_value)
    new_prompts = prompts - learn_rate[0] * (
        first_hat / (jnp.sqrt(second_hat) + adam_eps) + decay_rate * prompts
    )
    return (block_output, gradient, new_prompts, new_first, new_second, grad_norm.reshape(1))


def solution(mesh):
    seq_size, mlp_size = mesh.shape["seq"], mesh.shape["mlp"]
    grid = Mesh(mesh.devices.reshape(seq_size // 4, 2, 2, mlp_size), ALL)
    seq, mlp = ("z", "x", "core"), "y"
    in_specs = (
        P(ALL, None),
        P(ALL),
        P(ALL),
        P(),
        P(None, seq, None),
        P(None, seq, None),
        P(None, seq, mlp),
        P(None, mlp, seq),
        P(ALL, None),
        P(ALL),
        P(ALL),
        P(ALL),
        P(),
        P(),
    )
    out_specs = (P(ALL, None), P(ALL, None), P(ALL), P(ALL), P(ALL), P())
    return jax.shard_map(
        per_device, mesh=grid, in_specs=in_specs, out_specs=out_specs, check_vma=False
    )
```
